32 devices in a mesh: dp: 8 (over y, x, core), fsdp: 4 (over z).
Axes of the slice: x: 2, y: 2, z: 4, core: 2. Of those that a mesh axis runs over, the one named last changes fastest.
Arguments:
- tokens: bfloat16 [32768, 768], P(('dp', 'fsdp')), may hold values from -8 to 8
- chip_ids: int32 [32768], P(('dp', 'fsdp')), may hold values from 0 to 511, as said below
- ln1_gain: bfloat16 [768], P('fsdp'), may hold values from 0.5 to 1.5
- ln1_bias: bfloat16 [768], P('fsdp'), may hold values from -1.5 to 1.5
- w_qkv: bfloat16 [768, 2304], P('fsdp'), may hold values from -0.3125 to 0.3125
- w_out: bfloat16 [768, 768], P('fsdp'), may hold values from -0.625 to 0.625
- b_out: bfloat16 [768], P('fsdp'), may hold values from -1.5 to 1.5
- ln2_gain: bfloat16 [768], P('fsdp'), may hold values from 0.5 to 1.5
- ln2_bias: bfloat16 [768], P('fsdp'), may hold values from -1.5 to 1.5
- w_fc1: bfloat16 [768, 3072], P('fsdp'), may hold values from -0.21875 to 0.21875
- b_fc1: bfloat16 [3072], P('fsdp'), may hold values from -2.5 to 2.5
- w_fc2: bfloat16 [3072, 768], P('fsdp'), may hold values from -0.15625 to 0.15625
- b_fc2: bfloat16 [768], P('fsdp'), may hold values from -1.5 to 1.5
- cotangent: bfloat16 [32768, 768], P(('dp', 'fsdp')), may hold values from -6 to 6
Outputs:
- layer_out: bfloat16 [32768, 768], P(('dp', 'fsdp'))
- grad_tokens: float32 [32768, 768], P(('dp', 'fsdp'))
- grad_ln1_gain: float32 [768], P('fsdp')
- grad_ln1_bias: float32 [768], P('fsdp')
- grad_w_qkv: float32 [768, 2304], P('fsdp')
- grad_w_out: float32 [768, 768], P('fsdp')
- grad_b_out: float32 [768], P('fsdp')
- grad_ln2_gain: float32 [768], P('fsdp')
- grad_ln2_bias: float32 [768], P('fsdp')
- grad_w_fc1: float32 [768, 3072], P('fsdp')
- grad_b_fc1: float32 [3072], P('fsdp')
- grad_w_fc2: float32 [3072, 768], P('fsdp')
- grad_b_fc2: float32 [768], P('fsdp')
The draws below stay inside these ranges and needn't reach their ends.
Inputs may be any that keep to these rules, and one draw needn't show every extreme that they name: `chip_ids`: chip numbers never fall along the tokens. Each chip holds exactly 64 or 256 tokens and lies inside one device's block of 1024 rows; every such block holds at least one chip of 256 tokens and may hold only such chips. The chips of the d-th block of rows carry numbers from d * 16 to (d + 1) * 16 - 1, the first and the last of them always used.
All inputs are finite; a program needn't handle non-finite values.
Results may differ from the reference program's by a relative error of at most 0.015.
Values may be sent and summed in bfloat16 or wider, within the bound.
No kernel may reach another device: no remote copies, remote signals or barrier semaphores. Data moves between devices by JAX's collectives and lax.ppermute only.
A program may use at most 320 MiB of HBM per device.

```python
import math
import jax
import jax.numpy as jnp
from jax import lax

D = 768
HEADS = 12
HEAD = 64
FF = 3072
SHORT_CHIP = 64
LONG_CHIP = 256
TOK_DEV = 1024
TOKENS = 32768


def draw_tokens(key, part):
    key_base, key_cols, key_rows = jax.random.split(key, 3)
    base_vals = jax.random.normal(key_base, (TOKENS, D), jnp.float32)
    col_scale = jnp.exp(jax.random.uniform(key_cols, (1, D), jnp.float32, math.log(0.3), math.log(3.0)))
    row_scale = jnp.exp(jax.random.uniform(key_rows, (TOKENS, 1), jnp.float32, math.log(0.5), math.log(2.0)))
    return jnp.clip(base_vals * col_scale * row_scale, -8.0, 8.0).astype(jnp.bfloat16)


def draw_chip_ids(key, part):
    units = TOK_DEV // SHORT_CHIP
    ratio = LONG_CHIP // SHORT_CHIP
    blocks = TOKENS // TOK_DEV

    def one_device(device_number):
        device_key = jax.random.fold_in(key, device_number)
        key_count, key_order = jax.random.split(device_key)
        longs = jax.random.randint(key_count, (), 1, TOK_DEV // LONG_CHIP + 1)
        chips = longs + units - ratio * longs
        order = jax.random.permutation(key_order, units)
        slot = jnp.arange(units)
        used = slot < chips
        below = jnp.sum(((order[None, :] < order[:, None]) & used[None, :]).astype(jnp.int32), axis=1)
        is_long = below < longs
        sizes = jnp.where(used, jnp.where(is_long, LONG_CHIP, SHORT_CHIP), 0)
        starts = jnp.cumsum(sizes) - sizes
        places = jnp.arange(TOK_DEV)
        local = jnp.sum(((starts[None, :] <= places[:, None]) & used[None, :]).astype(jnp.int32), axis=1) - 1
        local = jnp.where(local == chips - 1, units - 1, local)
        return (local + device_number * units).astype(jnp.int32)
    return jax.vmap(one_device)(jnp.arange(blocks)).reshape(TOKENS).astype(jnp.int32)


def shard_levels(own_key, dims, cuts, low, high):
    gain, own = 1.0, jax.random.fold_in(own_key, 6)
    for position, parts in cuts:
        draws = jnp.exp(jax.random.uniform(jax.random.fold_in(own, position), (parts,), jnp.float32, low / len(cuts), high / len(cuts)))
        gain = gain * jnp.repeat(draws, dims[position] // parts).reshape([-1 if axis == position else 1 for axis in range(len(dims))])
    return gain


def scatter_about(own_key, extent, width, reach, pieces=(), kind=jnp.bfloat16):
    values = jax.random.normal(own_key, extent, jnp.float32) * width
    if len(pieces) > 0:
        values = shard_levels(own_key, extent, pieces, -0.22, 0.18) * values
    return jnp.clip(values, min=-reach, max=reach).astype(kind)


def setup_inputs(seed: int = 0) -> dict:
    key_list = jax.random.split(jax.random.key(seed), 15)
    tokens = draw_tokens(jax.random.fold_in(key_list[14], 71), 0)
    chip_ids = draw_chip_ids(jax.random.fold_in(key_list[14], 71), 0)
    ln1_gain = jnp.clip(1.0 + 0.1 * jax.random.normal(key_list[2], (D,), jnp.float32), 0.5, 1.5).astype(jnp.bfloat16)
    ln1_bias = scatter_about(key_list[3], (D,), 0.3, 1.5, ((0, 4),))
    w_qkv = scatter_about(key_list[4], (D, 3 * D), (D // 2) ** -0.5, 0.3125, ((0, 4),))
    w_out = scatter_about(key_list[5], (D, D), (D // 8) ** -0.5, 0.625, ((0, 4),))
    b_out = scatter_about(key_list[6], (D,), 0.3, 1.5, ((0, 4),))
    ln2_gain = jnp.clip(1.0 + 0.1 * jax.random.normal(key_list[7], (D,), jnp.float32), 0.5, 1.5).astype(jnp.bfloat16)
    ln2_bias = scatter_about(key_list[8], (D,), 0.3, 1.5, ((0, 4),))
    w_fc1 = scatter_about(key_list[9], (D, FF), D ** -0.5, 0.21875, ((0, 4),))
    b_fc1 = scatter_about(key_list[10], (FF,), 0.5, 2.5, ((0, 4),))
    w_fc2 = scatter_about(key_list[11], (FF, D), (FF // 2) ** -0.5, 0.15625, ((0, 4),))
    b_fc2 = scatter_about(key_list[12], (D,), 0.3, 1.5, ((0, 4),))
    cotangent = scatter_about(key_list[13], (TOKENS, D), 1.0, 6.0, ((0, 32),))
    return dict(tokens=tokens, chip_ids=chip_ids, ln1_gain=ln1_gain, ln1_bias=ln1_bias, w_qkv=w_qkv, w_out=w_out, b_out=b_out, ln2_gain=ln2_gain, ln2_bias=ln2_bias, w_fc1=w_fc1, b_fc1=b_fc1, w_fc2=w_fc2, b_fc2=b_fc2, cotangent=cotangent)


epsilon = 1e-05
neg_big = -1e+30
highest = lax.Precision.HIGHEST

@jax.custom_vjp
def low(v):
    return lax.optimization_barrier(v.astype(jnp.bfloat16)).astype(jnp.float32)

@jax.custom_vjp
def low_back(v):
    return v

def low_keep(v):
    return (low(v), None)

def low_pass(kept, grad):
    return (grad,)

def back_keep(v):
    return (v, None)

def back_low(kept, grad):
    return (low(grad),)
low.defvjp(low_keep, low_pass)
low_back.defvjp(back_keep, back_low)

def product(left_side, right_side):
    return jnp.dot(left_side, right_side, precision=highest, preferred_element_type=jnp.float32)

def layer_norm(token_rows, gain_vec, shift_vec):
    centred = token_rows - lax.optimization_barrier(jnp.mean(token_rows, axis=-1, keepdims=True))
    spread = lax.optimization_barrier(jnp.mean(centred * centred, axis=-1, keepdims=True))
    return centred * lax.rsqrt(spread + epsilon) * gain_vec + shift_vec

def layer(token_rows, chip_rows, params):
    ln1_gain, ln1_bias, w_qkv, w_out, b_out, ln2_gain, ln2_bias, w_fc1, b_fc1, w_fc2, b_fc2 = params
    length = token_rows.shape[0]
    normed_in = low(layer_norm(token_rows, ln1_gain, ln1_bias))
    qkv_all = low_back(low(product(normed_in, w_qkv)))
    queries = qkv_all[:, :D].reshape(length, HEADS, HEAD)
    key_heads = qkv_all[:, D:2 * D].reshape(length, HEADS, HEAD)
    value_heads = qkv_all[:, 2 * D:].reshape(length, HEADS, HEAD)
    scores = jnp.einsum('qhe,khe->hqk', queries, key_heads, precision=highest) * (1.0 / math.sqrt(HEAD))
    scores = low_back(scores)
    same_chip = chip_rows[:, None] == chip_rows[None, :]
    scores = jnp.where(same_chip[None], scores, neg_big)
    row_max = lax.optimization_barrier(jnp.max(scores, axis=-1, keepdims=True))
    exp_score = jnp.exp(scores - row_max)
    attn_probs = low(exp_score / lax.optimization_barrier(jnp.sum(exp_score, axis=-1, keepdims=True)))
    attn_mixed = jnp.einsum('hqk,khe->qhe', attn_probs, value_heads, precision=highest).reshape(length, D)
    attn_mixed = low_back(low(attn_mixed))
    hidden_one = token_rows + low_back(product(attn_mixed, w_out) + b_out)
    normed_mid = low(layer_norm(hidden_one, ln2_gain, ln2_bias))
    pre_act = low_back(product(normed_mid, w_fc1) + b_fc1)
    activated = low(jax.nn.gelu(pre_act, approximate=False))
    return hidden_one + low_back(product(activated, w_fc2) + b_fc2)

def reference(tokens, chip_ids, ln1_gain, ln1_bias, w_qkv, w_out, b_out, ln2_gain, ln2_bias, w_fc1, b_fc1, w_fc2, b_fc2, cotangent):
    params = tuple((member.astype(jnp.float32) for member in (ln1_gain, ln1_bias, w_qkv, w_out, b_out, ln2_gain, ln2_bias, w_fc1, b_fc1, w_fc2, b_fc2)))
    blocks = TOKENS // TOK_DEV
    chip_blocks = chip_ids.reshape(blocks, TOK_DEV)

    def forward(token_rows, weights_all):

        def one_block(block_pair):
            return layer(block_pair[0], block_pair[1], weights_all)
        stacked = lax.map(jax.checkpoint(one_block), (token_rows.reshape(blocks, TOK_DEV, D), chip_blocks))
        return stacked.reshape(TOKENS, D)
    output, backward = jax.vjp(forward, tokens.astype(jnp.float32), params)
    d_tokens, d_params = backward(cotangent.astype(jnp.float32))
    return (output.astype(jnp.bfloat16), d_tokens, d_params[0], d_params[1], d_params[2], d_params[3], d_params[4], d_params[5], d_params[6], d_params[7], d_params[8], d_params[9], d_params[10])
```

```python
import functools
import math

import jax
import jax.numpy as jnp
from jax import lax
from jax.experimental import pallas as pl
from jax.experimental.pallas import tpu as pltpu
from jax.sharding import PartitionSpec as P

HEADS = 12
HEAD = 64
UNIT = 64
BLOCK = 256
PER = BLOCK // UNIT
EPS = 1e-05
NEG = -1e30
RSQRT2 = 1.0 / math.sqrt(2.0)
RSQRT_TAU = 1.0 / math.sqrt(2.0 * math.pi)
SCALE = 1.0 / math.sqrt(HEAD)
EXT = 256
VMEM_LIMIT = 64 * 1024 * 1024 - 65536
ALL = ("dp", "fsdp")
F32 = jnp.float32
BF16 = jnp.bfloat16

I_LONG, I_C, I_X, I_Y, I_Z, I_B1, I_B2 = 16, 17, 18, 19, 20, 21, 22


def nn(a, b):
    return lax.dot_general(a, b, (((1,), (0,)), ((), ())), preferred_element_type=F32)


def nt(a, b):
    return lax.dot_general(a, b, (((1,), (1,)), ((), ())), preferred_element_type=F32)


def tn(a, b):
    return lax.dot_general(a, b, (((0,), (0,)), ((), ())), preferred_element_type=F32)


def params(**kw):
    return pltpu.CompilerParams(vmem_limit_bytes=VMEM_LIMIT, **kw)


ANY = pl.BlockSpec(memory_space=pl.ANY)
WHOLE = pl.BlockSpec(memory_space=pltpu.VMEM)


def tie(a, *after):
    return lax.optimization_barrier((a,) + after)[0]


class Routes:
    def __init__(self, n_dp, n_z):
        self.n_dp, self.n_z = n_dp, n_z

    def table(self, move):
        pairs = []
        for d in range(self.n_dp):
            for z in range(self.n_z):
                e, w = move(d, z)
                pairs.append((d * self.n_z + z, e * self.n_z + w % self.n_z))
        return pairs

    def core(self, a):
        return lax.ppermute(a, ALL, self.table(lambda d, z: (d ^ 1, z)))

    def first(self, a):
        return lax.ppermute(a, ALL, self.table(lambda d, z: (d ^ (2 if d % 2 == 0 else 4), z)))

    def second(self, a):
        return lax.ppermute(a, ALL, self.table(lambda d, z: (d ^ (4 if d % 2 == 0 else 2), z)))

    def z_near(self, a):
        return lax.ppermute(a, ALL, self.table(lambda d, z: (d, z + (1 if d % 2 == 0 else self.n_z - 1))))

    def z_far(self, a):
        return lax.ppermute(a, ALL, self.table(lambda d, z: (d, z + 2)))

    def z_flip(self, a, bit):
        return lax.ppermute(a, ALL, self.table(lambda d, z: (d, z ^ bit)))

    def diagonal(self, a):
        return lax.ppermute(a, ALL, self.table(lambda d, z: (d ^ 6, z)))


def spread(routes, block):
    own = around(routes, block)
    return own + [routes.core(b) for b in own]


def around(routes, block):
    return [block, routes.first(block), routes.second(block), routes.diagonal(block)]


def holder(meta, t):
    flip = t // 4
    cc = meta[I_C] if flip == 0 else 1 - meta[I_C]
    x, y = meta[I_X], meta[I_Y]
    t = t % 4
    if t == 1:
        x, y = x ^ (1 - cc), y ^ cc
    elif t == 2:
        x, y = x ^ cc, y ^ (1 - cc)
    elif t == 3:
        x, y = x ^ 1, y ^ 1
    return cc, x, y


def gather_mixed(routes, near, far):
    near = routes.z_near(near)
    far = routes.z_far(far)
    block = jnp.concatenate([near, far], axis=1)
    one = routes.first(block)
    two = routes.second(block)
    own = [block, one, two, routes.second(one)]
    return own + [routes.core(b) for b in own], (near, far)


def mixed_copies(meta, shard, blocks, w, sems):
    rows, wide = shard.shape
    quarter, part = rows // 4, wide // 2
    z = meta[I_Z]
    out = [(shard, w.at[pl.ds(pl.multiple_of(z * rows, 16), rows)])]
    for t, block in enumerate(blocks):
        cc, x, y = holder(meta, t)
        q = 2 * y + x
        plane = lax.rem(z + jnp.where(cc == 0, 3, 1), 4)
        far = lax.rem(z + 2, 4)
        out.append((block.at[:, pl.ds(0, wide)],
                    w.at[pl.ds(pl.multiple_of(plane * rows + q * quarter, 16), quarter)]))
        out.append((block.at[:, pl.ds(wide, part)],
                    w.at[pl.ds(pl.multiple_of(far * rows + q * quarter, 16), quarter),
                         pl.ds(pl.multiple_of(cc * part, 128), part)]))
    return [pltpu.make_async_copy(s, d, sems.at[i]) for i, (s, d) in enumerate(out)]


PARTS = ((1, 0), (2, 1))


def piece_rows(ng, rows, d):
    return 4 * ng * (rows // 4) + ng * (d // 128) * 32


def pack_body(pos, *refs):
    w_qkv, w_out = refs[0:2]
    vecs, b1, f1, f2 = refs[2:8], refs[8], refs[9], refs[10]
    mixed, near, far = refs[11:14]
    outs, sems = refs[14:16], refs[16]
    c, x, y = pos[0] & 1, (pos[0] >> 1) & 1, (pos[0] >> 2) & 1
    p = 2 * y + x
    d = w_out.shape[1]
    rows = w_out.shape[0]
    quarter = rows // 4
    ff = f1.shape[1]
    copies = []
    for out, (ng, go) in zip(outs, PARTS):
        for zz in range(4):
            for g in range(ng):
                col = pl.multiple_of(zz * (ff // 4) + c * (ff // 8) + (go + g) * 128, 128)
                copies.append((f1.at[pl.ds(pl.multiple_of(p * quarter, 16), quarter), pl.ds(col, 128)],
                               out.at[pl.ds((zz * ng + g) * quarter, quarter)]))
        base = 4 * ng * quarter
        for g in range(ng):
            row = pl.multiple_of(c * (ff // 8) + (go + g) * 128 + p * 32, 32)
            for k in range(d // 128):
                copies.append((f2.at[pl.ds(row, 32), pl.ds(k * 128, 128)],
                               out.at[pl.ds(base + (g * (d // 128) + k) * 32, 32)]))
    copies = [pltpu.make_async_copy(s, t, sems.at[i]) for i, (s, t) in enumerate(copies)]
    for cp in copies:
        cp.start()
    mixed[:, 0 : 3 * d] = w_qkv[...]
    mixed[:, 3 * d : 4 * d] = w_out[...]
    lines = [v[...].astype(F32).reshape(1, rows) for v in vecs] + [jnp.zeros((128 - len(vecs), rows), F32)]
    mixed[:, 4 * d : 4 * d + 128] = jnp.concatenate(lines, axis=0).T.astype(BF16)
    n = b1.shape[0] // 128
    lines = [b1[pl.ds(128 * i, 128)].astype(F32).reshape(1, 128) for i in range(n)] + [jnp.zeros((rows - n, 128), F32)]
    mixed[:, 4 * d + 128 :] = jnp.concatenate(lines, axis=0).astype(BF16)
    own = pl.ds(pl.multiple_of(p * quarter, 16), quarter)
    near[...] = mixed[own, :]
    part = mixed.shape[1] // 2
    far[...] = mixed[own, pl.ds(pl.multiple_of(c * part, 128), part)]
    for cp in copies:
        cp.wait()


def pack(pos, w_qkv, w_out, vecs, b1, f1, f2):
    rows, d = w_out.shape
    wide = 4 * d + EXT
    sd = jax.ShapeDtypeStruct
    count = sum(4 * ng + ng * (d // 128) for ng, _ in PARTS)
    return pl.pallas_call(
        pack_body,
        in_specs=[pl.BlockSpec(memory_space=pltpu.SMEM)] + [WHOLE] * 9 + [ANY] * 2,
        out_specs=[WHOLE] * 5,
        scratch_shapes=[pltpu.SemaphoreType.DMA((count,))],
        out_shape=[sd((rows, wide), BF16), sd((rows // 4, wide), BF16), sd((rows // 4, wide // 2), BF16)]
        + [sd((piece_rows(ng, rows, d), 128), BF16) for ng, _ in PARTS],
        compiler_params=params(),
        name="pack",
    )(pos, w_qkv, w_out, *vecs, b1, f1, f2)


def norm_stats(rows):
    centred = rows - jnp.mean(rows, axis=-1, keepdims=True)
    inverse = lax.rsqrt(jnp.mean(centred * centred, axis=-1, keepdims=True) + EPS)
    return centred * inverse, inverse


def norm_back(grad, normed, inverse, gain):
    e = grad * gain
    return inverse * (
        e - jnp.mean(e, axis=-1, keepdims=True) - normed * jnp.mean(e * normed, axis=-1, keepdims=True)
    )


def lane_masks():
    lane = lax.broadcasted_iota(jnp.int32, (1, 2 * HEAD), 1)
    low = jnp.where(lane < HEAD, 1.0, 0.0).astype(BF16)
    return low, (1.0 - low.astype(F32)).astype(BF16)


def k1_body(meta, *refs):
    tok, cot = refs[0:4], refs[4:8]
    shard, blocks = refs[8], refs[9:17]
    qkv_o, prob_o, o_o, x1_o, a2_o, a1_o, gp_o, w_o, vec_o, b1_o, dbf_o = refs[17:28]
    w, vec, sems, out_sem = refs[28:]
    b = pl.program_id(0)
    d = w.shape[0]

    @pl.when(b == 0)
    def _():
        copies = mixed_copies(meta, shard, blocks, w, sems)
        for cp in copies:
            cp.start()
        for cp in copies:
            cp.wait()
        pltpu.make_async_copy(w, w_o, out_sem).start()
        ext = w[:, 4 * d : 4 * d + 128].astype(F32).T
        vec[...] = ext[0:16]
        vec_o[...] = ext[0:16]
        dbf_o[...] = jnp.zeros_like(dbf_o)
        rows = d // 4
        for zz in range(4):
            for r in range(b1_o.shape[1] // 128):
                b1_o[zz : zz + 1, 128 * r : 128 * (r + 1)] = w[
                    zz * rows : zz * rows + 8, 4 * d + 128 : 4 * d + 256
                ].astype(F32)[r : r + 1]

    g1, s1, b_out = vec[0:1], vec[1:2], vec[2:3]
    g2, s2 = vec[3:4], vec[4:5]
    x = jnp.concatenate([r[...] for r in tok], axis=0).astype(F32)
    g = jnp.concatenate([r[...] for r in cot], axis=0)
    gp_o[...] = g
    dbf_o[0:1] += jnp.sum(g.astype(F32), axis=0, keepdims=True)
    n1, _ = norm_stats(x)
    a1 = (n1 * g1 + s1).astype(BF16)
    a1_o[...] = a1
    for k in range(3):
        qkv_o[:, k * d : (k + 1) * d] = nn(a1, w[:, k * d : (k + 1) * d]).astype(BF16)
    row = lax.broadcasted_iota(jnp.int32, (BLOCK, BLOCK), 0) // UNIT
    col = lax.broadcasted_iota(jnp.int32, (BLOCK, BLOCK), 1) // UNIT
    keep = (row == col) | (b < meta[I_LONG])
    low, high = lane_masks()
    for j in range(HEADS // 2):
        s = slice(128 * j, 128 * (j + 1))
        q = qkv_o[:, s]
        k = qkv_o[:, d + 128 * j : d + 128 * (j + 1)]
        v = qkv_o[:, 2 * d + 128 * j : 2 * d + 128 * (j + 1)]
        mixed = None
        for h, m in ((0, low), (1, high)):
            sc = jnp.where(keep, nt(q * m, k) * SCALE, NEG)
            e = jnp.exp(sc - jnp.max(sc, axis=-1, keepdims=True))
            p = (e * (1.0 / jnp.sum(e, axis=-1, keepdims=True))).astype(BF16)
            prob_o[0, 2 * j + h] = p
            part = nn(p, v * m)
            mixed = part if mixed is None else mixed + part
        o_o[:, s] = mixed.astype(BF16)
    x1 = x + (nn(o_o[...], w[:, 3 * d : 4 * d]) + b_out)
    x1_o[...] = x1
    n2, _ = norm_stats(x1)
    a2_o[...] = (n2 * g2 + s2).astype(BF16)

    @pl.when(b == pl.num_programs(0) - 1)
    def _():
        pltpu.make_async_copy(w, w_o, out_sem).wait()


def unit_spec(i, d):
    return pl.BlockSpec((UNIT, d), lambda b, meta: (meta[PER * b + i], 0))


def k1(meta, tokens, cot, shard, blocks, ff):
    t, d = tokens.shape
    nb = t // BLOCK
    wide = shard.shape[1]
    blk = lambda n: pl.BlockSpec((BLOCK, n), lambda b, meta: (b, 0))
    fixed = lambda s: pl.BlockSpec(s, lambda b, meta: (0,) * len(s))
    sd = jax.ShapeDtypeStruct
    return pl.pallas_call(
        k1_body,
        grid_spec=pltpu.PrefetchScalarGridSpec(
            num_scalar_prefetch=1,
            grid=(nb,),
            in_specs=[unit_spec(i, d) for i in range(PER)] * 2 + [ANY] * 9,
            out_specs=[
                blk(3 * d),
                pl.BlockSpec((1, HEADS, BLOCK, BLOCK), lambda b, meta: (b, 0, 0, 0)),
                blk(d), blk(d), blk(d), blk(d), blk(d), ANY,
                fixed((16, d)), fixed((4, ff // 4)), fixed((8, d)),
            ],
            scratch_shapes=[
                pltpu.VMEM((d, wide), BF16),
                pltpu.VMEM((16, d), F32),
                pltpu.SemaphoreType.DMA((17,)),
                pltpu.SemaphoreType.DMA,
            ],
        ),
        out_shape=[
            sd((t, 3 * d), BF16), sd((nb, HEADS, BLOCK, BLOCK), BF16), sd((t, d), BF16), sd((t, d), F32),
            sd((t, d), BF16), sd((t, d), BF16), sd((t, d), BF16), sd((d, wide), BF16),
            sd((16, d), F32), sd((4, ff // 4), F32), sd((8, d), F32),
        ],
        compiler_params=params(),
        cost_estimate=pl.CostEstimate(flops=2 * t * d * 5 * d, bytes_accessed=40 << 20, transcendentals=t * BLOCK * HEADS),
        name="norm_qkv_attend",
    )(meta, *([tokens] * PER), *([cot] * PER), shard, *blocks)


def gelu_and_slope(z):
    t = 1.0 / (1.0 + (0.3275911 * RSQRT2) * jnp.abs(z))
    e = jnp.exp(-0.5 * z * z)
    poly = t * (0.5 * 0.254829592 + t * (-0.5 * 0.284496736 + t * (0.5 * 1.421413741 + t * (
        -0.5 * 1.453152027 + t * (0.5 * 1.061405429)))))
    tail = poly * e
    cdf = jnp.where(z >= 0.0, 1.0 - tail, tail)
    return z * cdf, cdf + z * e * RSQRT_TAU


def mlp_body(ng, go, first, meta, *refs):
    a2o, a2p, g_o, g_p, b1, f1, f2 = refs[0:7]
    blocks = refs[7:11]
    at = 11
    prev = None
    if not first:
        prev, at = refs[11:15], 15
    yo, do, yp, dp, send, keep, db = refs[at : at + 7]
    a2, g, u_s, dz_s, w1, w2, dw1, dw2, sems = refs[at + 7 :]
    b = pl.program_id(0)
    last = pl.num_programs(0) - 1
    t, d = a2o.shape
    nb = t // BLOCK
    n = 128 * ng
    c, x, y, z = meta[I_C], meta[I_X], meta[I_Y], meta[I_Z]
    rows = f1.shape[0]
    quarter = rows // 4
    nk = d // 128

    def loads():
        ff = f1.shape[1]
        early = [(a2o, a2.at[pl.ds(0, t)]), (g_o, g.at[pl.ds(0, t)])]
        for zz in range(4):
            col = pl.multiple_of(zz * (ff // 4) + c * (ff // 8) + go * 128, 128)
            early.append((f1.at[:, pl.ds(col, n)], w1.at[pl.ds(pl.multiple_of(z * rows, 16), rows), pl.ds(zz * n, n)]))
        row = pl.multiple_of(c * (ff // 8) + go * 128, 128)
        early.append((f2.at[pl.ds(row, n)], w2.at[pl.ds(pl.multiple_of(z * n, 128), n)]))
        late = [(a2p, a2.at[pl.ds(t, t)]), (g_p, g.at[pl.ds(t, t)])]
        cps = [pltpu.make_async_copy(s, q, sems.at[i]) for i, (s, q) in enumerate(early + late)]
        return cps[: len(early)], cps[len(early) :]

    @pl.when(b == 0)
    def _():
        early, late = loads()
        for cp in early + late:
            cp.start()
        db[...] = jnp.zeros_like(db)
        for k, blk in enumerate(blocks):
            xx, yy = x, y
            if k == 1:
                xx, yy = x ^ (1 - c), y ^ c
            elif k == 2:
                xx, yy = x ^ c, y ^ (1 - c)
            elif k == 3:
                xx, yy = x ^ 1, y ^ 1
            p = 2 * yy + xx

            def place(f, carry):
                plane = z ^ (f + 1)
                r1 = pl.ds(pl.multiple_of(plane * rows + p * quarter, 16), quarter)
                for j in range(4 * ng):
                    w1[r1, j * 128 : (j + 1) * 128] = blk[f, j * quarter : (j + 1) * quarter, :]
                for gg in range(ng):
                    r2 = pl.ds(pl.multiple_of(plane * n + gg * 128 + p * 32, 32), 32)
                    for kk in range(nk):
                        lo = 4 * ng * quarter + (gg * nk + kk) * 32
                        w2[r2, kk * 128 : (kk + 1) * 128] = blk[f, lo : lo + 32, :]
                return carry

            lax.fori_loop(0, 3, place, 0)
        for cp in early:
            cp.wait()

    @pl.when(b == nb)
    def _():
        for cp in loads()[1]:
            cp.wait()

    rr = pl.ds(pl.multiple_of(b * BLOCK, BLOCK), BLOCK)
    a = a2[rr, :]
    gr = g[rr, :]
    per = 2 // ng
    for k in range(2 * ng):
        cols = slice(k * 256, (k + 1) * 256)
        lane = pl.ds(pl.multiple_of(c * (b1.shape[1] // 2) + go * 128, 128), n)
        bias = jnp.concatenate([b1[zz : zz + 1, lane] for zz in range(k * per, (k + 1) * per)], axis=1)
        u, s = gelu_and_slope(nn(a, w1[:, cols]) + bias)
        u_s[rr, cols] = u.astype(BF16)
        dz = (nt(gr, w2[cols, :]) * s).astype(BF16)
        dz_s[rr, cols] = dz
        db[0:1, cols] += jnp.sum(dz.astype(F32), axis=0, keepdims=True)
    yv = nn(u_s[rr, :], w2[...])
    dv = nt(dz_s[rr, :], w1[...])

    def put(y_ref, d_ref, y_old, d_old):
        y_ref[...] = (yv if y_old is None else yv + y_old[...].astype(F32)).astype(BF16)
        d_ref[...] = (dv if d_old is None else dv + d_old[...].astype(F32)).astype(BF16)

    @pl.when(b < nb)
    def _():
        put(yo, do, *((None, None) if first else prev[0:2]))

    @pl.when(b >= nb)
    def _():
        put(yp, dp, *((None, None) if first else prev[2:4]))

    @pl.when(b == last)
    def _():
        for k in range(2 * ng):
            cols = slice(k * 256, (k + 1) * 256)
            dw1[:, cols] = tn(a2[...], dz_s[:, cols]).astype(BF16)
            dw2[cols, :] = tn(u_s[:, cols], g[...]).astype(BF16)
        for out, sel in ((send, 1 - meta[I_B1]), (keep, meta[I_B1])):
            for i in range(2):

                def cut(plane, carry):
                    r1 = pl.ds(pl.multiple_of(plane * rows + sel * 2 * quarter + i * quarter, 16), quarter)
                    for j in range(4 * ng):
                        out[i, plane, j * quarter : (j + 1) * quarter, :] = dw1[r1, j * 128 : (j + 1) * 128]
                    for gg in range(ng):
                        r2 = pl.ds(pl.multiple_of(plane * n + gg * 128 + sel * 64 + i * 32, 32), 32)
                        for kk in range(nk):
                            lo = 4 * ng * quarter + (gg * nk + kk) * 32
                            out[i, plane, lo : lo + 32, :] = dw2[r2, kk * 128 : (kk + 1) * 128]
                    return carry

                lax.fori_loop(0, 4, cut, 0)


def mlp(part, meta, a2o, a2p, g_o, g_p, b1, f1, f2, blocks, prev=()):
    ng, go = PARTS[part]
    first = not prev
    t, d = a2o.shape
    nb = t // BLOCK
    n = 128 * ng
    size = blocks[0].shape[1]
    sd = jax.ShapeDtypeStruct
    fixed = lambda s: pl.BlockSpec(s, lambda i, meta: (0,) * len(s), pipeline_mode=pl.Buffered(1))
    outf = lambda s: pl.BlockSpec(s, lambda i, meta: (0,) * len(s))
    own = pl.BlockSpec((BLOCK, d), lambda i, meta: (jnp.minimum(i, nb - 1), 0))
    other = pl.BlockSpec((BLOCK, d), lambda i, meta: (jnp.maximum(i - nb, 0), 0))
    tok = sd((t, d), BF16)
    half = (2, 4, size, 128)
    return pl.pallas_call(
        functools.partial(mlp_body, ng, go, first),
        grid_spec=pltpu.PrefetchScalarGridSpec(
            num_scalar_prefetch=1,
            grid=(2 * nb,),
            in_specs=[ANY] * 4 + [fixed(b1.shape)] + [ANY] * 2 + [fixed(k.shape) for k in blocks]
            + ([] if first else [own, own, other, other]),
            out_specs=[own, own, other, other, outf(half), outf(half), outf((8, 4 * n))],
            scratch_shapes=[
                pltpu.VMEM((2 * t, d), BF16), pltpu.VMEM((2 * t, d), BF16),
                pltpu.VMEM((2 * t, 4 * n), BF16), pltpu.VMEM((2 * t, 4 * n), BF16),
                pltpu.VMEM((d, 4 * n), BF16), pltpu.VMEM((4 * n, d), BF16),
                pltpu.VMEM((d, 4 * n), BF16), pltpu.VMEM((4 * n, d), BF16),
                pltpu.SemaphoreType.DMA((9,)),
            ],
        ),
        out_shape=[tok, tok, tok, tok, sd(half, BF16), sd(half, BF16), sd((8, 4 * n), F32)],
        compiler_params=params(),
        cost_estimate=pl.CostEstimate(flops=2 * 2 * t * d * 4 * n * 6, bytes_accessed=30 << 20, transcendentals=2 * t * 4 * n),
        name="hidden_first" if first else "hidden_second",
    )(meta, a2o, a2p, g_o, g_p, b1, f1, f2, *blocks, *prev)


def back_body(first, start, meta, *refs):
    tok = refs[0:4]
    gp, da_o, da_p, x1_r, prob, qkv, w, vec = refs[4:12]
    if first:
        acc_in, at = refs[12], 13
    else:
        acc_in, at = refs[12], 14
    gt_o, dqkv, dx1l, acc = refs[at : at + 4]
    gt, sems = refs[at + 4 :]
    b = pl.program_id(0)
    nb = pl.num_programs(0)
    d = da_o.shape[1]
    slot = lax.rem(b, 2)

    def puts(step, sl):
        return [
            pltpu.make_async_copy(
                gt.at[sl, pl.ds(i * UNIT, UNIT)],
                gt_o.at[pl.ds(pl.multiple_of(meta[PER * (step + start) + i] * UNIT, UNIT), UNIT)],
                sems.at[sl, i],
            )
            for i in range(PER)
        ]

    @pl.when(b == 0)
    def _():
        if first:
            acc[...] = jnp.zeros_like(acc)
            acc[5:6] = acc_in[0:1]
        else:
            acc[...] = acc_in[...]

    @pl.when(b >= 2)
    def _():
        for cp in puts(b - 2, slot):
            cp.wait()

    g1, g2 = vec[0:1], vec[3:4]
    da2 = da_o[...].astype(F32) + da_p[...].astype(F32)
    n2, r2 = norm_stats(x1_r[...])
    dx1 = gp[...].astype(F32) + norm_back(da2, n2, r2, g2)
    low = dx1.astype(BF16)
    acc[3:4] += jnp.sum(da2 * n2, axis=0, keepdims=True)
    acc[4:5] += jnp.sum(da2, axis=0, keepdims=True)
    acc[2:3] += jnp.sum(low.astype(F32), axis=0, keepdims=True)
    dx1l[...] = low
    do = nt(low, w[:, 3 * d : 4 * d]).astype(BF16)
    lo_m, hi_m = lane_masks()
    for j in range(HEADS // 2):
        cs = [slice(k * d + 128 * j, k * d + 128 * (j + 1)) for k in range(3)]
        q, k, v = (qkv[:, s] for s in cs)
        dop = do[:, 128 * j : 128 * (j + 1)]
        dq = dk = dv = None
        for h, m in ((0, lo_m), (1, hi_m)):
            p = prob[0, 2 * j + h]
            dom = dop * m
            dp = nt(dom, v)
            pf = p.astype(F32)
            ds = (pf * (dp - jnp.sum(dp * pf, axis=-1, keepdims=True))).astype(BF16)
            parts = (nn(ds, k * m), tn(ds, q * m), tn(p, dom))
            dq, dk, dv = parts if dq is None else (dq + parts[0], dk + parts[1], dv + parts[2])
        dqkv[:, cs[0]] = (dq * SCALE).astype(BF16)
        dqkv[:, cs[1]] = (dk * SCALE).astype(BF16)
        dqkv[:, cs[2]] = dv.astype(BF16)
    da1 = nt(dqkv[...], w[:, 0 : 3 * d])
    x = jnp.concatenate([r[...] for r in tok], axis=0).astype(F32)
    n1, r1 = norm_stats(x)
    acc[0:1] += jnp.sum(da1 * n1, axis=0, keepdims=True)
    acc[1:2] += jnp.sum(da1, axis=0, keepdims=True)
    gt[slot] = dx1 + norm_back(da1, n1, r1, g1)
    for cp in puts(b, slot):
        cp.start()

    @pl.when(b == nb - 1)
    def _():
        for cp in puts(b - 1, 1 - slot) + puts(b, slot):
            cp.wait()


def back(start, count, meta, tokens, gp, da_o, da_p, x1, prob, qkv, w, vec, acc_in, gt_in=None):
    t, d = tokens.shape
    first = gt_in is None
    wide = w.shape[1]
    blk = lambda n: pl.BlockSpec((BLOCK, n), lambda b, meta: (b + start, 0))
    out = lambda n: pl.BlockSpec((BLOCK, n), lambda b, meta: (b, 0))
    unit = lambda i: pl.BlockSpec((UNIT, d), lambda b, meta: (meta[PER * (b + start) + i], 0))
    sd = jax.ShapeDtypeStruct
    fixed = lambda s: pl.BlockSpec(s, lambda b, meta: (0,) * len(s), pipeline_mode=pl.Buffered(1))
    ins = [tokens] * PER + [gp, da_o, da_p, x1, prob, qkv, w, vec, acc_in]
    specs = [unit(i) for i in range(PER)] + [
        blk(d), blk(d), blk(d), blk(d),
        pl.BlockSpec((1, HEADS, BLOCK, BLOCK), lambda b, meta: (b + start, 0, 0, 0)), blk(3 * d),
    ] + [fixed(a.shape) for a in (w, vec, acc_in)]
    alias = {}
    if not first:
        alias = {1 + len(ins): 0}
        ins, specs = ins + [gt_in], specs + [ANY]
    return pl.pallas_call(
        functools.partial(back_body, first, start),
        grid_spec=pltpu.PrefetchScalarGridSpec(
            num_scalar_prefetch=1,
            grid=(count,),
            in_specs=specs,
            out_specs=[ANY, out(3 * d), out(d), pl.BlockSpec((128, d), lambda b, meta: (0, 0))],
            scratch_shapes=[pltpu.VMEM((2, BLOCK, d), F32), pltpu.SemaphoreType.DMA((2, PER))],
        ),
        out_shape=[sd((t, d), F32), sd((count * BLOCK, 3 * d), BF16), sd((count * BLOCK, d), BF16), sd((128, d), F32)],
        input_output_aliases=alias,
        compiler_params=params(),
        cost_estimate=pl.CostEstimate(
            flops=2 * count * BLOCK * d * 8 * d, bytes_accessed=20 << 20, transcendentals=0),
        name="attend_back_first" if first else "attend_back_second",
    )(meta, *ins)


def grads_body(meta, a1, dq0, dq1, o, dl0, dl1, acc, dba, dbb, send_o, keep_o, stage):
    d = a1.shape[1]
    c = meta[I_C]
    s = pl.program_id(0)
    rows = d // 4
    n = rows // 2
    t0 = dq0.shape[0]

    def split(at, width):
        for zz in range(4):
            for i in range(2):
                for out, h in ((send_o, 1 - c), (keep_o, c)):
                    lot = stage[pl.ds(pl.multiple_of(zz * rows + n * h + (n // 2) * i, 16), n // 2), 0:width]
                    out[i, 0, zz, :, pl.ds(at, width)] = lot[0 : n // 4]
                    out[i, 1, zz, :, pl.ds(at, width)] = lot[n // 4 :]

    @pl.when(s < 3)
    def _():
        stage[...] = (tn(a1[0:t0], dq0[...]) + tn(a1[t0:], dq1[...])).astype(BF16)
        split(pl.multiple_of(s * d, 128), d)

    @pl.when(s == 3)
    def _():
        stage[...] = (tn(o[0:t0], dl0[...]) + tn(o[t0:], dl1[...])).astype(BF16)
        split(3 * d, d)
        stage[:, 0:128] = acc[...].T.astype(BF16)
        stage[:, 128:256] = jnp.zeros((d, 128), BF16)
        for zz in range(4):
            parts = []
            for hh in range(2):
                for src, (ng, go) in ((dba, PARTS[0]), (dbb, PARTS[1])):
                    for k in range(ng):
                        at = (zz * ng + k) * 128
                        parts.append(jnp.where(hh == c, src[0:1, at : at + 128], 0.0))
            parts.append(jnp.zeros((16 - len(parts), 128), F32))
            stage[zz * rows : zz * rows + 16, 128:256] = jnp.concatenate(parts, axis=0).astype(BF16)
        split(4 * d, EXT)


def grads(meta, a1, dq0, dq1, o, dl0, dl1, acc, dba, dbb):
    t, d = a1.shape
    wide = 4 * d + EXT
    half = (2, 2, 4, d // 32, wide)
    sd = jax.ShapeDtypeStruct
    fixed = lambda a: pl.BlockSpec(a.shape, lambda s, meta: (0,) * a.ndim, pipeline_mode=pl.Buffered(1))
    outf = pl.BlockSpec(half, lambda s, meta: (0,) * 5)
    col = lambda a: pl.BlockSpec((a.shape[0], d), lambda s, meta: (0, jnp.minimum(s, 2)))
    return pl.pallas_call(
        grads_body,
        grid_spec=pltpu.PrefetchScalarGridSpec(
            num_scalar_prefetch=1,
            grid=(4,),
            in_specs=[fixed(a1), col(dq0), col(dq1)] + [fixed(a) for a in (o, dl0, dl1, acc, dba, dbb)],
            out_specs=[outf, outf],
            scratch_shapes=[pltpu.VMEM((d, d), BF16)],
        ),
        out_shape=[sd(half, BF16), sd(half, BF16)],
        compiler_params=params(),
        cost_estimate=pl.CostEstimate(flops=2 * t * d * 4 * d, bytes_accessed=16 << 20, transcendentals=0),
        name="weight_grads",
    )(meta, a1, dq0, dq1, o, dl0, dl1, acc, dba, dbb)


def out_body(meta, ya, yb, x1, vec, out, buf, sems):
    b = pl.program_id(0)
    slot = lax.rem(b, 2)

    def puts(step, sl):
        return [
            pltpu.make_async_copy(
                buf.at[sl, pl.ds(i * UNIT, UNIT)],
                out.at[pl.ds(pl.multiple_of(meta[PER * step + i] * UNIT, UNIT), UNIT)],
                sems.at[sl, i],
            )
            for i in range(PER)
        ]

    @pl.when(b >= 2)
    def _():
        for cp in puts(b - 2, slot):
            cp.wait()

    y = ya[...].astype(F32) + yb[...].astype(F32)
    buf[slot] = (x1[...] + (y + vec[5:6])).astype(BF16)
    for cp in puts(b, slot):
        cp.start()

    @pl.when(b == pl.num_programs(0) - 1)
    def _():
        for cp in puts(b - 1, 1 - slot) + puts(b, slot):
            cp.wait()


def layer_output(meta, ya, yb, x1, vec):
    t, d = x1.shape
    blk = lambda n: pl.BlockSpec((BLOCK, n), lambda b, meta: (b, 0))
    fixed = lambda s: pl.BlockSpec(s, lambda b, meta: (0,) * len(s), pipeline_mode=pl.Buffered(1))
    return pl.pallas_call(
        out_body,
        grid_spec=pltpu.PrefetchScalarGridSpec(
            num_scalar_prefetch=1,
            grid=(t // BLOCK,),
            in_specs=[blk(d), blk(d), blk(d), fixed(vec.shape)],
            out_specs=ANY,
            scratch_shapes=[pltpu.VMEM((2, BLOCK, d), BF16), pltpu.SemaphoreType.DMA((2, PER))],
        ),
        out_shape=jax.ShapeDtypeStruct((t, d), BF16),
        compiler_params=params(),
        cost_estimate=pl.CostEstimate(flops=4 * t * d, bytes_accessed=8 << 20, transcendentals=0),
        name="layer_out",
    )(meta, ya, yb, x1, vec)


def halve_body(jobs, meta, *refs):
    outs = refs[2 * len(jobs) :]
    for i, (place, loops) in enumerate(jobs):
        k, v = refs[2 * i : 2 * i + 2]
        bit = meta[place]
        for out, sel in ((outs[2 * i], 1 - bit), (outs[2 * i + 1], bit)):
            for pre in range(k.shape[0]):

                def step(r, carry):
                    out[pre, r] = (k[pre, sel, r].astype(F32) + v[pre, sel, r].astype(F32)).astype(BF16)
                    return carry

                lax.fori_loop(0, loops, step, 0)


def halve(meta, *jobs):
    sd = jax.ShapeDtypeStruct
    outs = []
    for _, k, _ in jobs:
        outs += [sd((k.shape[0],) + k.shape[2:], BF16)] * 2
    size = sum(k.size for _, k, _ in jobs)
    return pl.pallas_call(
        functools.partial(halve_body, tuple((place, k.shape[2]) for place, k, _ in jobs)),
        in_specs=[pl.BlockSpec(memory_space=pltpu.SMEM)] + [WHOLE] * (2 * len(jobs)),
        out_specs=[WHOLE] * len(outs),
        out_shape=outs,
        compiler_params=params(),
        cost_estimate=pl.CostEstimate(flops=size, bytes_accessed=6 * size, transcendentals=0),
        name="add_halve",
    )(meta, *(a for _, k, v in jobs for a in (k, v)))


def total(routes, k, v):
    piece = k.astype(F32) + v.astype(F32)
    if routes.n_dp > 8:
        groups = [[j + 8 * o for o in range(routes.n_dp // 8)] for j in range(8)]
        piece = lax.psum(piece, "dp", axis_index_groups=groups)
    return piece.astype(BF16)


def ranks(meta, t):
    cc, x, y = holder(meta, t)
    return cc, 2 * jnp.where(cc == 0, x, y) + jnp.where(cc == 0, y, x)


def final_hidden_body(meta, *refs):
    pieces = refs[:8]
    d1, d2 = refs[8:10]
    rows, ff = d1.shape
    d = d2.shape[1]
    quarter = rows // 4
    nk = d // 128
    for t in range(8):
        cc, q = ranks(meta, t)
        at = 0
        for ng, go in PARTS:
            r1 = pl.ds(pl.multiple_of(q * quarter, 16), quarter)
            for zz in range(4):
                for g in range(ng):
                    col = pl.multiple_of(zz * (ff // 4) + cc * (ff // 8) + (go + g) * 128, 128)
                    d1[r1, pl.ds(col, 128)] = pieces[t][at : at + quarter, :].astype(F32)
                    at += quarter
            for g in range(ng):
                r2 = pl.ds(pl.multiple_of(cc * (ff // 8) + (go + g) * 128 + q * 32, 32), 32)
                for k in range(nk):
                    d2[r2, k * 128 : (k + 1) * 128] = pieces[t][at : at + 32, :].astype(F32)
                    at += 32


def final_mixed_body(meta, *refs):
    pieces = refs[:8]
    dqkv, dout, dg1, ds1, dbo, dg2, ds2, dbf, db1 = refs[8:17]
    ext = refs[17]
    n = pieces[0].shape[0]
    d = dout.shape[1]
    for t in range(8):
        cc, x, y = holder(meta, t)
        first, second = jnp.where(cc == 0, x, y), jnp.where(cc == 0, y, x)
        rows = pl.ds(pl.multiple_of(n * (4 * cc + 2 * first + second), n), n)
        v = pieces[t][...].astype(F32)
        dqkv[rows, :] = v[:, 0 : 3 * d]
        dout[rows, :] = v[:, 3 * d : 4 * d]
        ext[rows, :] = v[:, 4 * d :]
    vec = ext[:, 0:128].T
    for i, ref in enumerate((dg1, ds1, dbo, dg2, ds2, dbf)):
        ref[...] = vec[i]
    for r in range(db1.shape[0] // 128):
        db1[pl.ds(128 * r, 128)] = ext[r, 128:256]


def final(body, meta, pieces, outs, scratch=()):
    sd = [jax.ShapeDtypeStruct(s, F32) for s in outs]
    res = pl.pallas_call(
        body,
        in_specs=[pl.BlockSpec(memory_space=pltpu.SMEM)] + [WHOLE] * 8,
        out_specs=[WHOLE] * len(outs),
        scratch_shapes=list(scratch),
        out_shape=sd,
        compiler_params=params(),
        name="place_sums",
    )(meta, *pieces)
    return res


def scalars(chip_ids):
    n = chip_ids.shape[0] // UNIT
    ids = chip_ids.reshape(n, UNIT)[:, 0]
    here = jnp.arange(n, dtype=jnp.int32)
    same = (ids[:, None] == ids[None, :]).astype(jnp.int32)
    long = jnp.sum(same, axis=1) > 1
    longs = long.astype(jnp.int32)
    before = jnp.sum(jnp.where(here[None, :] < here[:, None], longs[None, :], 0), axis=1)
    total = jnp.sum(longs)
    pos = jnp.where(long, before, total + here - before)
    src = jnp.sum(jnp.where(pos[None, :] == here[:, None], here[None, :], 0), axis=1)
    dp, z = lax.axis_index("dp"), lax.axis_index("fsdp")
    c, x, y = dp & 1, (dp >> 1) & 1, (dp >> 2) & 1
    b1, b2 = jnp.where(c == 0, x, y), jnp.where(c == 0, y, x)
    rest = jnp.stack([total >> 2, c, x, y, z, b1, b2, jnp.zeros_like(z), z & 1, z >> 1]).astype(jnp.int32)
    return jnp.concatenate([src.astype(jnp.int32), rest])


def on_device(n_dp, n_z, tokens, chip_ids, ln1_gain, ln1_bias, w_qkv, w_out, b_out, ln2_gain, ln2_bias,
              w_fc1, b_fc1, w_fc2, b_fc2, cotangent):
    routes = Routes(n_dp, n_z)
    t, d = tokens.shape
    ff = w_fc1.shape[1]
    rows = w_qkv.shape[0]
    pos = lax.axis_index("dp").astype(jnp.int32).reshape(1)
    meta = scalars(chip_ids)

    vecs = (ln1_gain, ln1_bias, b_out, ln2_gain, ln2_bias, b_fc2)
    mixed, near, far, ha, hb = pack(pos, w_qkv, w_out, vecs, b_fc1, w_fc1, w_fc2)

    p_mixed, got = gather_mixed(routes, near, far)

    def planes(own, other):
        return routes.z_flip(jnp.stack([own, other]), 2)

    join = lambda other, two: jnp.concatenate([other[None], two], axis=0)
    mate_a = routes.z_flip(tie(ha, *got), 1)
    two_a = planes(ha, mate_a)
    mate_b = routes.z_flip(tie(hb, mate_a), 1)
    block_a = join(mate_a, two_a)
    p_a = around(routes, block_a)
    two_b = planes(hb, tie(mate_b, block_a))
    qkv, prob, o, x1, a2, a1, gp, w, vec, b1, dbf = k1(meta, tokens, cotangent, tie(mixed, block_a), p_mixed, ff)
    block_b = join(mate_b, tie(two_b, a2))
    p_b = around(routes, block_b)

    swap = lax.optimization_barrier((a2, gp, block_b, *p_a))
    a2p, gpp = routes.core(swap[0]), routes.core(swap[1])
    *part, sa, ka, dba = mlp(0, meta, a2, a2p, gp, gpp, b1, w_fc1, w_fc2, p_a)
    got_a = routes.first(sa)
    yo, do, yp, dp, sb, kb, dbb = mlp(1, meta, a2, a2p, gp, gpp, b1, w_fc1, w_fc2, p_b, part)

    def view(a, pre, rest):
        return a.reshape((pre, 2) + rest)

    tall = lambda a: (4 * a.shape[2] // 96, 96, 128)
    flat = lambda a: (a.shape[2] // 96, 96, 128)
    size_a, size_b = tall(sa), tall(sb)
    s_a, k_a = halve(meta, (I_B2, view(ka, 1, size_a), view(got_a, 1, size_a)))
    dp, yp, sb = lax.optimization_barrier((dp, yp, sb, got_a))[:3]
    dq = routes.core(dp)
    yq = routes.core(yp)
    got_a, got_b = routes.second(s_a), routes.first(sb)
    gt, dq0, dl0, acc = back(0, 2, meta, tokens, tie(gp, s_a), do, dq, x1, prob, qkv, w, vec, dbf)

    lo_a, lo_b = (2, 2) + flat(sa), (2, 2) + flat(sb)
    s_a, k_a, s_b, k_b = halve(meta, (I_Z + 4, k_a.reshape(lo_a), tie(got_a, acc).reshape(lo_a)),
                               (I_B2, view(kb, 1, size_b), view(tie(got_b, acc), 1, size_b)))
    got_a, got_b = routes.z_flip(s_a, 1), routes.second(s_b)
    gt, dq1, dl1, acc = back(2, 2, meta, tokens, tie(gp, s_a, yq), do, dq, x1, prob, qkv, w, vec, acc, gt)

    hi_a, hi_b = (1,) + lo_a[1:], (1,) + lo_b[1:]
    s_a, k_a, s_b, k_b = halve(meta, (I_Z + 5, k_a.reshape(hi_a), tie(got_a, acc).reshape(hi_a)),
                               (I_Z + 4, k_b.reshape(lo_b), tie(got_b, acc).reshape(lo_b)))
    got_a, got_b = routes.z_flip(s_a, 2), routes.z_flip(s_b, 1)
    sm, km = grads(meta, tie(a1, s_a), dq0, dq1, o, dl0, dl1, acc, dba, dbb)

    got_m = routes.core(tie(sm, got_a, got_b))
    s_b, k_b = halve(meta, (I_Z + 5, k_b.reshape(hi_b), tie(got_b, sm).reshape(hi_b)))
    got_b = routes.z_flip(s_b, 2)
    wide = sm.shape[-1]
    shape = (1, 2, 8, d // 32, wide)
    s_m, k_m = halve(meta, (I_B1, km.reshape(shape), tie(got_m, s_b).reshape(shape)))
    shape = (1, 2, 4, d // 32, wide)
    got_m = routes.first(s_m)
    layer_out = layer_output(meta, yo, yq, x1, tie(vec, s_m))
    joint = lambda a, b: jnp.concatenate([a.reshape(-1, 128), b.reshape(-1, 128)], axis=0)
    near_by = around(routes, total(routes, joint(k_a, k_b), joint(got_a, tie(got_b, s_m))))
    s_m, k_m = halve(meta, (I_B2, k_m.reshape(shape), tie(got_m, layer_out).reshape(shape)))
    shape = (2, 2, 1, d // 32, wide)
    s_m, k_m = halve(meta, (I_Z + 4, k_m.reshape(shape), routes.second(s_m).reshape(shape)))
    shape = (1, 2, 1, d // 32, wide)
    got_m = tie(routes.z_flip(s_m, 1), *near_by)
    pieces = near_by + [routes.core(b) for b in near_by]
    s_m, k_m = halve(meta, (I_Z + 5, k_m.reshape(shape), got_m.reshape(shape)))
    got_m = tie(routes.z_flip(s_m, 2), *pieces)
    pieces_m = spread(routes, total(routes, k_m.reshape(-1, wide), got_m.reshape(-1, wide)))
    g_fc1, g_fc2 = final(final_hidden_body, meta, pieces, [w_fc1.shape, w_fc2.shape])

    vecs = [(rows,)] * 6
    g_qkv, g_out, dg1, ds1, dbo, dg2, ds2, dbf2, db1 = final(
        final_mixed_body, meta, pieces_m, [w_qkv.shape, w_out.shape, *vecs, b_fc1.shape],
        [pltpu.VMEM((rows, EXT), F32)])
    return (layer_out, gt, dg1, ds1, g_qkv, g_out, dbo, dg2, ds2, g_fc1, db1, g_fc2, dbf2)


def solution(mesh):
    token, part, plain = P(ALL, None), P("fsdp", None), P("fsdp")
    return jax.shard_map(
        functools.partial(on_device, mesh.shape["dp"], mesh.shape["fsdp"]),
        mesh=mesh,
        in_specs=(token, P(ALL), plain, plain, part, part, plain, plain, plain, part, plain, part, plain, token),
        out_specs=(token, token, plain, plain, part, part, plain, plain, plain, part, plain, part, plain),
        check_vma=False,
    )
```

```python
import functools
import math

import jax
import jax.numpy as jnp
from jax import lax
from jax.experimental import pallas as pl
from jax.experimental.pallas import tpu as pltpu
from jax.sharding import PartitionSpec as P

HEADS = 12
HEAD = 64
UNIT = 64
BLOCK = 256
PER = BLOCK // UNIT
EPS = 1e-05
NEG = -1e30
RSQRT2 = 1.0 / math.sqrt(2.0)
RSQRT_TAU = 1.0 / math.sqrt(2.0 * math.pi)
SCALE = 1.0 / math.sqrt(HEAD)
EXT = 256
VMEM_LIMIT = 64 * 1024 * 1024 - 65536
ALL = ("dp", "fsdp")
F32 = jnp.float32
BF16 = jnp.bfloat16

I_LONG, I_C, I_X, I_Y, I_Z, I_B1, I_B2 = 16, 17, 18, 19, 20, 21, 22


def nn(a, b):
    return lax.dot_general(a, b, (((1,), (0,)), ((), ())), preferred_element_type=F32)


def nt(a, b):
    return lax.dot_general(a, b, (((1,), (1,)), ((), ())), preferred_element_type=F32)


def tn(a, b):
    return lax.dot_general(a, b, (((0,), (0,)), ((), ())), preferred_element_type=F32)


SHORT = pl.CostEstimate(flops=1, bytes_accessed=1, transcendentals=0)


def params(**kw):
    return pltpu.CompilerParams(vmem_limit_bytes=VMEM_LIMIT, **kw)


ANY = pl.BlockSpec(memory_space=pl.ANY)
WHOLE = pl.BlockSpec(memory_space=pltpu.VMEM)


def tie(a, *after):
    return lax.optimization_barrier((a,) + after)[0]


class Routes:
    def __init__(self, n_dp, n_z):
        self.n_dp, self.n_z = n_dp, n_z

    def table(self, move):
        pairs = []
        for d in range(self.n_dp):
            for z in range(self.n_z):
                e, w = move(d, z)
                pairs.append((d * self.n_z + z, e * self.n_z + w % self.n_z))
        return pairs

    def core(self, a):
        return lax.ppermute(a, ALL, self.table(lambda d, z: (d ^ 1, z)))

    def first(self, a):
        return lax.ppermute(a, ALL, self.table(lambda d, z: (d ^ (2 if d % 2 == 0 else 4), z)))

    def second(self, a):
        return lax.ppermute(a, ALL, self.table(lambda d, z: (d ^ (4 if d % 2 == 0 else 2), z)))

    def z_near(self, a):
        return lax.ppermute(a, ALL, self.table(lambda d, z: (d, z + (1 if d % 2 == 0 else self.n_z - 1))))

    def z_far(self, a):
        return lax.ppermute(a, ALL, self.table(lambda d, z: (d, z + 2)))

    def z_flip(self, a, bit):
        return lax.ppermute(a, ALL, self.table(lambda d, z: (d, z ^ bit)))

    def diagonal(self, a):
        return lax.ppermute(a, ALL, self.table(lambda d, z: (d ^ 6, z)))


def spread(routes, block):
    own = around(routes, block)
    return own + [routes.core(b) for b in own]


def around(routes, block):
    return [block, routes.first(block), routes.second(block), routes.diagonal(block)]


def holder(meta, t):
    flip = t // 4
    cc = meta[I_C] if flip == 0 else 1 - meta[I_C]
    x, y = meta[I_X], meta[I_Y]
    t = t % 4
    if t == 1:
        x, y = x ^ (1 - cc), y ^ cc
    elif t == 2:
        x, y = x ^ cc, y ^ (1 - cc)
    elif t == 3:
        x, y = x ^ 1, y ^ 1
    return cc, x, y


def gather_mixed(routes, near, far, early, late):
    block = jnp.concatenate([routes.z_near(near), routes.z_far(far)], axis=1)
    block = tie(block, early)
    one = routes.first(block)
    two = routes.second(block)
    own = [block, one, two, routes.second(tie(one, *late))]
    return own + [routes.core(b) for b in own]


def mixed_copies(meta, shard, blocks, w, sems):
    rows, wide = shard.shape
    quarter, part = rows // 4, wide // 2
    z = meta[I_Z]
    out = [(shard, w.at[pl.ds(pl.multiple_of(z * rows, 16), rows)])]
    for t, block in enumerate(blocks):
        cc, x, y = holder(meta, t)
        q = 2 * y + x
        plane = lax.rem(z + jnp.where(cc == 0, 3, 1), 4)
        far = lax.rem(z + 2, 4)
        out.append((block.at[:, pl.ds(0, wide)],
                    w.at[pl.ds(pl.multiple_of(plane * rows + q * quarter, 16), quarter)]))
        out.append((block.at[:, pl.ds(wide, part)],
                    w.at[pl.ds(pl.multiple_of(far * rows + q * quarter, 16), quarter),
                         pl.ds(pl.multiple_of(cc * part, 128), part)]))
    return [pltpu.make_async_copy(s, d, sems.at[i]) for i, (s, d) in enumerate(out)]


PARTS = ((1, 0), (2, 1))


def piece_rows(ng, rows, d):
    return 4 * ng * (rows // 4) + ng * (d // 128) * 32


def pack_body(pos, *refs):
    w_qkv, w_out = refs[0:2]
    vecs, b1, f1, f2 = refs[2:8], refs[8], refs[9], refs[10]
    mixed, near, far = refs[11:14]
    outs, sems = refs[14:16], refs[16]
    c, x, y = pos[0] & 1, (pos[0] >> 1) & 1, (pos[0] >> 2) & 1
    p = 2 * y + x
    d = w_out.shape[1]
    rows = w_out.shape[0]
    quarter = rows // 4
    ff = f1.shape[1]
    copies = []
    for out, (ng, go) in zip(outs, PARTS):
        for zz in range(4):
            for g in range(ng):
                col = pl.multiple_of(zz * (ff // 4) + c * (ff // 8) + (go + g) * 128, 128)
                copies.append((f1.at[pl.ds(pl.multiple_of(p * quarter, 16), quarter), pl.ds(col, 128)],
                               out.at[pl.ds((zz * ng + g) * quarter, quarter)]))
        base = 4 * ng * quarter
        for g in range(ng):
            row = pl.multiple_of(c * (ff // 8) + (go + g) * 128 + p * 32, 32)
            for k in range(d // 128):
                copies.append((f2.at[pl.ds(row, 32), pl.ds(k * 128, 128)],
                               out.at[pl.ds(base + (g * (d // 128) + k) * 32, 32)]))
    copies = [pltpu.make_async_copy(s, t, sems.at[i]) for i, (s, t) in enumerate(copies)]
    for cp in copies:
        cp.start()
    mixed[:, 0 : 3 * d] = w_qkv[...]
    mixed[:, 3 * d : 4 * d] = w_out[...]
    lines = [v[...].astype(F32).reshape(1, rows) for v in vecs] + [jnp.zeros((128 - len(vecs), rows), F32)]
    mixed[:, 4 * d : 4 * d + 128] = jnp.concatenate(lines, axis=0).T.astype(BF16)
    n = b1.shape[0] // 128
    lines = [b1[pl.ds(128 * i, 128)].astype(F32).reshape(1, 128) for i in range(n)] + [jnp.zeros((rows - n, 128), F32)]
    mixed[:, 4 * d + 128 :] = jnp.concatenate(lines, axis=0).astype(BF16)
    own = pl.ds(pl.multiple_of(p * quarter, 16), quarter)
    near[...] = mixed[own, :]
    part = mixed.shape[1] // 2
    far[...] = mixed[own, pl.ds(pl.multiple_of(c * part, 128), part)]
    for cp in copies:
        cp.wait()


def pack(pos, w_qkv, w_out, vecs, b1, f1, f2):
    rows, d = w_out.shape
    wide = 4 * d + EXT
    sd = jax.ShapeDtypeStruct
    count = sum(4 * ng + ng * (d // 128) for ng, _ in PARTS)
    return pl.pallas_call(
        pack_body,
        in_specs=[pl.BlockSpec(memory_space=pltpu.SMEM)] + [WHOLE] * 9 + [ANY] * 2,
        out_specs=[WHOLE] * 5,
        scratch_shapes=[pltpu.SemaphoreType.DMA((count,))],
        out_shape=[sd((rows, wide), BF16), sd((rows // 4, wide), BF16), sd((rows // 4, wide // 2), BF16)]
        + [sd((piece_rows(ng, rows, d), 128), BF16) for ng, _ in PARTS],
        compiler_params=params(),
        name="pack",
    )(pos, w_qkv, w_out, *vecs, b1, f1, f2)


def norm_stats(rows):
    centred = rows - jnp.mean(rows, axis=-1, keepdims=True)
    inverse = lax.rsqrt(jnp.mean(centred * centred, axis=-1, keepdims=True) + EPS)
    return centred * inverse, inverse


def norm_back(grad, normed, inverse, gain):
    e = grad * gain
    return inverse * (
        e - jnp.mean(e, axis=-1, keepdims=True) - normed * jnp.mean(e * normed, axis=-1, keepdims=True)
    )


def lane_masks():
    lane = lax.broadcasted_iota(jnp.int32, (1, 2 * HEAD), 1)
    low = jnp.where(lane < HEAD, 1.0, 0.0).astype(BF16)
    return low, (1.0 - low.astype(F32)).astype(BF16)


def k1_body(meta, *refs):
    tok, cot = refs[0:4], refs[4:8]
    shard, blocks = refs[8], refs[9:17]
    qkv_o, prob_o, inv_o, o_o, x1_o, a2_o, a1_o, gp_o, w_o, vec_o, b1_o, dbf_o = refs[17:29]
    w, vec, sems, out_sem = refs[29:]
    b = pl.program_id(0)
    d = w.shape[0]

    @pl.when(b == 0)
    def _():
        copies = mixed_copies(meta, shard, blocks, w, sems)
        for cp in copies:
            cp.start()
        for cp in copies:
            cp.wait()
        pltpu.make_async_copy(w, w_o, out_sem).start()
        ext = w[:, 4 * d : 4 * d + 128].astype(F32).T
        vec[...] = ext[0:16]
        vec_o[...] = ext[0:16]
        dbf_o[...] = jnp.zeros_like(dbf_o)
        rows = d // 4
        for zz in range(4):
            for r in range(b1_o.shape[1] // 128):
                b1_o[zz : zz + 1, 128 * r : 128 * (r + 1)] = w[
                    zz * rows : zz * rows + 8, 4 * d + 128 : 4 * d + 256
                ].astype(F32)[r : r + 1]

    g1, s1, b_out = vec[0:1], vec[1:2], vec[2:3]
    g2, s2 = vec[3:4], vec[4:5]
    x = jnp.concatenate([r[...] for r in tok], axis=0).astype(F32)
    g = jnp.concatenate([r[...] for r in cot], axis=0)
    gp_o[...] = g
    dbf_o[0:1] += jnp.sum(g.astype(F32), axis=0, keepdims=True)
    n1, _ = norm_stats(x)
    a1 = (n1 * g1 + s1).astype(BF16)
    a1_o[...] = a1
    for k in range(3):
        qkv_o[:, k * d : (k + 1) * d] = nn(a1, w[:, k * d : (k + 1) * d]).astype(BF16)
    row = lax.broadcasted_iota(jnp.int32, (BLOCK, BLOCK), 0) // UNIT
    col = lax.broadcasted_iota(jnp.int32, (BLOCK, BLOCK), 1) // UNIT
    keep = (row == col) | (b < meta[I_LONG])
    low, high = lane_masks()
    left = lax.broadcasted_iota(jnp.int32, (BLOCK, 2 * HEAD), 1) < HEAD
    for j in range(HEADS // 2):
        s = slice(128 * j, 128 * (j + 1))
        q = qkv_o[:, s]
        k = qkv_o[:, d + 128 * j : d + 128 * (j + 1)]
        v = qkv_o[:, 2 * d + 128 * j : 2 * d + 128 * (j + 1)]
        mixed, inv = None, []
        for h, m in ((0, low), (1, high)):
            sc = jnp.where(keep, nt(q * (m * SCALE), k), NEG)
            e = jnp.exp(sc - jnp.max(sc, axis=-1, keepdims=True))
            inv.append(1.0 / jnp.sum(e, axis=-1, keepdims=True))
            e = e.astype(BF16)
            prob_o[0, 2 * j + h] = e
            part = nn(e, v * m)
            mixed = part if mixed is None else mixed + part
        inv = jnp.where(left, inv[0], inv[1])
        inv_o[:, s] = inv
        o_o[:, s] = (mixed * inv).astype(BF16)
    x1 = x + (nn(o_o[...], w[:, 3 * d : 4 * d]) + b_out)
    x1_o[...] = x1
    n2, _ = norm_stats(x1)
    a2_o[...] = (n2 * g2 + s2).astype(BF16)

    @pl.when(b == pl.num_programs(0) - 1)
    def _():
        pltpu.make_async_copy(w, w_o, out_sem).wait()


def unit_spec(i, d):
    return pl.BlockSpec((UNIT, d), lambda b, meta: (meta[PER * b + i], 0))


def k1(meta, tokens, cot, shard, blocks, ff):
    t, d = tokens.shape
    nb = t // BLOCK
    wide = shard.shape[1]
    blk = lambda n: pl.BlockSpec((BLOCK, n), lambda b, meta: (b, 0))
    fixed = lambda s: pl.BlockSpec(s, lambda b, meta: (0,) * len(s))
    sd = jax.ShapeDtypeStruct
    return pl.pallas_call(
        k1_body,
        grid_spec=pltpu.PrefetchScalarGridSpec(
            num_scalar_prefetch=1,
            grid=(nb,),
            in_specs=[unit_spec(i, d) for i in range(PER)] * 2 + [ANY] * 9,
            out_specs=[
                blk(3 * d),
                pl.BlockSpec((1, HEADS, BLOCK, BLOCK), lambda b, meta: (b, 0, 0, 0)),
                blk(d), blk(d), blk(d), blk(d), blk(d), blk(d), ANY,
                fixed((16, d)), fixed((4, ff // 4)), fixed((8, d)),
            ],
            scratch_shapes=[
                pltpu.VMEM((d, wide), BF16),
                pltpu.VMEM((16, d), F32),
                pltpu.SemaphoreType.DMA((17,)),
                pltpu.SemaphoreType.DMA,
            ],
        ),
        out_shape=[
            sd((t, 3 * d), BF16), sd((nb, HEADS, BLOCK, BLOCK), BF16), sd((t, d), F32), sd((t, d), BF16), sd((t, d), F32),
            sd((t, d), BF16), sd((t, d), BF16), sd((t, d), BF16), sd((d, wide), BF16),
            sd((16, d), F32), sd((4, ff // 4), F32), sd((8, d), F32),
        ],
        compiler_params=params(),
        cost_estimate=pl.CostEstimate(flops=2 * t * d * 5 * d, bytes_accessed=40 << 20, transcendentals=t * BLOCK * HEADS),
        name="norm_qkv_attend",
    )(meta, *([tokens] * PER), *([cot] * PER), shard, *blocks)


def gelu_and_slope(z):
    t = 1.0 / (1.0 + (0.3275911 * RSQRT2) * jnp.abs(z))
    e = jnp.exp(-0.5 * z * z)
    poly = t * (0.5 * 0.254829592 + t * (-0.5 * 0.284496736 + t * (0.5 * 1.421413741 + t * (
        -0.5 * 1.453152027 + t * (0.5 * 1.061405429)))))
    tail = poly * e
    cdf = jnp.where(z >= 0.0, 1.0 - tail, tail)
    return z * cdf, cdf + z * e * RSQRT_TAU


def mlp_body(ng, go, first, meta, *refs):
    a2o, a2p, g_o, g_p, b1, f1, f2 = refs[0:7]
    blocks = refs[7:11]
    at = 11
    prev = None
    if not first:
        prev, at = refs[11:15], 15
    yo, do, yp, dp, send, keep, db = refs[at : at + 7]
    a2, g, u_s, dz_s, w1, w2, dw1, dw2, sems = refs[at + 7 :]
    b = pl.program_id(0)
    last = pl.num_programs(0) - 1
    t, d = a2o.shape
    nb = t // BLOCK
    n = 128 * ng
    c, x, y, z = meta[I_C], meta[I_X], meta[I_Y], meta[I_Z]
    rows = f1.shape[0]
    quarter = rows // 4
    nk = d // 128

    def loads():
        ff = f1.shape[1]
        early = [(a2o, a2.at[pl.ds(0, t)]), (g_o, g.at[pl.ds(0, t)])]
        for zz in range(4):
            col = pl.multiple_of(zz * (ff // 4) + c * (ff // 8) + go * 128, 128)
            early.append((f1.at[:, pl.ds(col, n)], w1.at[pl.ds(pl.multiple_of(z * rows, 16), rows), pl.ds(zz * n, n)]))
        row = pl.multiple_of(c * (ff // 8) + go * 128, 128)
        early.append((f2.at[pl.ds(row, n)], w2.at[pl.ds(pl.multiple_of(z * n, 128), n)]))
        late = [(a2p, a2.at[pl.ds(t, t)]), (g_p, g.at[pl.ds(t, t)])]
        cps = [pltpu.make_async_copy(s, q, sems.at[i]) for i, (s, q) in enumerate(early + late)]
        return cps[: len(early)], cps[len(early) :]

    @pl.when(b == 0)
    def _():
        early, late = loads()
        for cp in early + late:
            cp.start()
        db[...] = jnp.zeros_like(db)
        for k, blk in enumerate(blocks):
            xx, yy = x, y
            if k == 1:
                xx, yy = x ^ (1 - c), y ^ c
            elif k == 2:
                xx, yy = x ^ c, y ^ (1 - c)
            elif k == 3:
                xx, yy = x ^ 1, y ^ 1
            p = 2 * yy + xx

            def place(f, carry):
                plane = z ^ (f + 1)
                r1 = pl.ds(pl.multiple_of(plane * rows + p * quarter, 16), quarter)
                for j in range(4 * ng):
                    w1[r1, j * 128 : (j + 1) * 128] = blk[f, j * quarter : (j + 1) * quarter, :]
                for gg in range(ng):
                    r2 = pl.ds(pl.multiple_of(plane * n + gg * 128 + p * 32, 32), 32)
                    for kk in range(nk):
                        lo = 4 * ng * quarter + (gg * nk + kk) * 32
                        w2[r2, kk * 128 : (kk + 1) * 128] = blk[f, lo : lo + 32, :]
                return carry

            lax.fori_loop(0, 3, place, 0)
        for cp in early:
            cp.wait()

    @pl.when(b == nb)
    def _():
        for cp in loads()[1]:
            cp.wait()

    rr = pl.ds(pl.multiple_of(b * BLOCK, BLOCK), BLOCK)
    a = a2[rr, :]
    gr = g[rr, :]
    per = 2 // ng
    for k in range(2 * ng):
        cols = slice(k * 256, (k + 1) * 256)
        lane = pl.ds(pl.multiple_of(c * (b1.shape[1] // 2) + go * 128, 128), n)
        bias = jnp.concatenate([b1[zz : zz + 1, lane] for zz in range(k * per, (k + 1) * per)], axis=1)
        u, s = gelu_and_slope(nn(a, w1[:, cols]) + bias)
        u_s[rr, cols] = u.astype(BF16)
        dz = (nt(gr, w2[cols, :]) * s).astype(BF16)
        dz_s[rr, cols] = dz
        db[0:1, cols] += jnp.sum(dz.astype(F32), axis=0, keepdims=True)
    yv = nn(u_s[rr, :], w2[...])
    dv = nt(dz_s[rr, :], w1[...])

    def put(y_ref, d_ref, y_old, d_old):
        y_ref[...] = (yv if y_old is None else yv + y_old[...].astype(F32)).astype(BF16)
        d_ref[...] = (dv if d_old is None else dv + d_old[...].astype(F32)).astype(BF16)

    @pl.when(b < nb)
    def _():
        put(yo, do, *((None, None) if first else prev[0:2]))

    @pl.when(b >= nb)
    def _():
        put(yp, dp, *((None, None) if first else prev[2:4]))

    @pl.when(b == last)
    def _():
        def weights(k, carry):
            cols = pl.ds(pl.multiple_of(k * 256, 256), 256)
            dw1[:, cols] = tn(a2[...], dz_s[:, cols]).astype(BF16)
            dw2[cols, :] = tn(u_s[:, cols], g[...]).astype(BF16)
            return carry

        lax.fori_loop(0, 2 * ng, weights, 0)
        for out, sel in ((send, 1 - meta[I_B1]), (keep, meta[I_B1])):
            for i in range(2):

                def cut(plane, carry):
                    r1 = pl.ds(pl.multiple_of(plane * rows + sel * 2 * quarter + i * quarter, 16), quarter)
                    for j in range(4 * ng):
                        out[i, plane, j * quarter : (j + 1) * quarter, :] = dw1[r1, j * 128 : (j + 1) * 128]
                    for gg in range(ng):
                        r2 = pl.ds(pl.multiple_of(plane * n + gg * 128 + sel * 64 + i * 32, 32), 32)
                        for kk in range(nk):
                            lo = 4 * ng * quarter + (gg * nk + kk) * 32
                            out[i, plane, lo : lo + 32, :] = dw2[r2, kk * 128 : (kk + 1) * 128]
                    return carry

                lax.fori_loop(0, 4, cut, 0)


def mlp(part, meta, a2o, a2p, g_o, g_p, b1, f1, f2, blocks, prev=()):
    ng, go = PARTS[part]
    first = not prev
    t, d = a2o.shape
    nb = t // BLOCK
    n = 128 * ng
    size = blocks[0].shape[1]
    sd = jax.ShapeDtypeStruct
    fixed = lambda s: pl.BlockSpec(s, lambda i, meta: (0,) * len(s), pipeline_mode=pl.Buffered(1))
    outf = lambda s: pl.BlockSpec(s, lambda i, meta: (0,) * len(s))
    own = pl.BlockSpec((BLOCK, d), lambda i, meta: (jnp.minimum(i, nb - 1), 0))
    other = pl.BlockSpec((BLOCK, d), lambda i, meta: (jnp.maximum(i - nb, 0), 0))
    tok = sd((t, d), BF16)
    half = (2, 4, size, 128)
    return pl.pallas_call(
        functools.partial(mlp_body, ng, go, first),
        grid_spec=pltpu.PrefetchScalarGridSpec(
            num_scalar_prefetch=1,
            grid=(2 * nb,),
            in_specs=[ANY] * 4 + [fixed(b1.shape)] + [ANY] * 2 + [fixed(k.shape) for k in blocks]
            + ([] if first else [own, own, other, other]),
            out_specs=[own, own, other, other, outf(half), outf(half), outf((8, 4 * n))],
            scratch_shapes=[
                pltpu.VMEM((2 * t, d), BF16), pltpu.VMEM((2 * t, d), BF16),
                pltpu.VMEM((2 * t, 4 * n), BF16), pltpu.VMEM((2 * t, 4 * n), BF16),
                pltpu.VMEM((d, 4 * n), BF16), pltpu.VMEM((4 * n, d), BF16),
                pltpu.VMEM((d, 4 * n), BF16), pltpu.VMEM((4 * n, d), BF16),
                pltpu.SemaphoreType.DMA((9,)),
            ],
        ),
        out_shape=[tok, tok, tok, tok, sd(half, BF16), sd(half, BF16), sd((8, 4 * n), F32)],
        compiler_params=params(),
        cost_estimate=pl.CostEstimate(flops=2 * 2 * t * d * 4 * n * 6, bytes_accessed=30 << 20, transcendentals=2 * t * 4 * n),
        name="hidden_first" if first else "hidden_second",
    )(meta, a2o, a2p, g_o, g_p, b1, f1, f2, *blocks, *prev)


EARLY = 8


def heads_back(pairs, lo, do, prob, inv, o, qkv, out):
    d = qkv.shape[1] // 3
    n = 128 * pairs
    lo_m, hi_m = lane_masks()
    for j in range(pairs):
        cols = slice(128 * (lo + j), 128 * (lo + j + 1))
        q, k, v = (qkv[:, i * d + cols.start : i * d + cols.stop] for i in range(3))
        dop = (do[:, 128 * j : 128 * (j + 1)].astype(F32) * inv[:, cols]).astype(BF16)
        dot = dop.astype(F32) * o[:, cols].astype(F32)
        dq = dk = dv = None
        for h, m in ((0, lo_m), (1, hi_m)):
            e = prob[0, 2 * j + h]
            mean = jnp.sum(dot * m.astype(F32), axis=-1, keepdims=True)
            dom = dop * m
            ds = (e.astype(F32) * (nt(dom, v) - mean)).astype(BF16)
            ms = m * SCALE
            parts = (nn(ds, k * ms), tn(ds, q * ms), tn(e, dom))
            dq, dk, dv = parts if dq is None else (dq + parts[0], dk + parts[1], dv + parts[2])
        for i, a in enumerate((dq, dk, dv)):
            out[:, i * n + 128 * j : i * n + 128 * (j + 1)] = a.astype(BF16)


def back_early_body(gp, da_o, da_p, x1_r, prob, inv, o, qkv, w_out, vec, dbf, dx1_o, dl, dq, acc):
    n = 64 * EARLY

    @pl.when(pl.program_id(0) == 0)
    def _():
        acc[...] = jnp.zeros_like(acc)
        acc[5:6] = dbf[0:1]

    da2 = da_o[...].astype(F32) + da_p[...].astype(F32)
    n2, r2 = norm_stats(x1_r[...])
    dx1 = gp[...].astype(F32) + norm_back(da2, n2, r2, vec[3:4])
    low = dx1.astype(BF16)
    acc[3:4] += jnp.sum(da2 * n2, axis=0, keepdims=True)
    acc[4:5] += jnp.sum(da2, axis=0, keepdims=True)
    acc[2:3] += jnp.sum(low.astype(F32), axis=0, keepdims=True)
    dx1_o[...] = dx1
    dl[...] = low
    do = nt(low, w_out[0:n, :]).astype(BF16)
    heads_back(EARLY // 2, 0, do, prob, inv, o, qkv, dq)


def back_early(gp, da_o, da_p, x1, prob, inv, o, qkv, w, vec, dbf):
    t, d = gp.shape
    blk = lambda n: pl.BlockSpec((BLOCK, n), lambda b: (b, 0))
    sd = jax.ShapeDtypeStruct
    fixed = lambda s: pl.BlockSpec(s, lambda b: (0,) * len(s), pipeline_mode=pl.Buffered(1))
    cols = 3 * 64 * EARLY
    return pl.pallas_call(
        back_early_body,
        grid=(t // BLOCK,),
        in_specs=[blk(d), blk(d), blk(d), blk(d),
                  pl.BlockSpec((1, EARLY, BLOCK, BLOCK), lambda b: (b, 0, 0, 0)), blk(d), blk(d), blk(3 * d),
                  pl.BlockSpec((d, d), lambda b: (0, 3), pipeline_mode=pl.Buffered(1)),
                  fixed(vec.shape), fixed(dbf.shape)],
        out_specs=[blk(d), blk(d), blk(cols), pl.BlockSpec((128, d), lambda b: (0, 0))],
        out_shape=[sd((t, d), F32), sd((t, d), BF16), sd((t, cols), BF16), sd((128, d), F32)],
        compiler_params=params(),
        cost_estimate=pl.CostEstimate(flops=2 * t * d * 4 * d, bytes_accessed=24 << 20, transcendentals=0),
        name="attend_back_early",
    )(gp, da_o, da_p, x1, prob, inv, o, qkv, w, vec, dbf)


def back_late_body(meta, *refs):
    tok = refs[0:4]
    dx1, dl, dqe, prob, inv, o, qkv, w, vec, acc_in = refs[4:14]
    gt_o, dq, acc = refs[14:17]
    gt, sems = refs[17:]
    b = pl.program_id(0)
    nb = pl.num_programs(0)
    d = dl.shape[1]
    slot = lax.rem(b, 2)
    n = 64 * EARLY

    def puts(step, sl):
        return [
            pltpu.make_async_copy(
                gt.at[sl, pl.ds(i * UNIT, UNIT)],
                gt_o.at[pl.ds(pl.multiple_of(meta[PER * step + i] * UNIT, UNIT), UNIT)],
                sems.at[sl, i],
            )
            for i in range(PER)
        ]

    @pl.when(b == 0)
    def _():
        acc[...] = acc_in[...]

    @pl.when(b >= 2)
    def _():
        for cp in puts(b - 2, slot):
            cp.wait()

    do = nt(dl[...], w[n:, 3 * d : 4 * d]).astype(BF16)
    heads_back((HEADS - EARLY) // 2, EARLY // 2, do, prob, inv, o, qkv, dq)
    rest = d - n
    da1 = None
    for i in range(3):
        part = nt(dqe[:, i * n : (i + 1) * n], w[:, i * d : i * d + n])
        part = part + nt(dq[:, i * rest : (i + 1) * rest], w[:, i * d + n : (i + 1) * d])
        da1 = part if da1 is None else da1 + part
    x = jnp.concatenate([r[...] for r in tok], axis=0).astype(F32)
    n1, r1 = norm_stats(x)
    acc[0:1] += jnp.sum(da1 * n1, axis=0, keepdims=True)
    acc[1:2] += jnp.sum(da1, axis=0, keepdims=True)
    gt[slot] = dx1[...] + norm_back(da1, n1, r1, vec[0:1])
    for cp in puts(b, slot):
        cp.start()

    @pl.when(b == nb - 1)
    def _():
        for cp in puts(b - 1, 1 - slot) + puts(b, slot):
            cp.wait()


def back_late(meta, tokens, dx1, dl, dqe, prob, inv, o, qkv, w, vec, acc_in):
    t, d = tokens.shape
    late = HEADS - EARLY
    blk = lambda n: pl.BlockSpec((BLOCK, n), lambda b, meta: (b, 0))
    sd = jax.ShapeDtypeStruct
    fixed = lambda s: pl.BlockSpec(s, lambda b, meta: (0,) * len(s), pipeline_mode=pl.Buffered(1))
    return pl.pallas_call(
        back_late_body,
        grid_spec=pltpu.PrefetchScalarGridSpec(
            num_scalar_prefetch=1,
            grid=(t // BLOCK,),
            in_specs=[unit_spec(i, d) for i in range(PER)] + [
                blk(d), blk(d), blk(dqe.shape[1]),
                pl.BlockSpec((1, late, BLOCK, BLOCK), lambda b, meta: (b, EARLY // late, 0, 0)), blk(d), blk(d), blk(3 * d),
            ] + [fixed(a.shape) for a in (w, vec, acc_in)],
            out_specs=[ANY, blk(3 * 64 * late), pl.BlockSpec((128, d), lambda b, meta: (0, 0))],
            scratch_shapes=[pltpu.VMEM((2, BLOCK, d), F32), pltpu.SemaphoreType.DMA((2, PER))],
        ),
        out_shape=[sd((t, d), F32), sd((t, 3 * 64 * late), BF16), sd((128, d), F32)],
        compiler_params=params(),
        cost_estimate=pl.CostEstimate(flops=2 * t * d * 5 * d, bytes_accessed=20 << 20, transcendentals=0),
        name="attend_back_late",
    )(meta, *([tokens] * PER), dx1, dl, dqe, prob, inv, o, qkv, w, vec, acc_in)


def split(meta, stage, send_o, keep_o, at, width):
    c = meta[I_C]
    rows = stage.shape[0] // 4
    n = rows // 2
    for zz in range(4):
        for i in range(2):
            for out, h in ((send_o, 1 - c), (keep_o, c)):
                lot = stage[pl.ds(pl.multiple_of(zz * rows + n * h + (n // 2) * i, 16), n // 2), 0:width]
                out[i, 0, zz, :, pl.ds(at, width)] = lot[0 : n // 4]
                out[i, 1, zz, :, pl.ds(at, width)] = lot[n // 4 :]


def grads_early_body(meta, a1, dq, o, dl, send_o, keep_o, stage):
    d = a1.shape[1]
    s = pl.program_id(0)
    last = pl.num_programs(0) - 1

    @pl.when(s < last)
    def _():
        stage[...] = tn(a1[...], dq[...]).astype(BF16)

    @pl.when(s == last)
    def _():
        stage[...] = tn(o[...], dl[...]).astype(BF16)

    split(meta, stage, send_o, keep_o, pl.multiple_of(s * d, 128), d)


def grads_late_body(meta, a1, dq, acc, dba, dbb, send_o, keep_o, stage):
    d = a1.shape[1]
    c = meta[I_C]
    rows = d // 4
    stage[...] = tn(a1[...], dq[...]).astype(BF16)
    split(meta, stage, send_o, keep_o, 0, d)
    stage[:, 0:128] = acc[...].T.astype(BF16)
    stage[:, 128:256] = jnp.zeros((d, 128), BF16)
    for zz in range(4):
        parts = []
        for hh in range(2):
            for src, (ng, go) in ((dba, PARTS[0]), (dbb, PARTS[1])):
                for k in range(ng):
                    at = (zz * ng + k) * 128
                    parts.append(jnp.where(hh == c, src[0:1, at : at + 128], 0.0))
        parts.append(jnp.zeros((16 - len(parts), 128), F32))
        stage[zz * rows : zz * rows + 16, 128:256] = jnp.concatenate(parts, axis=0).astype(BF16)
    split(meta, stage, send_o, keep_o, d, EXT)


def grads(body, steps, wide, meta, a1, dq, *rest, cost=None):
    t, d = a1.shape
    cost = cost or pl.CostEstimate(flops=2 * t * d * steps * d, bytes_accessed=12 << 20, transcendentals=0)
    half = (2, 2, 4, d // 32, wide)
    sd = jax.ShapeDtypeStruct
    fixed = lambda a: pl.BlockSpec(a.shape, lambda s, meta: (0,) * a.ndim, pipeline_mode=pl.Buffered(1))
    outf = pl.BlockSpec(half, lambda s, meta: (0,) * 5)
    last = dq.shape[1] // d - 1
    return pl.pallas_call(
        body,
        grid_spec=pltpu.PrefetchScalarGridSpec(
            num_scalar_prefetch=1,
            grid=(steps,),
            in_specs=[fixed(a1), pl.BlockSpec((t, d), lambda s, meta: (0, jnp.minimum(s, last)))]
            + [fixed(a) for a in rest],
            out_specs=[outf, outf],
            scratch_shapes=[pltpu.VMEM((d, d), BF16)],
        ),
        out_shape=[sd(half, BF16), sd(half, BF16)],
        compiler_params=params(),
        cost_estimate=cost,
        name="weight_grads",
    )(meta, a1, dq, *rest)


def out_body(meta, ya, yb, x1, vec, out, buf, sems):
    b = pl.program_id(0)
    slot = lax.rem(b, 2)

    def puts(step, sl):
        return [
            pltpu.make_async_copy(
                buf.at[sl, pl.ds(i * UNIT, UNIT)],
                out.at[pl.ds(pl.multiple_of(meta[PER * step + i] * UNIT, UNIT), UNIT)],
                sems.at[sl, i],
            )
            for i in range(PER)
        ]

    @pl.when(b >= 2)
    def _():
        for cp in puts(b - 2, slot):
            cp.wait()

    y = ya[...].astype(F32) + yb[...].astype(F32)
    buf[slot] = (x1[...] + (y + vec[5:6])).astype(BF16)
    for cp in puts(b, slot):
        cp.start()

    @pl.when(b == pl.num_programs(0) - 1)
    def _():
        for cp in puts(b - 1, 1 - slot) + puts(b, slot):
            cp.wait()


def layer_output(meta, ya, yb, x1, vec):
    t, d = x1.shape
    blk = lambda n: pl.BlockSpec((BLOCK, n), lambda b, meta: (b, 0))
    fixed = lambda s: pl.BlockSpec(s, lambda b, meta: (0,) * len(s), pipeline_mode=pl.Buffered(1))
    return pl.pallas_call(
        out_body,
        grid_spec=pltpu.PrefetchScalarGridSpec(
            num_scalar_prefetch=1,
            grid=(t // BLOCK,),
            in_specs=[blk(d), blk(d), blk(d), fixed(vec.shape)],
            out_specs=ANY,
            scratch_shapes=[pltpu.VMEM((2, BLOCK, d), BF16), pltpu.SemaphoreType.DMA((2, PER))],
        ),
        out_shape=jax.ShapeDtypeStruct((t, d), BF16),
        compiler_params=params(),
        cost_estimate=pl.CostEstimate(flops=4 * t * d, bytes_accessed=8 << 20, transcendentals=0),
        name="layer_out",
    )(meta, ya, yb, x1, vec)


def halve_body(jobs, meta, *refs):
    at, to = 0, sum(2 * n for _, n, _ in jobs)
    for place, n, loops in jobs:
        ks, vs, (send, keep) = refs[at : at + n], refs[at + n : at + 2 * n], refs[to : to + 2]
        at, to = at + 2 * n, to + 2
        bit = meta[place]
        for out, sel in ((send, 1 - bit), (keep, bit)):
            for pre in range(ks[0].shape[0]):

                def step(r, carry):
                    col = 0
                    for k, v in zip(ks, vs):
                        w = k.shape[-1]
                        part = k[pre, sel, r].astype(F32) + v[pre, sel, r].astype(F32)
                        out[pre, r, :, col : col + w] = part.astype(BF16)
                        col += w
                    return carry

                lax.fori_loop(0, loops, step, 0)


def halve(meta, *jobs):
    sd = jax.ShapeDtypeStruct
    jobs = [(p, k if isinstance(k, list) else [k], v if isinstance(v, list) else [v]) for p, k, v in jobs]
    outs = []
    for _, ks, _ in jobs:
        shape = ks[0].shape
        outs += [sd((shape[0],) + shape[2:-1] + (sum(k.shape[-1] for k in ks),), BF16)] * 2
    arrays = [a for _, ks, vs in jobs for a in (*ks, *vs)]
    size = sum(a.size for a in arrays) // 2
    return pl.pallas_call(
        functools.partial(halve_body, tuple((p, len(ks), ks[0].shape[2]) for p, ks, _ in jobs)),
        in_specs=[pl.BlockSpec(memory_space=pltpu.SMEM)] + [WHOLE] * len(arrays),
        out_specs=[WHOLE] * len(outs),
        out_shape=outs,
        compiler_params=params(),
        cost_estimate=pl.CostEstimate(flops=size, bytes_accessed=6 * size, transcendentals=0),
        name="add_halve",
    )(meta, *arrays)


def total(routes, k, v):
    piece = k.astype(F32) + v.astype(F32)
    if routes.n_dp > 8:
        groups = [[j + 8 * o for o in range(routes.n_dp // 8)] for j in range(8)]
        piece = lax.psum(piece, "dp", axis_index_groups=groups)
    return piece.astype(BF16)


def ranks(meta, t):
    cc, x, y = holder(meta, t)
    return cc, 2 * jnp.where(cc == 0, x, y) + jnp.where(cc == 0, y, x)


def final_hidden_body(meta, *refs):
    pieces = refs[:8]
    d1, d2 = refs[8:10]
    rows, ff = d1.shape
    d = d2.shape[1]
    quarter = rows // 4
    nk = d // 128
    for t in range(8):
        cc, q = ranks(meta, t)
        at = 0
        for ng, go in PARTS:
            r1 = pl.ds(pl.multiple_of(q * quarter, 16), quarter)
            for zz in range(4):
                for g in range(ng):
                    col = pl.multiple_of(zz * (ff // 4) + cc * (ff // 8) + (go + g) * 128, 128)
                    d1[r1, pl.ds(col, 128)] = pieces[t][at : at + quarter, :].astype(F32)
                    at += quarter
            for g in range(ng):
                r2 = pl.ds(pl.multiple_of(cc * (ff // 8) + (go + g) * 128 + q * 32, 32), 32)
                for k in range(nk):
                    d2[r2, k * 128 : (k + 1) * 128] = pieces[t][at : at + 32, :].astype(F32)
                    at += 32


def final_mixed_body(meta, *refs):
    pieces = refs[:8]
    dqkv, dout, dg1, ds1, dbo, dg2, ds2, dbf, db1 = refs[8:17]
    ext = refs[17]
    n = pieces[0].shape[0]
    d = dout.shape[1]
    for t in range(8):
        cc, x, y = holder(meta, t)
        first, second = jnp.where(cc == 0, x, y), jnp.where(cc == 0, y, x)
        rows = pl.ds(pl.multiple_of(n * (4 * cc + 2 * first + second), n), n)
        v = pieces[t][...].astype(F32)
        m = 64 * EARLY
        for k in range(3):
            dqkv[rows, k * d : k * d + m] = v[:, k * m : (k + 1) * m]
            at = 3 * m + d + k * (d - m)
            dqkv[rows, k * d + m : (k + 1) * d] = v[:, at : at + d - m]
        dout[rows, :] = v[:, 3 * m : 3 * m + d]
        ext[rows, :] = v[:, 4 * d :]
    vec = ext[:, 0:128].T
    for i, ref in enumerate((dg1, ds1, dbo, dg2, ds2, dbf)):
        ref[...] = vec[i]
    for r in range(db1.shape[0] // 128):
        db1[pl.ds(128 * r, 128)] = ext[r, 128:256]


def final(body, meta, pieces, outs, scratch=()):
    sd = [jax.ShapeDtypeStruct(s, F32) for s in outs]
    res = pl.pallas_call(
        body,
        in_specs=[pl.BlockSpec(memory_space=pltpu.SMEM)] + [WHOLE] * 8,
        out_specs=[WHOLE] * len(outs),
        scratch_shapes=list(scratch),
        out_shape=sd,
        compiler_params=params(),
        name="place_sums",
    )(meta, *pieces)
    return res


def scalars(chip_ids):
    n = chip_ids.shape[0] // UNIT
    ids = chip_ids.reshape(n, UNIT)[:, 0]
    here = jnp.arange(n, dtype=jnp.int32)
    same = (ids[:, None] == ids[None, :]).astype(jnp.int32)
    long = jnp.sum(same, axis=1) > 1
    longs = long.astype(jnp.int32)
    before = jnp.sum(jnp.where(here[None, :] < here[:, None], longs[None, :], 0), axis=1)
    total = jnp.sum(longs)
    pos = jnp.where(long, before, total + here - before)
    src = jnp.sum(jnp.where(pos[None, :] == here[:, None], here[None, :], 0), axis=1)
    dp, z = lax.axis_index("dp"), lax.axis_index("fsdp")
    c, x, y = dp & 1, (dp >> 1) & 1, (dp >> 2) & 1
    b1, b2 = jnp.where(c == 0, x, y), jnp.where(c == 0, y, x)
    rest = jnp.stack([total >> 2, c, x, y, z, b1, b2, jnp.zeros_like(z), z & 1, z >> 1]).astype(jnp.int32)
    return jnp.concatenate([src.astype(jnp.int32), rest])


def on_device(n_dp, n_z, tokens, chip_ids, ln1_gain, ln1_bias, w_qkv, w_out, b_out, ln2_gain, ln2_bias,
              w_fc1, b_fc1, w_fc2, b_fc2, cotangent):
    routes = Routes(n_dp, n_z)
    t, d = tokens.shape
    ff = w_fc1.shape[1]
    rows = w_qkv.shape[0]
    pos = lax.axis_index("dp").astype(jnp.int32).reshape(1)
    meta = scalars(chip_ids)

    vecs = (ln1_gain, ln1_bias, b_out, ln2_gain, ln2_bias, b_fc2)
    mixed, near, far, ha, hb = pack(pos, w_qkv, w_out, vecs, b_fc1, w_fc1, w_fc2)

    def planes(own, other):
        return routes.z_flip(jnp.stack([own, other]), 2)

    join = lambda other, two: jnp.concatenate([other[None], two], axis=0)
    mate_a, mate_b = routes.z_flip(ha, 1), routes.z_flip(hb, 1)
    two_a = planes(ha, mate_a)
    p_mixed = gather_mixed(routes, near, far, mate_a, (two_a, mate_b))
    block_a = join(mate_a, two_a)
    p_a = around(routes, block_a)
    two_b = planes(hb, tie(mate_b, block_a))
    qkv, prob, inv, o, x1, a2, a1, gp, w, vec, b1, dbf = k1(meta, tokens, cotangent, tie(mixed, block_a), p_mixed, ff)
    block_b = join(mate_b, tie(two_b, a2))
    p_b = around(routes, block_b)

    swap = lax.optimization_barrier((a2, gp, block_b, *p_a))
    a2p, gpp = routes.core(swap[0]), routes.core(swap[1])
    *part, sa, ka, dba = mlp(0, meta, a2, a2p, gp, gpp, b1, w_fc1, w_fc2, p_a)
    got_a = routes.first(sa)
    yo, do, yp, dp, sb, kb, dbb = mlp(1, meta, a2, a2p, gp, gpp, b1, w_fc1, w_fc2, p_b, part)

    def view(a, pre, rest):
        return a.reshape((pre, 2) + rest)

    tall = lambda a: (4 * a.shape[2] // 96, 96, 128)
    flat = lambda a: (a.shape[2] // 96, 96, 128)
    size_a, size_b = tall(sa), tall(sb)
    s_a, k_a = halve(meta, (I_B2, view(ka, 1, size_a), view(got_a, 1, size_a)))
    dp, yp, sb = lax.optimization_barrier((dp, yp, sb, got_a))[:3]
    dq = routes.core(dp)
    yq = routes.core(yp)
    got_a, got_b = routes.second(s_a), routes.first(sb)
    dx1, dl, dqe, acc = back_early(tie(gp, s_a), do, dq, x1, prob, inv, o, qkv, w, vec, dbf)
    early = 3 * 64 * EARLY + d
    late = 4 * d - early + EXT
    sm, km = grads(grads_early_body, early // d, early, meta, tie(a1, yq), dqe, o, dl, cost=SHORT)
    got_m = routes.core(tie(sm, got_a, got_b))

    lo_a, lo_b = (2, 2) + flat(sa), (2, 2) + flat(sb)
    hi_a, hi_b = (1,) + lo_a[1:], (1,) + lo_b[1:]
    s_a, k_a, s_b, k_b = halve(meta, (I_Z + 4, k_a.reshape(lo_a), tie(got_a, sm).reshape(lo_a)),
                               (I_B2, view(kb, 1, size_b), view(tie(got_b, sm), 1, size_b)))
    got_a, got_b = routes.z_flip(s_a, 1), routes.second(s_b)
    chunk = lambda a, pre, loops: a.reshape(pre, 2, loops, d // 32, a.shape[-1])
    s_m, k_m = halve(meta, (I_B1, chunk(km, 1, 8), chunk(tie(got_m, s_b), 1, 8)))
    got_m = routes.first(s_m)
    gt, dql, acc = back_late(meta, tokens, tie(dx1, s_m), dl, dqe, prob, inv, o, qkv, w, vec, acc)

    s_a, k_a, s_b, k_b, s_m, k_m = halve(
        meta, (I_Z + 5, k_a.reshape(hi_a), tie(got_a, acc).reshape(hi_a)),
        (I_Z + 4, k_b.reshape(lo_b), tie(got_b, acc).reshape(lo_b)),
        (I_B2, chunk(k_m, 1, 4), chunk(tie(got_m, acc), 1, 4)))
    got_m = routes.second(s_m)
    got_a, got_b = routes.z_flip(s_a, 2), routes.z_flip(s_b, 1)
    sl, kl = grads(grads_late_body, 1, late, meta, tie(a1, s_m), dql, acc, dba, dbb)
    joint = lambda a, b: jnp.concatenate([a.reshape(-1, 128), b.reshape(-1, 128)], axis=0)
    got_l = routes.core(tie(sl, got_m, got_a, got_b))
    s_m, k_m, s_b, k_b = halve(
        meta, (I_Z + 4, chunk(k_m, 2, 1), chunk(tie(got_m, sl), 2, 1)),
        (I_Z + 5, k_b.reshape(hi_b), tie(got_b, sl).reshape(hi_b)))
    got_m, got_b = routes.z_flip(s_m, 1), routes.z_flip(s_b, 2)
    s_l, k_l = halve(meta, (I_B1, chunk(kl, 1, 8), chunk(tie(got_l, s_b), 1, 8)))
    got_l = routes.first(s_l)
    layer_out = layer_output(meta, yo, yq, x1, tie(vec, s_l))
    s_l, k_l, s_m, k_m = halve(meta, (I_B2, chunk(k_l, 1, 4), chunk(tie(got_l, layer_out), 1, 4)),
                               (I_Z + 5, chunk(k_m, 1, 1), chunk(tie(got_m, layer_out), 1, 1)))
    got_l, got_m = routes.second(s_l), routes.z_flip(s_m, 2)
    piece = total(routes, joint(k_a, k_b), joint(got_a, tie(got_b, s_l)))
    near_by = around(routes, piece)
    s_l, k_l = halve(meta, (I_Z + 4, chunk(k_l, 2, 1), chunk(tie(got_l, piece), 2, 1)))
    s_l, k_l = halve(meta, (I_Z + 5, chunk(k_l, 1, 1), chunk(tie(routes.z_flip(s_l, 1), got_m), 1, 1)))
    got_l = tie(routes.z_flip(s_l, 2), *near_by)
    side = lambda a, b: jnp.concatenate([a.reshape(d // 32, -1), b.reshape(d // 32, -1)], axis=1)
    piece = total(routes, side(k_m, k_l), side(got_m, got_l))
    near_m = around(routes, piece)
    pieces = near_by + [routes.core(b) for b in lax.optimization_barrier((*near_by, piece))[:4]]
    g_fc1, g_fc2 = final(final_hidden_body, meta, pieces, [w_fc1.shape, w_fc2.shape])
    near_m = list(lax.optimization_barrier((*near_m, g_fc1))[:4])
    pieces_m = near_m + [routes.core(b) for b in near_m]

    vecs = [(rows,)] * 6
    g_qkv, g_out, dg1, ds1, dbo, dg2, ds2, dbf2, db1 = final(
        final_mixed_body, meta, pieces_m, [w_qkv.shape, w_out.shape, *vecs, b_fc1.shape],
        [pltpu.VMEM((rows, EXT), F32)])
    return (layer_out, gt, dg1, ds1, g_qkv, g_out, dbo, dg2, ds2, g_fc1, db1, g_fc2, dbf2)


def solution(mesh):
    token, part, plain = P(ALL, None), P("fsdp", None), P("fsdp")
    return jax.shard_map(
        functools.partial(on_device, mesh.shape["dp"], mesh.shape["fsdp"]),
        mesh=mesh,
        in_specs=(token, P(ALL), plain, plain, part, part, plain, plain, plain, part, plain, part, plain, token),
        out_specs=(token, token, plain, plain, part, part, plain, plain, plain, part, plain, part, plain),
        check_vma=False,
    )
```

```python
import functools
import math

import jax
import jax.numpy as jnp
from jax import lax
from jax.experimental import pallas as pl
from jax.experimental.pallas import tpu as pltpu
from jax.sharding import PartitionSpec as P

HEADS = 12
HEAD = 64
UNIT = 64
BLOCK = 256
PER = BLOCK // UNIT
EPS = 1e-05
NEG = -1e30
RSQRT2 = 1.0 / math.sqrt(2.0)
RSQRT_TAU = 1.0 / math.sqrt(2.0 * math.pi)
SCALE = 1.0 / math.sqrt(HEAD)
EXT = 256
VMEM_LIMIT = 64 * 1024 * 1024 - 65536
ALL = ("dp", "fsdp")
F32 = jnp.float32
BF16 = jnp.bfloat16

I_LONG, I_C, I_X, I_Y, I_Z, I_B1, I_B2 = 16, 17, 18, 19, 20, 21, 22


def nn(a, b):
    return lax.dot_general(a, b, (((1,), (0,)), ((), ())), preferred_element_type=F32)


def nt(a, b):
    return lax.dot_general(a, b, (((1,), (1,)), ((), ())), preferred_element_type=F32)


def tn(a, b):
    return lax.dot_general(a, b, (((0,), (0,)), ((), ())), preferred_element_type=F32)


SHORT = pl.CostEstimate(flops=1, bytes_accessed=1, transcendentals=0)


def params(**kw):
    return pltpu.CompilerParams(vmem_limit_bytes=VMEM_LIMIT, **kw)


ANY = pl.BlockSpec(memory_space=pl.ANY)
WHOLE = pl.BlockSpec(memory_space=pltpu.VMEM)


def tie(a, *after):
    return lax.optimization_barrier((a,) + after)[0]


class Routes:
    def __init__(self, n_dp, n_z):
        self.n_dp, self.n_z = n_dp, n_z

    def table(self, move):
        pairs = []
        for d in range(self.n_dp):
            for z in range(self.n_z):
                e, w = move(d, z)
                pairs.append((d * self.n_z + z, e * self.n_z + w % self.n_z))
        return pairs

    def core(self, a):
        return lax.ppermute(a, ALL, self.table(lambda d, z: (d ^ 1, z)))

    def first(self, a):
        return lax.ppermute(a, ALL, self.table(lambda d, z: (d ^ (2 if d % 2 == 0 else 4), z)))

    def second(self, a):
        return lax.ppermute(a, ALL, self.table(lambda d, z: (d ^ (4 if d % 2 == 0 else 2), z)))

    def z_near(self, a):
        return lax.ppermute(a, ALL, self.table(lambda d, z: (d, z + (1 if d % 2 == 0 else self.n_z - 1))))

    def z_far(self, a):
        return lax.ppermute(a, ALL, self.table(lambda d, z: (d, z + 2)))

    def z_flip(self, a, bit):
        return lax.ppermute(a, ALL, self.table(lambda d, z: (d, z ^ bit)))

    def diagonal(self, a):
        return lax.ppermute(a, ALL, self.table(lambda d, z: (d ^ 6, z)))


def spread(routes, block):
    own = around(routes, block)
    return own + [routes.core(b) for b in own]


def around(routes, block):
    return [block, routes.first(block), routes.second(block), routes.diagonal(block)]


def holder(meta, t):
    flip = t // 4
    cc = meta[I_C] if flip == 0 else 1 - meta[I_C]
    x, y = meta[I_X], meta[I_Y]
    t = t % 4
    if t == 1:
        x, y = x ^ (1 - cc), y ^ cc
    elif t == 2:
        x, y = x ^ cc, y ^ (1 - cc)
    elif t == 3:
        x, y = x ^ 1, y ^ 1
    return cc, x, y


def gather_mixed(routes, near, far, early, late):
    block = jnp.concatenate([routes.z_near(near), routes.z_far(far)], axis=1)
    one = routes.first(block)
    two = routes.second(block)
    own = [block, one, two, routes.second(tie(one, two, *early))]
    return own + [routes.core(b) for b in own[:3]] + [routes.core(tie(own[3], late))]


def mixed_copies(meta, shard, blocks, w, sems):
    rows, wide = shard.shape
    quarter, part = rows // 4, wide // 2
    z = meta[I_Z]
    out = [(shard, w.at[pl.ds(pl.multiple_of(z * rows, 16), rows)])]
    for t, block in enumerate(blocks):
        cc, x, y = holder(meta, t)
        q = 2 * y + x
        plane = lax.rem(z + jnp.where(cc == 0, 3, 1), 4)
        far = lax.rem(z + 2, 4)
        out.append((block.at[:, pl.ds(0, wide)],
                    w.at[pl.ds(pl.multiple_of(plane * rows + q * quarter, 16), quarter)]))
        out.append((block.at[:, pl.ds(wide, part)],
                    w.at[pl.ds(pl.multiple_of(far * rows + q * quarter, 16), quarter),
                         pl.ds(pl.multiple_of(cc * part, 128), part)]))
    return [pltpu.make_async_copy(s, d, sems.at[i]) for i, (s, d) in enumerate(out)]


PARTS = ((3, 0),)


def piece_rows(ng, rows, d):
    return 4 * ng * (rows // 4) + ng * (d // 128) * 32


def pack_body(pos, *refs):
    w_qkv, w_out = refs[0:2]
    vecs, b1, f1, f2 = refs[2:8], refs[8], refs[9], refs[10]
    mixed, near, far = refs[11:14]
    outs, sems = refs[14 : 14 + len(PARTS)], refs[14 + len(PARTS)]
    c, x, y = pos[0] & 1, (pos[0] >> 1) & 1, (pos[0] >> 2) & 1
    p = 2 * y + x
    d = w_out.shape[1]
    rows = w_out.shape[0]
    quarter = rows // 4
    ff = f1.shape[1]
    copies = []
    for out, (ng, go) in zip(outs, PARTS):
        for zz in range(4):
            for g in range(ng):
                col = pl.multiple_of(zz * (ff // 4) + c * (ff // 8) + (go + g) * 128, 128)
                copies.append((f1.at[pl.ds(pl.multiple_of(p * quarter, 16), quarter), pl.ds(col, 128)],
                               out.at[pl.ds((zz * ng + g) * quarter, quarter)]))
        base = 4 * ng * quarter
        for g in range(ng):
            row = pl.multiple_of(c * (ff // 8) + (go + g) * 128 + p * 32, 32)
            for k in range(d // 128):
                copies.append((f2.at[pl.ds(row, 32), pl.ds(k * 128, 128)],
                               out.at[pl.ds(base + (g * (d // 128) + k) * 32, 32)]))
    copies = [pltpu.make_async_copy(s, t, sems.at[i]) for i, (s, t) in enumerate(copies)]
    for cp in copies:
        cp.start()
    mixed[:, 0 : 3 * d] = w_qkv[...]
    mixed[:, 3 * d : 4 * d] = w_out[...]
    lines = [v[...].astype(F32).reshape(1, rows) for v in vecs] + [jnp.zeros((128 - len(vecs), rows), F32)]
    mixed[:, 4 * d : 4 * d + 128] = jnp.concatenate(lines, axis=0).T.astype(BF16)
    n = b1.shape[0] // 128
    lines = [b1[pl.ds(128 * i, 128)].astype(F32).reshape(1, 128) for i in range(n)] + [jnp.zeros((rows - n, 128), F32)]
    mixed[:, 4 * d + 128 :] = jnp.concatenate(lines, axis=0).astype(BF16)
    own = pl.ds(pl.multiple_of(p * quarter, 16), quarter)
    near[...] = mixed[own, :]
    part = mixed.shape[1] // 2
    far[...] = mixed[own, pl.ds(pl.multiple_of(c * part, 128), part)]
    for cp in copies:
        cp.wait()


def pack(pos, w_qkv, w_out, vecs, b1, f1, f2):
    rows, d = w_out.shape
    wide = 4 * d + EXT
    sd = jax.ShapeDtypeStruct
    count = sum(4 * ng + ng * (d // 128) for ng, _ in PARTS)
    return pl.pallas_call(
        pack_body,
        in_specs=[pl.BlockSpec(memory_space=pltpu.SMEM)] + [WHOLE] * 9 + [ANY] * 2,
        out_specs=[WHOLE] * (3 + len(PARTS)),
        scratch_shapes=[pltpu.SemaphoreType.DMA((count,))],
        out_shape=[sd((rows, wide), BF16), sd((rows // 4, wide), BF16), sd((rows // 4, wide // 2), BF16)]
        + [sd((piece_rows(ng, rows, d), 128), BF16) for ng, _ in PARTS],
        compiler_params=params(),
        name="pack",
    )(pos, w_qkv, w_out, *vecs, b1, f1, f2)


def norm_stats(rows):
    centred = rows - jnp.mean(rows, axis=-1, keepdims=True)
    inverse = lax.rsqrt(jnp.mean(centred * centred, axis=-1, keepdims=True) + EPS)
    return centred * inverse, inverse


def norm_back(grad, normed, inverse, gain):
    e = grad * gain
    return inverse * (
        e - jnp.mean(e, axis=-1, keepdims=True) - normed * jnp.mean(e * normed, axis=-1, keepdims=True)
    )


def lane_masks():
    lane = lax.broadcasted_iota(jnp.int32, (1, 2 * HEAD), 1)
    low = jnp.where(lane < HEAD, 1.0, 0.0).astype(BF16)
    return low, (1.0 - low.astype(F32)).astype(BF16)


def k1_body(meta, *refs):
    tok, cot = refs[0:4], refs[4:8]
    shard, blocks = refs[8], refs[9:17]
    qkv_o, prob_o, inv_o, o_o, x1_o, a2_o, a1_o, gp_o, w_o, vec_o, b1_o, dbf_o = refs[17:29]
    w, vec, sems, out_sem = refs[29:]
    b = pl.program_id(0)
    d = w.shape[0]

    @pl.when(b == 0)
    def _():
        copies = mixed_copies(meta, shard, blocks, w, sems)
        for cp in copies:
            cp.start()
        for cp in copies:
            cp.wait()
        pltpu.make_async_copy(w, w_o, out_sem).start()
        ext = w[:, 4 * d : 4 * d + 128].astype(F32).T
        vec[...] = ext[0:16]
        vec_o[...] = ext[0:16]
        dbf_o[...] = jnp.zeros_like(dbf_o)
        rows = d // 4
        for zz in range(4):
            for r in range(b1_o.shape[1] // 128):
                b1_o[zz : zz + 1, 128 * r : 128 * (r + 1)] = w[
                    zz * rows : zz * rows + 8, 4 * d + 128 : 4 * d + 256
                ].astype(F32)[r : r + 1]

    g1, s1, b_out = vec[0:1], vec[1:2], vec[2:3]
    g2, s2 = vec[3:4], vec[4:5]
    x = jnp.concatenate([r[...] for r in tok], axis=0).astype(F32)
    g = jnp.concatenate([r[...] for r in cot], axis=0)
    gp_o[...] = g
    dbf_o[0:1] += jnp.sum(g.astype(F32), axis=0, keepdims=True)
    n1, _ = norm_stats(x)
    a1 = (n1 * g1 + s1).astype(BF16)
    a1_o[...] = a1
    for k in range(3):
        qkv_o[:, k * d : (k + 1) * d] = nn(a1, w[:, k * d : (k + 1) * d]).astype(BF16)
    row = lax.broadcasted_iota(jnp.int32, (BLOCK, BLOCK), 0) // UNIT
    col = lax.broadcasted_iota(jnp.int32, (BLOCK, BLOCK), 1) // UNIT
    keep = (row == col) | (b < meta[I_LONG])
    low, high = lane_masks()
    left = lax.broadcasted_iota(jnp.int32, (BLOCK, 2 * HEAD), 1) < HEAD
    for j in range(HEADS // 2):
        s = slice(128 * j, 128 * (j + 1))
        q = qkv_o[:, s]
        k = qkv_o[:, d + 128 * j : d + 128 * (j + 1)]
        v = qkv_o[:, 2 * d + 128 * j : 2 * d + 128 * (j + 1)]
        mixed, inv = None, []
        for h, m in ((0, low), (1, high)):
            sc = jnp.where(keep, nt(q * (m * SCALE), k), NEG)
            e = jnp.exp(sc - jnp.max(sc, axis=-1, keepdims=True))
            inv.append(1.0 / jnp.sum(e, axis=-1, keepdims=True))
            e = e.astype(BF16)
            prob_o[0, 2 * j + h] = e
            part = nn(e, v * m)
            mixed = part if mixed is None else mixed + part
        inv = jnp.where(left, inv[0], inv[1])
        inv_o[:, s] = inv
        o_o[:, s] = (mixed * inv).astype(BF16)
    x1 = x + (nn(o_o[...], w[:, 3 * d : 4 * d]) + b_out)
    x1_o[...] = x1
    n2, _ = norm_stats(x1)
    a2_o[...] = (n2 * g2 + s2).astype(BF16)

    @pl.when(b == pl.num_programs(0) - 1)
    def _():
        pltpu.make_async_copy(w, w_o, out_sem).wait()


def unit_spec(i, d):
    return pl.BlockSpec((UNIT, d), lambda b, meta: (meta[PER * b + i], 0))


def k1(meta, tokens, cot, shard, blocks, ff):
    t, d = tokens.shape
    nb = t // BLOCK
    wide = shard.shape[1]
    blk = lambda n: pl.BlockSpec((BLOCK, n), lambda b, meta: (b, 0))
    fixed = lambda s: pl.BlockSpec(s, lambda b, meta: (0,) * len(s))
    sd = jax.ShapeDtypeStruct
    return pl.pallas_call(
        k1_body,
        grid_spec=pltpu.PrefetchScalarGridSpec(
            num_scalar_prefetch=1,
            grid=(nb,),
            in_specs=[unit_spec(i, d) for i in range(PER)] * 2 + [ANY] * 9,
            out_specs=[
                blk(3 * d),
                pl.BlockSpec((1, HEADS, BLOCK, BLOCK), lambda b, meta: (b, 0, 0, 0)),
                blk(d), blk(d), blk(d), blk(d), blk(d), blk(d), ANY,
                fixed((16, d)), fixed((4, ff // 4)), fixed((8, d)),
            ],
            scratch_shapes=[
                pltpu.VMEM((d, wide), BF16),
                pltpu.VMEM((16, d), F32),
                pltpu.SemaphoreType.DMA((17,)),
                pltpu.SemaphoreType.DMA,
            ],
        ),
        out_shape=[
            sd((t, 3 * d), BF16), sd((nb, HEADS, BLOCK, BLOCK), BF16), sd((t, d), F32), sd((t, d), BF16), sd((t, d), F32),
            sd((t, d), BF16), sd((t, d), BF16), sd((t, d), BF16), sd((d, wide), BF16),
            sd((16, d), F32), sd((4, ff // 4), F32), sd((8, d), F32),
        ],
        compiler_params=params(),
        cost_estimate=pl.CostEstimate(flops=2 * t * d * 5 * d, bytes_accessed=40 << 20, transcendentals=t * BLOCK * HEADS),
        name="norm_qkv_attend",
    )(meta, *([tokens] * PER), *([cot] * PER), shard, *blocks)


def gelu_and_slope(z):
    t = 1.0 / (1.0 + (0.3275911 * RSQRT2) * jnp.abs(z))
    e = jnp.exp(-0.5 * z * z)
    poly = t * (0.5 * 0.254829592 + t * (-0.5 * 0.284496736 + t * (0.5 * 1.421413741 + t * (
        -0.5 * 1.453152027 + t * (0.5 * 1.061405429)))))
    tail = poly * e
    cdf = jnp.where(z >= 0.0, 1.0 - tail, tail)
    return z * cdf, cdf + z * e * RSQRT_TAU


def mlp_body(ng, go, first, meta, *refs):
    a2o, a2p, g_o, g_p, b1, f1, f2 = refs[0:7]
    blocks = refs[7:11]
    at = 11
    prev = None
    if not first:
        prev, at = refs[11:15], 15
    yo, do, yp, dp, send, keep, db = refs[at : at + 7]
    a2, g, u_s, dz_s, w1, w2, dw1, dw2, sems = refs[at + 7 :]
    b = pl.program_id(0)
    last = pl.num_programs(0) - 1
    t, d = a2o.shape
    nb = t // BLOCK
    n = 128 * ng
    c, x, y, z = meta[I_C], meta[I_X], meta[I_Y], meta[I_Z]
    rows = f1.shape[0]
    quarter = rows // 4
    nk = d // 128

    def loads():
        ff = f1.shape[1]
        early = [(a2o, a2.at[pl.ds(0, t)]), (g_o, g.at[pl.ds(0, t)])]
        for zz in range(4):
            col = pl.multiple_of(zz * (ff // 4) + c * (ff // 8) + go * 128, 128)
            early.append((f1.at[:, pl.ds(col, n)], w1.at[pl.ds(pl.multiple_of(z * rows, 16), rows), pl.ds(zz * n, n)]))
        row = pl.multiple_of(c * (ff // 8) + go * 128, 128)
        early.append((f2.at[pl.ds(row, n)], w2.at[pl.ds(pl.multiple_of(z * n, 128), n)]))
        late = [(a2p, a2.at[pl.ds(t, t)]), (g_p, g.at[pl.ds(t, t)])]
        cps = [pltpu.make_async_copy(s, q, sems.at[i]) for i, (s, q) in enumerate(early + late)]
        return cps[: len(early)], cps[len(early) :]

    @pl.when(b == 0)
    def _():
        early, late = loads()
        for cp in early + late:
            cp.start()
        db[...] = jnp.zeros_like(db)
        for k, blk in enumerate(blocks):
            xx, yy = x, y
            if k == 1:
                xx, yy = x ^ (1 - c), y ^ c
            elif k == 2:
                xx, yy = x ^ c, y ^ (1 - c)
            elif k == 3:
                xx, yy = x ^ 1, y ^ 1
            p = 2 * yy + xx

            def place(f, carry):
                plane = z ^ (f + 1)
                r1 = pl.ds(pl.multiple_of(plane * rows + p * quarter, 16), quarter)
                for j in range(4 * ng):
                    w1[r1, j * 128 : (j + 1) * 128] = blk[f, j * quarter : (j + 1) * quarter, :]
                for gg in range(ng):
                    r2 = pl.ds(pl.multiple_of(plane * n + gg * 128 + p * 32, 32), 32)
                    for kk in range(nk):
                        lo = 4 * ng * quarter + (gg * nk + kk) * 32
                        w2[r2, kk * 128 : (kk + 1) * 128] = blk[f, lo : lo + 32, :]
                return carry

            lax.fori_loop(0, 3, place, 0)
        for cp in early:
            cp.wait()

    @pl.when(b == nb)
    def _():
        for cp in loads()[1]:
            cp.wait()

    rr = pl.ds(pl.multiple_of(b * BLOCK, BLOCK), BLOCK)
    a = a2[rr, :]
    gr = g[rr, :]
    lane = pl.ds(pl.multiple_of(c * (b1.shape[1] // 2) + go * 128, 128), n)
    bias = jnp.concatenate([b1[zz : zz + 1, lane] for zz in range(4)], axis=1)
    for k in range(2 * ng):
        cols = slice(k * 256, (k + 1) * 256)
        u, s = gelu_and_slope(nn(a, w1[:, cols]) + bias[:, cols])
        u_s[rr, cols] = u.astype(BF16)
        dz = (nt(gr, w2[cols, :]) * s).astype(BF16)
        dz_s[rr, cols] = dz
        db[0:1, cols] += jnp.sum(dz.astype(F32), axis=0, keepdims=True)
    yv = nn(u_s[rr, :], w2[...])
    dv = nt(dz_s[rr, :], w1[...])

    def put(y_ref, d_ref, y_old, d_old):
        y_ref[...] = (yv if y_old is None else yv + y_old[...].astype(F32)).astype(BF16)
        d_ref[...] = (dv if d_old is None else dv + d_old[...].astype(F32)).astype(BF16)

    @pl.when(b < nb)
    def _():
        put(yo, do, *((None, None) if first else prev[0:2]))

    @pl.when(b >= nb)
    def _():
        put(yp, dp, *((None, None) if first else prev[2:4]))

    @pl.when(b == last)
    def _():
        def weights(k, carry):
            cols = pl.ds(pl.multiple_of(k * 256, 256), 256)
            dw1[:, cols] = tn(a2[...], dz_s[:, cols]).astype(BF16)
            dw2[cols, :] = tn(u_s[:, cols], g[...]).astype(BF16)
            return carry

        lax.fori_loop(0, 2 * ng, weights, 0)
        for out, sel in ((send, 1 - meta[I_B1]), (keep, meta[I_B1])):
            for i in range(2):

                def cut(plane, carry):
                    r1 = pl.ds(pl.multiple_of(plane * rows + sel * 2 * quarter + i * quarter, 16), quarter)
                    for j in range(4 * ng):
                        out[i, plane, j * quarter : (j + 1) * quarter, :] = dw1[r1, j * 128 : (j + 1) * 128]
                    for gg in range(ng):
                        r2 = pl.ds(pl.multiple_of(plane * n + gg * 128 + sel * 64 + i * 32, 32), 32)
                        for kk in range(nk):
                            lo = 4 * ng * quarter + (gg * nk + kk) * 32
                            out[i, plane, lo : lo + 32, :] = dw2[r2, kk * 128 : (kk + 1) * 128]
                    return carry

                lax.fori_loop(0, 4, cut, 0)


def mlp(part, meta, a2o, a2p, g_o, g_p, b1, f1, f2, blocks, prev=()):
    ng, go = PARTS[part]
    first = not prev
    t, d = a2o.shape
    nb = t // BLOCK
    n = 128 * ng
    size = blocks[0].shape[1]
    sd = jax.ShapeDtypeStruct
    fixed = lambda s: pl.BlockSpec(s, lambda i, meta: (0,) * len(s), pipeline_mode=pl.Buffered(1))
    outf = lambda s: pl.BlockSpec(s, lambda i, meta: (0,) * len(s))
    own = pl.BlockSpec((BLOCK, d), lambda i, meta: (jnp.minimum(i, nb - 1), 0))
    other = pl.BlockSpec((BLOCK, d), lambda i, meta: (jnp.maximum(i - nb, 0), 0))
    tok = sd((t, d), BF16)
    half = (2, 4, size, 128)
    return pl.pallas_call(
        functools.partial(mlp_body, ng, go, first),
        grid_spec=pltpu.PrefetchScalarGridSpec(
            num_scalar_prefetch=1,
            grid=(2 * nb,),
            in_specs=[ANY] * 4 + [fixed(b1.shape)] + [ANY] * 2 + [fixed(k.shape) for k in blocks]
            + ([] if first else [own, own, other, other]),
            out_specs=[own, own, other, other, outf(half), outf(half), outf((8, 4 * n))],
            scratch_shapes=[
                pltpu.VMEM((2 * t, d), BF16), pltpu.VMEM((2 * t, d), BF16),
                pltpu.VMEM((2 * t, 4 * n), BF16), pltpu.VMEM((2 * t, 4 * n), BF16),
                pltpu.VMEM((d, 4 * n), BF16), pltpu.VMEM((4 * n, d), BF16),
                pltpu.VMEM((d, 4 * n), BF16), pltpu.VMEM((4 * n, d), BF16),
                pltpu.SemaphoreType.DMA((9,)),
            ],
        ),
        out_shape=[tok, tok, tok, tok, sd(half, BF16), sd(half, BF16), sd((8, 4 * n), F32)],
        compiler_params=params(),
        cost_estimate=pl.CostEstimate(flops=2 * 2 * t * d * 4 * n * 6, bytes_accessed=30 << 20, transcendentals=2 * t * 4 * n),
        name="hidden_first" if first else "hidden_second",
    )(meta, a2o, a2p, g_o, g_p, b1, f1, f2, *blocks, *prev)


EARLY = 8


def heads_back(pairs, lo, do, prob, inv, o, qkv, out):
    d = qkv.shape[1] // 3
    n = 128 * pairs
    lo_m, hi_m = lane_masks()
    for j in range(pairs):
        cols = slice(128 * (lo + j), 128 * (lo + j + 1))
        q, k, v = (qkv[:, i * d + cols.start : i * d + cols.stop] for i in range(3))
        dop = (do[:, 128 * j : 128 * (j + 1)].astype(F32) * inv[:, cols]).astype(BF16)
        dot = dop.astype(F32) * o[:, cols].astype(F32)
        dq = dk = dv = None
        for h, m in ((0, lo_m), (1, hi_m)):
            e = prob[0, 2 * j + h]
            mean = jnp.sum(dot * m.astype(F32), axis=-1, keepdims=True)
            dom = dop * m
            ds = (e.astype(F32) * (nt(dom, v) - mean)).astype(BF16)
            ms = m * SCALE
            parts = (nn(ds, k * ms), tn(ds, q * ms), tn(e, dom))
            dq, dk, dv = parts if dq is None else (dq + parts[0], dk + parts[1], dv + parts[2])
        for i, a in enumerate((dq, dk, dv)):
            out[:, i * n + 128 * j : i * n + 128 * (j + 1)] = a.astype(BF16)


def back_early_body(gp, da_o, da_p, x1_r, prob, inv, o, qkv, w_out, vec, dbf, dx1_o, dl, dq, acc):
    n = 64 * EARLY

    @pl.when(pl.program_id(0) == 0)
    def _():
        acc[...] = jnp.zeros_like(acc)
        acc[5:6] = dbf[0:1]

    da2 = da_o[...].astype(F32) + da_p[...].astype(F32)
    n2, r2 = norm_stats(x1_r[...])
    dx1 = gp[...].astype(F32) + norm_back(da2, n2, r2, vec[3:4])
    low = dx1.astype(BF16)
    acc[3:4] += jnp.sum(da2 * n2, axis=0, keepdims=True)
    acc[4:5] += jnp.sum(da2, axis=0, keepdims=True)
    acc[2:3] += jnp.sum(low.astype(F32), axis=0, keepdims=True)
    dx1_o[...] = dx1
    dl[...] = low
    do = nt(low, w_out[0:n, :]).astype(BF16)
    heads_back(EARLY // 2, 0, do, prob, inv, o, qkv, dq)


def back_early(gp, da_o, da_p, x1, prob, inv, o, qkv, w, vec, dbf):
    t, d = gp.shape
    blk = lambda n: pl.BlockSpec((BLOCK, n), lambda b: (b, 0))
    sd = jax.ShapeDtypeStruct
    fixed = lambda s: pl.BlockSpec(s, lambda b: (0,) * len(s), pipeline_mode=pl.Buffered(1))
    cols = 3 * 64 * EARLY
    return pl.pallas_call(
        back_early_body,
        grid=(t // BLOCK,),
        in_specs=[blk(d), blk(d), blk(d), blk(d),
                  pl.BlockSpec((1, EARLY, BLOCK, BLOCK), lambda b: (b, 0, 0, 0)), blk(d), blk(d), blk(3 * d),
                  pl.BlockSpec((d, d), lambda b: (0, 3), pipeline_mode=pl.Buffered(1)),
                  fixed(vec.shape), fixed(dbf.shape)],
        out_specs=[blk(d), blk(d), blk(cols), pl.BlockSpec((128, d), lambda b: (0, 0))],
        out_shape=[sd((t, d), F32), sd((t, d), BF16), sd((t, cols), BF16), sd((128, d), F32)],
        compiler_params=params(),
        cost_estimate=pl.CostEstimate(flops=2 * t * d * 4 * d, bytes_accessed=24 << 20, transcendentals=0),
        name="attend_back_early",
    )(gp, da_o, da_p, x1, prob, inv, o, qkv, w, vec, dbf)


def back_late_body(meta, *refs):
    tok = refs[0:4]
    dx1, dl, dqe, prob, inv, o, qkv, w, vec, acc_in = refs[4:14]
    gt_o, dq, acc = refs[14:17]
    gt, sems = refs[17:]
    b = pl.program_id(0)
    nb = pl.num_programs(0)
    d = dl.shape[1]
    slot = lax.rem(b, 2)
    n = 64 * EARLY

    def puts(step, sl):
        return [
            pltpu.make_async_copy(
                gt.at[sl, pl.ds(i * UNIT, UNIT)],
                gt_o.at[pl.ds(pl.multiple_of(meta[PER * step + i] * UNIT, UNIT), UNIT)],
                sems.at[sl, i],
            )
            for i in range(PER)
        ]

    @pl.when(b == 0)
    def _():
        acc[...] = acc_in[...]

    @pl.when(b >= 2)
    def _():
        for cp in puts(b - 2, slot):
            cp.wait()

    do = nt(dl[...], w[n:, 3 * d : 4 * d]).astype(BF16)
    heads_back((HEADS - EARLY) // 2, EARLY // 2, do, prob, inv, o, qkv, dq)
    rest = d - n
    da1 = None
    for i in range(3):
        part = nt(dqe[:, i * n : (i + 1) * n], w[:, i * d : i * d + n])
        part = part + nt(dq[:, i * rest : (i + 1) * rest], w[:, i * d + n : (i + 1) * d])
        da1 = part if da1 is None else da1 + part
    x = jnp.concatenate([r[...] for r in tok], axis=0).astype(F32)
    n1, r1 = norm_stats(x)
    acc[0:1] += jnp.sum(da1 * n1, axis=0, keepdims=True)
    acc[1:2] += jnp.sum(da1, axis=0, keepdims=True)
    gt[slot] = dx1[...] + norm_back(da1, n1, r1, vec[0:1])
    for cp in puts(b, slot):
        cp.start()

    @pl.when(b == nb - 1)
    def _():
        for cp in puts(b - 1, 1 - slot) + puts(b, slot):
            cp.wait()


def back_late(meta, tokens, dx1, dl, dqe, prob, inv, o, qkv, w, vec, acc_in):
    t, d = tokens.shape
    late = HEADS - EARLY
    blk = lambda n: pl.BlockSpec((BLOCK, n), lambda b, meta: (b, 0))
    sd = jax.ShapeDtypeStruct
    fixed = lambda s: pl.BlockSpec(s, lambda b, meta: (0,) * len(s), pipeline_mode=pl.Buffered(1))
    return pl.pallas_call(
        back_late_body,
        grid_spec=pltpu.PrefetchScalarGridSpec(
            num_scalar_prefetch=1,
            grid=(t // BLOCK,),
            in_specs=[unit_spec(i, d) for i in range(PER)] + [
                blk(d), blk(d), blk(dqe.shape[1]),
                pl.BlockSpec((1, late, BLOCK, BLOCK), lambda b, meta: (b, EARLY // late, 0, 0)), blk(d), blk(d), blk(3 * d),
            ] + [fixed(a.shape) for a in (w, vec, acc_in)],
            out_specs=[ANY, blk(3 * 64 * late), pl.BlockSpec((128, d), lambda b, meta: (0, 0))],
            scratch_shapes=[pltpu.VMEM((2, BLOCK, d), F32), pltpu.SemaphoreType.DMA((2, PER))],
        ),
        out_shape=[sd((t, d), F32), sd((t, 3 * 64 * late), BF16), sd((128, d), F32)],
        compiler_params=params(),
        cost_estimate=pl.CostEstimate(flops=2 * t * d * 5 * d, bytes_accessed=20 << 20, transcendentals=0),
        name="attend_back_late",
    )(meta, *([tokens] * PER), dx1, dl, dqe, prob, inv, o, qkv, w, vec, acc_in)


def split(meta, stage, send_o, keep_o, at, width):
    c = meta[I_C]
    rows = stage.shape[0] // 4
    n = rows // 2
    for zz in range(4):
        for i in range(2):
            for out, h in ((send_o, 1 - c), (keep_o, c)):
                lot = stage[pl.ds(pl.multiple_of(zz * rows + n * h + (n // 2) * i, 16), n // 2), 0:width]
                out[i, 0, zz, :, pl.ds(at, width)] = lot[0 : n // 4]
                out[i, 1, zz, :, pl.ds(at, width)] = lot[n // 4 :]


def grads_early_body(meta, a1, dq, o, dl, send_o, keep_o, stage):
    d = a1.shape[1]
    s = pl.program_id(0)
    last = pl.num_programs(0) - 1

    @pl.when(s < last)
    def _():
        stage[...] = tn(a1[...], dq[...]).astype(BF16)

    @pl.when(s == last)
    def _():
        stage[...] = tn(o[...], dl[...]).astype(BF16)

    split(meta, stage, send_o, keep_o, pl.multiple_of(s * d, 128), d)


def grads_late_body(meta, a1, dq, acc, *refs):
    d = a1.shape[1]
    c = meta[I_C]
    rows = d // 4
    dbs, (send_o, keep_o, stage) = refs[: len(PARTS)], refs[len(PARTS) :]
    stage[...] = tn(a1[...], dq[...]).astype(BF16)
    split(meta, stage, send_o, keep_o, 0, d)
    stage[:, 0:128] = acc[...].T.astype(BF16)
    stage[:, 128:256] = jnp.zeros((d, 128), BF16)
    for zz in range(4):
        parts = []
        for hh in range(2):
            for src, (ng, go) in zip(dbs, PARTS):
                for k in range(ng):
                    at = (zz * ng + k) * 128
                    parts.append(jnp.where(hh == c, src[0:1, at : at + 128], 0.0))
        parts.append(jnp.zeros((16 - len(parts), 128), F32))
        stage[zz * rows : zz * rows + 16, 128:256] = jnp.concatenate(parts, axis=0).astype(BF16)
    split(meta, stage, send_o, keep_o, d, EXT)


def grads(body, steps, wide, meta, a1, dq, *rest, cost=None):
    t, d = a1.shape
    cost = cost or pl.CostEstimate(flops=2 * t * d * steps * d, bytes_accessed=12 << 20, transcendentals=0)
    half = (2, 2, 4, d // 32, wide)
    sd = jax.ShapeDtypeStruct
    fixed = lambda a: pl.BlockSpec(a.shape, lambda s, meta: (0,) * a.ndim, pipeline_mode=pl.Buffered(1))
    outf = pl.BlockSpec(half, lambda s, meta: (0,) * 5)
    last = dq.shape[1] // d - 1
    return pl.pallas_call(
        body,
        grid_spec=pltpu.PrefetchScalarGridSpec(
            num_scalar_prefetch=1,
            grid=(steps,),
            in_specs=[fixed(a1), pl.BlockSpec((t, d), lambda s, meta: (0, jnp.minimum(s, last)))]
            + [fixed(a) for a in rest],
            out_specs=[outf, outf],
            scratch_shapes=[pltpu.VMEM((d, d), BF16)],
        ),
        out_shape=[sd(half, BF16), sd(half, BF16)],
        compiler_params=params(),
        cost_estimate=cost,
        name="weight_grads",
    )(meta, a1, dq, *rest)


def out_body(meta, ya, yb, x1, vec, out, buf, sems):
    b = pl.program_id(0)
    slot = lax.rem(b, 2)

    def puts(step, sl):
        return [
            pltpu.make_async_copy(
                buf.at[sl, pl.ds(i * UNIT, UNIT)],
                out.at[pl.ds(pl.multiple_of(meta[PER * step + i] * UNIT, UNIT), UNIT)],
                sems.at[sl, i],
            )
            for i in range(PER)
        ]

    @pl.when(b >= 2)
    def _():
        for cp in puts(b - 2, slot):
            cp.wait()

    y = ya[...].astype(F32) + yb[...].astype(F32)
    buf[slot] = (x1[...] + (y + vec[5:6])).astype(BF16)
    for cp in puts(b, slot):
        cp.start()

    @pl.when(b == pl.num_programs(0) - 1)
    def _():
        for cp in puts(b - 1, 1 - slot) + puts(b, slot):
            cp.wait()


def layer_output(meta, ya, yb, x1, vec):
    t, d = x1.shape
    blk = lambda n: pl.BlockSpec((BLOCK, n), lambda b, meta: (b, 0))
    fixed = lambda s: pl.BlockSpec(s, lambda b, meta: (0,) * len(s), pipeline_mode=pl.Buffered(1))
    return pl.pallas_call(
        out_body,
        grid_spec=pltpu.PrefetchScalarGridSpec(
            num_scalar_prefetch=1,
            grid=(t // BLOCK,),
            in_specs=[blk(d), blk(d), blk(d), fixed(vec.shape)],
            out_specs=ANY,
            scratch_shapes=[pltpu.VMEM((2, BLOCK, d), BF16), pltpu.SemaphoreType.DMA((2, PER))],
        ),
        out_shape=jax.ShapeDtypeStruct((t, d), BF16),
        compiler_params=params(),
        cost_estimate=pl.CostEstimate(flops=4 * t * d, bytes_accessed=8 << 20, transcendentals=0),
        name="layer_out",
    )(meta, ya, yb, x1, vec)


def halve_body(jobs, meta, *refs):
    at, to = 0, sum(2 * n for _, n, _ in jobs)
    for place, n, loops in jobs:
        ks, vs, (send, keep) = refs[at : at + n], refs[at + n : at + 2 * n], refs[to : to + 2]
        at, to = at + 2 * n, to + 2
        bit = meta[place]
        for out, sel in ((send, 1 - bit), (keep, bit)):
            for pre in range(ks[0].shape[0]):

                def step(r, carry):
                    col = 0
                    for k, v in zip(ks, vs):
                        w = k.shape[-1]
                        part = k[pre, sel, r].astype(F32) + v[pre, sel, r].astype(F32)
                        out[pre, r, :, col : col + w] = part.astype(BF16)
                        col += w
                    return carry

                lax.fori_loop(0, loops, step, 0)


def halve(meta, *jobs):
    sd = jax.ShapeDtypeStruct
    jobs = [(p, k if isinstance(k, list) else [k], v if isinstance(v, list) else [v]) for p, k, v in jobs]
    outs = []
    for _, ks, _ in jobs:
        shape = ks[0].shape
        outs += [sd((shape[0],) + shape[2:-1] + (sum(k.shape[-1] for k in ks),), BF16)] * 2
    arrays = [a for _, ks, vs in jobs for a in (*ks, *vs)]
    size = sum(a.size for a in arrays) // 2
    return pl.pallas_call(
        functools.partial(halve_body, tuple((p, len(ks), ks[0].shape[2]) for p, ks, _ in jobs)),
        in_specs=[pl.BlockSpec(memory_space=pltpu.SMEM)] + [WHOLE] * len(arrays),
        out_specs=[WHOLE] * len(outs),
        out_shape=outs,
        compiler_params=params(),
        cost_estimate=pl.CostEstimate(flops=size, bytes_accessed=6 * size, transcendentals=0),
        name="add_halve",
    )(meta, *arrays)


def total(routes, k, v):
    piece = k.astype(F32) + v.astype(F32)
    if routes.n_dp > 8:
        groups = [[j + 8 * o for o in range(routes.n_dp // 8)] for j in range(8)]
        piece = lax.psum(piece, "dp", axis_index_groups=groups)
    return piece.astype(BF16)


def ranks(meta, t):
    cc, x, y = holder(meta, t)
    return cc, 2 * jnp.where(cc == 0, x, y) + jnp.where(cc == 0, y, x)


def final_hidden_body(meta, *refs):
    pieces = refs[:8]
    d1, d2 = refs[8:10]
    rows, ff = d1.shape
    d = d2.shape[1]
    quarter = rows // 4
    nk = d // 128
    for t in range(8):
        cc, q = ranks(meta, t)
        at = 0
        for ng, go in PARTS:
            r1 = pl.ds(pl.multiple_of(q * quarter, 16), quarter)
            for zz in range(4):
                for g in range(ng):
                    col = pl.multiple_of(zz * (ff // 4) + cc * (ff // 8) + (go + g) * 128, 128)
                    d1[r1, pl.ds(col, 128)] = pieces[t][at : at + quarter, :].astype(F32)
                    at += quarter
            for g in range(ng):
                r2 = pl.ds(pl.multiple_of(cc * (ff // 8) + (go + g) * 128 + q * 32, 32), 32)
                for k in range(nk):
                    d2[r2, k * 128 : (k + 1) * 128] = pieces[t][at : at + 32, :].astype(F32)
                    at += 32


def final_mixed_body(meta, *refs):
    pieces = refs[:8]
    dqkv, dout, dg1, ds1, dbo, dg2, ds2, dbf, db1 = refs[8:17]
    ext = refs[17]
    n = pieces[0].shape[0]
    d = dout.shape[1]
    for t in range(8):
        cc, x, y = holder(meta, t)
        first, second = jnp.where(cc == 0, x, y), jnp.where(cc == 0, y, x)
        rows = pl.ds(pl.multiple_of(n * (4 * cc + 2 * first + second), n), n)
        v = pieces[t][...].astype(F32)
        m = 64 * EARLY
        for k in range(3):
            dqkv[rows, k * d : k * d + m] = v[:, k * m : (k + 1) * m]
            at = 3 * m + d + k * (d - m)
            dqkv[rows, k * d + m : (k + 1) * d] = v[:, at : at + d - m]
        dout[rows, :] = v[:, 3 * m : 3 * m + d]
        ext[rows, :] = v[:, 4 * d :]
    vec = ext[:, 0:128].T
    for i, ref in enumerate((dg1, ds1, dbo, dg2, ds2, dbf)):
        ref[...] = vec[i]
    for r in range(db1.shape[0] // 128):
        db1[pl.ds(128 * r, 128)] = ext[r, 128:256]


def final(body, meta, pieces, outs, scratch=()):
    sd = [jax.ShapeDtypeStruct(s, F32) for s in outs]
    res = pl.pallas_call(
        body,
        in_specs=[pl.BlockSpec(memory_space=pltpu.SMEM)] + [WHOLE] * 8,
        out_specs=[WHOLE] * len(outs),
        scratch_shapes=list(scratch),
        out_shape=sd,
        compiler_params=params(),
        name="place_sums",
    )(meta, *pieces)
    return res


def scalars(chip_ids):
    n = chip_ids.shape[0] // UNIT
    ids = chip_ids.reshape(n, UNIT)[:, 0]
    here = jnp.arange(n, dtype=jnp.int32)
    same = (ids[:, None] == ids[None, :]).astype(jnp.int32)
    long = jnp.sum(same, axis=1) > 1
    longs = long.astype(jnp.int32)
    before = jnp.sum(jnp.where(here[None, :] < here[:, None], longs[None, :], 0), axis=1)
    total = jnp.sum(longs)
    pos = jnp.where(long, before, total + here - before)
    src = jnp.sum(jnp.where(pos[None, :] == here[:, None], here[None, :], 0), axis=1)
    dp, z = lax.axis_index("dp"), lax.axis_index("fsdp")
    c, x, y = dp & 1, (dp >> 1) & 1, (dp >> 2) & 1
    b1, b2 = jnp.where(c == 0, x, y), jnp.where(c == 0, y, x)
    rest = jnp.stack([total >> 2, c, x, y, z, b1, b2, jnp.zeros_like(z), z & 1, z >> 1]).astype(jnp.int32)
    return jnp.concatenate([src.astype(jnp.int32), rest])


def on_device(n_dp, n_z, tokens, chip_ids, ln1_gain, ln1_bias, w_qkv, w_out, b_out, ln2_gain, ln2_bias,
              w_fc1, b_fc1, w_fc2, b_fc2, cotangent):
    routes = Routes(n_dp, n_z)
    t, d = tokens.shape
    ff = w_fc1.shape[1]
    rows = w_qkv.shape[0]
    pos = lax.axis_index("dp").astype(jnp.int32).reshape(1)
    meta = scalars(chip_ids)

    vecs = (ln1_gain, ln1_bias, b_out, ln2_gain, ln2_bias, b_fc2)
    mixed, near, far, hid = pack(pos, w_qkv, w_out, vecs, b_fc1, w_fc1, w_fc2)

    mate, far_h = routes.z_flip(hid, 1), routes.z_flip(hid, 2)
    last_h = routes.z_flip(far_h, 1)
    p_mixed = gather_mixed(routes, near, far, (mate, far_h), last_h)
    block = jnp.stack([mate, far_h, last_h])
    p_hid = [block, routes.first(block), routes.second(block)]
    qkv, prob, inv, o, x1, a2, a1, gp, w, vec, b1, dbf = k1(
        meta, tokens, cotangent, tie(mixed, block), p_mixed, ff)
    swap = lax.optimization_barrier((a2, gp, *p_hid[1:]))
    p_hid.append(routes.second(swap[2]))
    a2p, gpp = routes.core(swap[0]), routes.core(swap[1])
    yo, do, yp, dp, sh, kh, db = mlp(0, meta, a2, a2p, gp, gpp, b1, w_fc1, w_fc2, p_hid)

    cut = lambda a, pre, loops: a.reshape(pre, 2, loops, 96, 128)
    nh = sh.shape[2] // 96
    yq, dq = routes.core(yp), routes.core(dp)
    got_h = routes.first(sh)
    dx1, dl, dqe, acc = back_early(gp, do, dq, x1, prob, inv, o, qkv, w, vec, dbf)
    early = 3 * 64 * EARLY + d
    late = 4 * d - early + EXT
    sm, km = grads(grads_early_body, early // d, early, meta, a1, dqe, o, dl, cost=SHORT)
    got_m = routes.core(tie(sm, got_h))
    s_h, k_h = halve(meta, (I_B2, cut(kh, 1, 4 * nh), cut(tie(got_h, sm), 1, 4 * nh)))
    got_h = routes.second(s_h)
    chunk = lambda a, pre, loops: a.reshape(pre, 2, loops, d // 32, a.shape[-1])
    s_m, k_m = halve(meta, (I_B1, chunk(km, 1, 8), chunk(tie(got_m, s_h), 1, 8)))
    got_m = routes.first(s_m)
    gt, dql, acc = back_late(meta, tokens, tie(dx1, s_m, yq), dl, dqe, prob, inv, o, qkv, w, vec, acc)

    s_h, k_h, s_m, k_m = halve(
        meta, (I_Z + 4, cut(k_h, 2, nh), cut(tie(got_h, acc), 2, nh)),
        (I_B2, chunk(k_m, 1, 4), chunk(tie(got_m, acc), 1, 4)))
    got_m, got_h = routes.second(s_m), routes.z_flip(s_h, 1)
    sl, kl = grads(grads_late_body, 1, late, meta, tie(a1, s_m), dql, acc, db)
    got_l = routes.core(tie(sl, got_m, got_h))
    s_m, k_m, s_h, k_h = halve(
        meta, (I_Z + 4, chunk(k_m, 2, 1), chunk(tie(got_m, sl), 2, 1)),
        (I_Z + 5, cut(k_h, 1, nh), cut(tie(got_h, sl), 1, nh)))
    got_m, got_h = routes.z_flip(s_m, 1), routes.z_flip(s_h, 2)
    s_l, k_l = halve(meta, (I_B1, chunk(kl, 1, 8), chunk(tie(got_l, s_h), 1, 8)))
    got_l = routes.first(s_l)
    layer_out = layer_output(meta, yo, yq, x1, tie(vec, s_l))
    s_l, k_l, s_m, k_m = halve(meta, (I_B2, chunk(k_l, 1, 4), chunk(tie(got_l, layer_out), 1, 4)),
                               (I_Z + 5, chunk(k_m, 1, 1), chunk(tie(got_m, layer_out), 1, 1)))
    got_l, got_m = routes.second(s_l), routes.z_flip(s_m, 2)
    piece = total(routes, k_h.reshape(-1, 128), tie(got_h, s_l).reshape(-1, 128))
    near_by = around(routes, piece)
    s_l, k_l = halve(meta, (I_Z + 4, chunk(k_l, 2, 1), chunk(tie(got_l, piece), 2, 1)))
    s_l, k_l = halve(meta, (I_Z + 5, chunk(k_l, 1, 1), chunk(tie(routes.z_flip(s_l, 1), got_m), 1, 1)))
    got_l = tie(routes.z_flip(s_l, 2), *near_by)
    side = lambda a, b: jnp.concatenate([a.reshape(d // 32, -1), b.reshape(d // 32, -1)], axis=1)
    piece = total(routes, side(k_m, k_l), side(got_m, got_l))
    near_m = around(routes, piece)
    pieces = near_by + [routes.core(b) for b in lax.optimization_barrier((*near_by, piece))[:4]]
    g_fc1, g_fc2 = final(final_hidden_body, meta, pieces, [w_fc1.shape, w_fc2.shape])
    near_m = list(lax.optimization_barrier((*near_m, g_fc1))[:4])
    pieces_m = near_m + [routes.core(b) for b in near_m]

    vecs = [(rows,)] * 6
    g_qkv, g_out, dg1, ds1, dbo, dg2, ds2, dbf2, db1 = final(
        final_mixed_body, meta, pieces_m, [w_qkv.shape, w_out.shape, *vecs, b_fc1.shape],
        [pltpu.VMEM((rows, EXT), F32)])
    return (layer_out, gt, dg1, ds1, g_qkv, g_out, dbo, dg2, ds2, g_fc1, db1, g_fc2, dbf2)


def solution(mesh):
    token, part, plain = P(ALL, None), P("fsdp", None), P("fsdp")
    return jax.shard_map(
        functools.partial(on_device, mesh.shape["dp"], mesh.shape["fsdp"]),
        mesh=mesh,
        in_specs=(token, P(ALL), plain, plain, part, part, plain, plain, plain, part, plain, part, plain, token),
        out_specs=(token, token, plain, plain, part, part, plain, plain, plain, part, plain, part, plain),
        check_vma=False,
    )
```

```python
import functools
import math

import jax
import jax.numpy as jnp
from jax import lax
from jax.experimental import pallas as pl
from jax.experimental.pallas import tpu as pltpu
from jax.sharding import PartitionSpec as P

HEADS = 12
HEAD = 64
UNIT = 64
BLOCK = 256
PER = BLOCK // UNIT
EPS = 1e-05
NEG = -1e30
RSQRT2 = 1.0 / math.sqrt(2.0)
RSQRT_TAU = 1.0 / math.sqrt(2.0 * math.pi)
SCALE = 1.0 / math.sqrt(HEAD)
EXT = 256
VMEM_LIMIT = 64 * 1024 * 1024 - 65536
ALL = ("dp", "fsdp")
F32 = jnp.float32
BF16 = jnp.bfloat16

I_LONG, I_C, I_X, I_Y, I_Z, I_B1, I_B2 = 16, 17, 18, 19, 20, 21, 22


def nn(a, b):
    return lax.dot_general(a, b, (((1,), (0,)), ((), ())), preferred_element_type=F32)


def nt(a, b):
    return lax.dot_general(a, b, (((1,), (1,)), ((), ())), preferred_element_type=F32)


def tn(a, b):
    return lax.dot_general(a, b, (((0,), (0,)), ((), ())), preferred_element_type=F32)


SHORT = pl.CostEstimate(flops=1, bytes_accessed=1, transcendentals=0)


def params(**kw):
    return pltpu.CompilerParams(vmem_limit_bytes=VMEM_LIMIT, **kw)


ANY = pl.BlockSpec(memory_space=pl.ANY)
WHOLE = pl.BlockSpec(memory_space=pltpu.VMEM)


def tie(a, *after):
    return lax.optimization_barrier((a,) + after)[0]


class Routes:
    def __init__(self, n_dp, n_z):
        self.n_dp, self.n_z = n_dp, n_z

    def table(self, move):
        pairs = []
        for d in range(self.n_dp):
            for z in range(self.n_z):
                e, w = move(d, z)
                pairs.append((d * self.n_z + z, e * self.n_z + w % self.n_z))
        return pairs

    def core(self, a):
        return lax.ppermute(a, ALL, self.table(lambda d, z: (d ^ 1, z)))

    def first(self, a):
        return lax.ppermute(a, ALL, self.table(lambda d, z: (d ^ (2 if d % 2 == 0 else 4), z)))

    def second(self, a):
        return lax.ppermute(a, ALL, self.table(lambda d, z: (d ^ (4 if d % 2 == 0 else 2), z)))

    def z_near(self, a):
        return lax.ppermute(a, ALL, self.table(lambda d, z: (d, z + (1 if d % 2 == 0 else self.n_z - 1))))

    def z_far(self, a):
        return lax.ppermute(a, ALL, self.table(lambda d, z: (d, z + 2)))

    def z_flip(self, a, bit):
        return lax.ppermute(a, ALL, self.table(lambda d, z: (d, z ^ bit)))

    def diagonal(self, a):
        return lax.ppermute(a, ALL, self.table(lambda d, z: (d ^ 6, z)))


def spread(routes, block):
    own = around(routes, block)
    return own + [routes.core(b) for b in own]


def around(routes, block):
    return [block, routes.first(block), routes.second(block), routes.diagonal(block)]


def holder(meta, t):
    flip = t // 4
    cc = meta[I_C] if flip == 0 else 1 - meta[I_C]
    x, y = meta[I_X], meta[I_Y]
    t = t % 4
    if t == 1:
        x, y = x ^ (1 - cc), y ^ cc
    elif t == 2:
        x, y = x ^ cc, y ^ (1 - cc)
    elif t == 3:
        x, y = x ^ 1, y ^ 1
    return cc, x, y


def gather_mixed(routes, near, far, early, late):
    block = jnp.concatenate([routes.z_near(near), routes.z_far(far)], axis=1)
    one = routes.first(block)
    two = routes.second(block)
    own = [block, one, two, routes.second(tie(one, two, *early))]
    return own + [routes.core(b) for b in own[:3]] + [routes.core(tie(own[3], late))]


def mixed_copies(meta, shard, blocks, w, sems):
    rows, wide = shard.shape
    quarter, part = rows // 4, wide // 2
    z = meta[I_Z]
    out = [(shard, w.at[pl.ds(pl.multiple_of(z * rows, 16), rows)])]
    for t, block in enumerate(blocks):
        cc, x, y = holder(meta, t)
        q = 2 * y + x
        plane = lax.rem(z + jnp.where(cc == 0, 3, 1), 4)
        far = lax.rem(z + 2, 4)
        out.append((block.at[:, pl.ds(0, wide)],
                    w.at[pl.ds(pl.multiple_of(plane * rows + q * quarter, 16), quarter)]))
        out.append((block.at[:, pl.ds(wide, part)],
                    w.at[pl.ds(pl.multiple_of(far * rows + q * quarter, 16), quarter),
                         pl.ds(pl.multiple_of(cc * part, 128), part)]))
    return [pltpu.make_async_copy(s, d, sems.at[i]) for i, (s, d) in enumerate(out)]


PARTS = ((3, 0),)


def piece_rows(ng, rows, d):
    return 4 * ng * (rows // 4) + ng * (d // 128) * 32


def pack_body(pos, *refs):
    w_qkv, w_out = refs[0:2]
    vecs, b1, f1, f2 = refs[2:8], refs[8], refs[9], refs[10]
    mixed, near, far = refs[11:14]
    outs, sems = refs[14 : 14 + len(PARTS)], refs[14 + len(PARTS)]
    c, x, y = pos[0] & 1, (pos[0] >> 1) & 1, (pos[0] >> 2) & 1
    p = 2 * y + x
    d = w_out.shape[1]
    rows = w_out.shape[0]
    quarter = rows // 4
    ff = f1.shape[1]
    copies = []
    for out, (ng, go) in zip(outs, PARTS):
        for zz in range(4):
            for g in range(ng):
                col = pl.multiple_of(zz * (ff // 4) + c * (ff // 8) + (go + g) * 128, 128)
                copies.append((f1.at[pl.ds(pl.multiple_of(p * quarter, 16), quarter), pl.ds(col, 128)],
                               out.at[pl.ds((zz * ng + g) * quarter, quarter)]))
        base = 4 * ng * quarter
        for g in range(ng):
            row = pl.multiple_of(c * (ff // 8) + (go + g) * 128 + p * 32, 32)
            for k in range(d // 128):
                copies.append((f2.at[pl.ds(row, 32), pl.ds(k * 128, 128)],
                               out.at[pl.ds(base + (g * (d // 128) + k) * 32, 32)]))
    copies = [pltpu.make_async_copy(s, t, sems.at[i]) for i, (s, t) in enumerate(copies)]
    for cp in copies:
        cp.start()
    mixed[:, 0 : 3 * d] = w_qkv[...]
    mixed[:, 3 * d : 4 * d] = w_out[...]
    lines = [v[...].astype(F32).reshape(1, rows) for v in vecs] + [jnp.zeros((128 - len(vecs), rows), F32)]
    mixed[:, 4 * d : 4 * d + 128] = jnp.concatenate(lines, axis=0).T.astype(BF16)
    n = b1.shape[0] // 128
    lines = [b1[pl.ds(128 * i, 128)].astype(F32).reshape(1, 128) for i in range(n)] + [jnp.zeros((rows - n, 128), F32)]
    mixed[:, 4 * d + 128 :] = jnp.concatenate(lines, axis=0).astype(BF16)
    own = pl.ds(pl.multiple_of(p * quarter, 16), quarter)
    near[...] = mixed[own, :]
    part = mixed.shape[1] // 2
    far[...] = mixed[own, pl.ds(pl.multiple_of(c * part, 128), part)]
    for cp in copies:
        cp.wait()


def pack(pos, w_qkv, w_out, vecs, b1, f1, f2):
    rows, d = w_out.shape
    wide = 4 * d + EXT
    sd = jax.ShapeDtypeStruct
    count = sum(4 * ng + ng * (d // 128) for ng, _ in PARTS)
    return pl.pallas_call(
        pack_body,
        in_specs=[pl.BlockSpec(memory_space=pltpu.SMEM)] + [WHOLE] * 9 + [ANY] * 2,
        out_specs=[WHOLE] * (3 + len(PARTS)),
        scratch_shapes=[pltpu.SemaphoreType.DMA((count,))],
        out_shape=[sd((rows, wide), BF16), sd((rows // 4, wide), BF16), sd((rows // 4, wide // 2), BF16)]
        + [sd((piece_rows(ng, rows, d), 128), BF16) for ng, _ in PARTS],
        compiler_params=params(),
        name="pack",
    )(pos, w_qkv, w_out, *vecs, b1, f1, f2)


def norm_stats(rows):
    centred = rows - jnp.mean(rows, axis=-1, keepdims=True)
    inverse = lax.rsqrt(jnp.mean(centred * centred, axis=-1, keepdims=True) + EPS)
    return centred * inverse, inverse


def norm_back(grad, normed, inverse, gain):
    e = grad * gain
    return inverse * (
        e - jnp.mean(e, axis=-1, keepdims=True) - normed * jnp.mean(e * normed, axis=-1, keepdims=True)
    )


def lane_masks():
    lane = lax.broadcasted_iota(jnp.int32, (1, 2 * HEAD), 1)
    low = jnp.where(lane < HEAD, 1.0, 0.0).astype(BF16)
    return low, (1.0 - low.astype(F32)).astype(BF16)


def k1_body(meta, *refs):
    tok, cot = refs[0:4], refs[4:8]
    shard, blocks = refs[8], refs[9:17]
    qkv_o, prob_o, inv_o, o_o, x1_o, a2_o, a1_o, gp_o, w_o, vec_o, b1_o, dbf_o = refs[17:29]
    w, vec, sems, out_sem = refs[29:]
    b = pl.program_id(0)
    d = w.shape[0]

    @pl.when(b == 0)
    def _():
        copies = mixed_copies(meta, shard, blocks, w, sems)
        for cp in copies:
            cp.start()
        for cp in copies:
            cp.wait()
        pltpu.make_async_copy(w, w_o, out_sem).start()
        ext = w[:, 4 * d : 4 * d + 128].astype(F32).T
        vec[...] = ext[0:16]
        vec_o[...] = ext[0:16]
        dbf_o[...] = jnp.zeros_like(dbf_o)
        rows = d // 4
        for zz in range(4):
            for r in range(b1_o.shape[1] // 128):
                b1_o[zz : zz + 1, 128 * r : 128 * (r + 1)] = w[
                    zz * rows : zz * rows + 8, 4 * d + 128 : 4 * d + 256
                ].astype(F32)[r : r + 1]

    g1, s1, b_out = vec[0:1], vec[1:2], vec[2:3]
    g2, s2 = vec[3:4], vec[4:5]
    x = jnp.concatenate([r[...] for r in tok], axis=0).astype(F32)
    g = jnp.concatenate([r[...] for r in cot], axis=0)
    gp_o[...] = g
    dbf_o[0:1] += jnp.sum(g.astype(F32), axis=0, keepdims=True)
    n1, _ = norm_stats(x)
    a1 = (n1 * g1 + s1).astype(BF16)
    a1_o[...] = a1
    for k in range(3):
        qkv_o[:, k * d : (k + 1) * d] = nn(a1, w[:, k * d : (k + 1) * d]).astype(BF16)
    row = lax.broadcasted_iota(jnp.int32, (BLOCK, BLOCK), 0) // UNIT
    col = lax.broadcasted_iota(jnp.int32, (BLOCK, BLOCK), 1) // UNIT
    keep = (row == col) | (b < meta[I_LONG])
    low, high = lane_masks()
    left = lax.broadcasted_iota(jnp.int32, (BLOCK, 2 * HEAD), 1) < HEAD
    for j in range(HEADS // 2):
        s = slice(128 * j, 128 * (j + 1))
        q = qkv_o[:, s]
        k = qkv_o[:, d + 128 * j : d + 128 * (j + 1)]
        v = qkv_o[:, 2 * d + 128 * j : 2 * d + 128 * (j + 1)]
        mixed, inv = None, []
        for h, m in ((0, low), (1, high)):
            sc = jnp.where(keep, nt(q * (m * SCALE), k), NEG)
            e = jnp.exp(sc - jnp.max(sc, axis=-1, keepdims=True))
            inv.append(1.0 / jnp.sum(e, axis=-1, keepdims=True))
            e = e.astype(BF16)
            prob_o[0, 2 * j + h] = e
            part = nn(e, v * m)
            mixed = part if mixed is None else mixed + part
        inv = jnp.where(left, inv[0], inv[1])
        inv_o[:, s] = inv
        o_o[:, s] = (mixed * inv).astype(BF16)
    x1 = x + (nn(o_o[...], w[:, 3 * d : 4 * d]) + b_out)
    x1_o[...] = x1
    n2, _ = norm_stats(x1)
    a2_o[...] = (n2 * g2 + s2).astype(BF16)

    @pl.when(b == pl.num_programs(0) - 1)
    def _():
        pltpu.make_async_copy(w, w_o, out_sem).wait()


def unit_spec(i, d):
    return pl.BlockSpec((UNIT, d), lambda b, meta: (meta[PER * b + i], 0))


def k1(meta, tokens, cot, shard, blocks, ff):
    t, d = tokens.shape
    nb = t // BLOCK
    wide = shard.shape[1]
    blk = lambda n: pl.BlockSpec((BLOCK, n), lambda b, meta: (b, 0))
    fixed = lambda s: pl.BlockSpec(s, lambda b, meta: (0,) * len(s))
    sd = jax.ShapeDtypeStruct
    return pl.pallas_call(
        k1_body,
        grid_spec=pltpu.PrefetchScalarGridSpec(
            num_scalar_prefetch=1,
            grid=(nb,),
            in_specs=[unit_spec(i, d) for i in range(PER)] * 2 + [ANY] * 9,
            out_specs=[
                blk(3 * d),
                pl.BlockSpec((1, HEADS, BLOCK, BLOCK), lambda b, meta: (b, 0, 0, 0)),
                blk(d), blk(d), blk(d), blk(d), blk(d), blk(d), ANY,
                fixed((16, d)), fixed((4, ff // 4)), fixed((8, d)),
            ],
            scratch_shapes=[
                pltpu.VMEM((d, wide), BF16),
                pltpu.VMEM((16, d), F32),
                pltpu.SemaphoreType.DMA((17,)),
                pltpu.SemaphoreType.DMA,
            ],
        ),
        out_shape=[
            sd((t, 3 * d), BF16), sd((nb, HEADS, BLOCK, BLOCK), BF16), sd((t, d), F32), sd((t, d), BF16), sd((t, d), F32),
            sd((t, d), BF16), sd((t, d), BF16), sd((t, d), BF16), sd((d, wide), BF16),
            sd((16, d), F32), sd((4, ff // 4), F32), sd((8, d), F32),
        ],
        compiler_params=params(),
        cost_estimate=pl.CostEstimate(flops=2 * t * d * 5 * d, bytes_accessed=40 << 20, transcendentals=t * BLOCK * HEADS),
        name="norm_qkv_attend",
    )(meta, *([tokens] * PER), *([cot] * PER), shard, *blocks)


def gelu_and_slope(z):
    t = 1.0 / (1.0 + (0.3275911 * RSQRT2) * jnp.abs(z))
    e = jnp.exp(-0.5 * z * z)
    poly = t * (0.5 * 0.254829592 + t * (-0.5 * 0.284496736 + t * (0.5 * 1.421413741 + t * (
        -0.5 * 1.453152027 + t * (0.5 * 1.061405429)))))
    tail = poly * e
    cdf = jnp.where(z >= 0.0, 1.0 - tail, tail)
    return z * cdf, cdf + z * e * RSQRT_TAU


def mlp_body(ng, go, first, meta, *refs):
    a2o, a2p, g_o, g_p, b1, f1, f2 = refs[0:7]
    blocks = refs[7:11]
    at = 11
    prev = None
    if not first:
        prev, at = refs[11:15], 15
    yo, do, yp, dp, send, keep, db = refs[at : at + 7]
    a2, g, u_s, dz_s, w1, w2, dw1, dw2, sems = refs[at + 7 :]
    b = pl.program_id(0)
    last = pl.num_programs(0) - 1
    t, d = a2o.shape
    nb = t // BLOCK
    n = 128 * ng
    c, x, y, z = meta[I_C], meta[I_X], meta[I_Y], meta[I_Z]
    rows = f1.shape[0]
    quarter = rows // 4
    nk = d // 128

    def loads():
        ff = f1.shape[1]
        early = [(a2o, a2.at[pl.ds(0, t)]), (g_o, g.at[pl.ds(0, t)])]
        for zz in range(4):
            col = pl.multiple_of(zz * (ff // 4) + c * (ff // 8) + go * 128, 128)
            early.append((f1.at[:, pl.ds(col, n)], w1.at[pl.ds(pl.multiple_of(z * rows, 16), rows), pl.ds(zz * n, n)]))
        row = pl.multiple_of(c * (ff // 8) + go * 128, 128)
        early.append((f2.at[pl.ds(row, n)], w2.at[pl.ds(pl.multiple_of(z * n, 128), n)]))
        late = [(a2p, a2.at[pl.ds(t, t)]), (g_p, g.at[pl.ds(t, t)])]
        cps = [pltpu.make_async_copy(s, q, sems.at[i]) for i, (s, q) in enumerate(early + late)]
        return cps[: len(early)], cps[len(early) :]

    @pl.when(b == 0)
    def _():
        early, late = loads()
        for cp in early + late:
            cp.start()
        db[...] = jnp.zeros_like(db)
        for k, blk in enumerate(blocks):
            xx, yy = x, y
            if k == 1:
                xx, yy = x ^ (1 - c), y ^ c
            elif k == 2:
                xx, yy = x ^ c, y ^ (1 - c)
            elif k == 3:
                xx, yy = x ^ 1, y ^ 1
            p = 2 * yy + xx

            def place(f, carry):
                plane = z ^ (f + 1)
                r1 = pl.ds(pl.multiple_of(plane * rows + p * quarter, 16), quarter)
                for j in range(4 * ng):
                    w1[r1, j * 128 : (j + 1) * 128] = blk[f, j * quarter : (j + 1) * quarter, :]
                for gg in range(ng):
                    r2 = pl.ds(pl.multiple_of(plane * n + gg * 128 + p * 32, 32), 32)
                    for kk in range(nk):
                        lo = 4 * ng * quarter + (gg * nk + kk) * 32
                        w2[r2, kk * 128 : (kk + 1) * 128] = blk[f, lo : lo + 32, :]
                return carry

            lax.fori_loop(0, 3, place, 0)
        for cp in early:
            cp.wait()

    @pl.when(b == nb)
    def _():
        for cp in loads()[1]:
            cp.wait()

    rr = pl.ds(pl.multiple_of(b * BLOCK, BLOCK), BLOCK)
    a = a2[rr, :]
    gr = g[rr, :]
    lane = pl.ds(pl.multiple_of(c * (b1.shape[1] // 2) + go * 128, 128), n)
    bias = jnp.concatenate([b1[zz : zz + 1, lane] for zz in range(4)], axis=1)
    for k in range(2 * ng):
        cols = slice(k * 256, (k + 1) * 256)
        u, s = gelu_and_slope(nn(a, w1[:, cols]) + bias[:, cols])
        u_s[rr, cols] = u.astype(BF16)
        dz = (nt(gr, w2[cols, :]) * s).astype(BF16)
        dz_s[rr, cols] = dz
        db[0:1, cols] += jnp.sum(dz.astype(F32), axis=0, keepdims=True)
    yv = nn(u_s[rr, :], w2[...])
    dv = nt(dz_s[rr, :], w1[...])

    def put(y_ref, d_ref, y_old, d_old):
        y_ref[...] = (yv if y_old is None else yv + y_old[...].astype(F32)).astype(BF16)
        d_ref[...] = (dv if d_old is None else dv + d_old[...].astype(F32)).astype(BF16)

    @pl.when(b < nb)
    def _():
        put(yo, do, *((None, None) if first else prev[0:2]))

    @pl.when(b >= nb)
    def _():
        put(yp, dp, *((None, None) if first else prev[2:4]))

    @pl.when(b == last)
    def _():
        def weights(k, carry):
            cols = pl.ds(pl.multiple_of(k * 256, 256), 256)
            dw1[:, cols] = tn(a2[...], dz_s[:, cols]).astype(BF16)
            dw2[cols, :] = tn(u_s[:, cols], g[...]).astype(BF16)
            return carry

        lax.fori_loop(0, 2 * ng, weights, 0)
        for out, sel in ((send, 1 - meta[I_B1]), (keep, meta[I_B1])):
            for i in range(2):

                def cut(plane, carry):
                    r1 = pl.ds(pl.multiple_of(plane * rows + sel * 2 * quarter + i * quarter, 16), quarter)
                    for j in range(4 * ng):
                        out[i, plane, j * quarter : (j + 1) * quarter, :] = dw1[r1, j * 128 : (j + 1) * 128]
                    for gg in range(ng):
                        r2 = pl.ds(pl.multiple_of(plane * n + gg * 128 + sel * 64 + i * 32, 32), 32)
                        for kk in range(nk):
                            lo = 4 * ng * quarter + (gg * nk + kk) * 32
                            out[i, plane, lo : lo + 32, :] = dw2[r2, kk * 128 : (kk + 1) * 128]
                    return carry

                lax.fori_loop(0, 4, cut, 0)


def mlp(part, meta, a2o, a2p, g_o, g_p, b1, f1, f2, blocks, prev=()):
    ng, go = PARTS[part]
    first = not prev
    t, d = a2o.shape
    nb = t // BLOCK
    n = 128 * ng
    size = blocks[0].shape[1]
    sd = jax.ShapeDtypeStruct
    fixed = lambda s: pl.BlockSpec(s, lambda i, meta: (0,) * len(s), pipeline_mode=pl.Buffered(1))
    outf = lambda s: pl.BlockSpec(s, lambda i, meta: (0,) * len(s))
    own = pl.BlockSpec((BLOCK, d), lambda i, meta: (jnp.minimum(i, nb - 1), 0))
    other = pl.BlockSpec((BLOCK, d), lambda i, meta: (jnp.maximum(i - nb, 0), 0))
    tok = sd((t, d), BF16)
    half = (2, 4, size, 128)
    return pl.pallas_call(
        functools.partial(mlp_body, ng, go, first),
        grid_spec=pltpu.PrefetchScalarGridSpec(
            num_scalar_prefetch=1,
            grid=(2 * nb,),
            in_specs=[ANY] * 4 + [fixed(b1.shape)] + [ANY] * 2 + [fixed(k.shape) for k in blocks]
            + ([] if first else [own, own, other, other]),
            out_specs=[own, own, other, other, outf(half), outf(half), outf((8, 4 * n))],
            scratch_shapes=[
                pltpu.VMEM((2 * t, d), BF16), pltpu.VMEM((2 * t, d), BF16),
                pltpu.VMEM((2 * t, 4 * n), BF16), pltpu.VMEM((2 * t, 4 * n), BF16),
                pltpu.VMEM((d, 4 * n), BF16), pltpu.VMEM((4 * n, d), BF16),
                pltpu.VMEM((d, 4 * n), BF16), pltpu.VMEM((4 * n, d), BF16),
                pltpu.SemaphoreType.DMA((9,)),
            ],
        ),
        out_shape=[tok, tok, tok, tok, sd(half, BF16), sd(half, BF16), sd((8, 4 * n), F32)],
        compiler_params=params(),
        cost_estimate=pl.CostEstimate(flops=2 * 2 * t * d * 4 * n * 6, bytes_accessed=30 << 20, transcendentals=2 * t * 4 * n),
        name="hidden_first" if first else "hidden_second",
    )(meta, a2o, a2p, g_o, g_p, b1, f1, f2, *blocks, *prev)


EARLY = 8


def heads_back(pairs, lo, do, prob, inv, o, qkv, out):
    d = qkv.shape[1] // 3
    n = 128 * pairs
    lo_m, hi_m = lane_masks()
    for j in range(pairs):
        cols = slice(128 * (lo + j), 128 * (lo + j + 1))
        q, k, v = (qkv[:, i * d + cols.start : i * d + cols.stop] for i in range(3))
        dop = (do[:, 128 * j : 128 * (j + 1)].astype(F32) * inv[:, cols]).astype(BF16)
        dot = dop.astype(F32) * o[:, cols].astype(F32)
        dq = dk = dv = None
        for h, m in ((0, lo_m), (1, hi_m)):
            e = prob[0, 2 * j + h]
            mean = jnp.sum(dot * m.astype(F32), axis=-1, keepdims=True)
            dom = dop * m
            ds = (e.astype(F32) * (nt(dom, v) - mean)).astype(BF16)
            ms = m * SCALE
            parts = (nn(ds, k * ms), tn(ds, q * ms), tn(e, dom))
            dq, dk, dv = parts if dq is None else (dq + parts[0], dk + parts[1], dv + parts[2])
        for i, a in enumerate((dq, dk, dv)):
            out[:, i * n + 128 * j : i * n + 128 * (j + 1)] = a.astype(BF16)


def back_early_body(gp, da_o, da_p, x1_r, prob, inv, o, qkv, w_out, vec, dbf, dx1_o, dl, dq, acc):
    n = 64 * EARLY

    @pl.when(pl.program_id(0) == 0)
    def _():
        acc[...] = jnp.zeros_like(acc)
        acc[5:6] = dbf[0:1]

    da2 = da_o[...].astype(F32) + da_p[...].astype(F32)
    n2, r2 = norm_stats(x1_r[...])
    dx1 = gp[...].astype(F32) + norm_back(da2, n2, r2, vec[3:4])
    low = dx1.astype(BF16)
    acc[3:4] += jnp.sum(da2 * n2, axis=0, keepdims=True)
    acc[4:5] += jnp.sum(da2, axis=0, keepdims=True)
    acc[2:3] += jnp.sum(low.astype(F32), axis=0, keepdims=True)
    dx1_o[...] = dx1
    dl[...] = low
    do = nt(low, w_out[0:n, :]).astype(BF16)
    heads_back(EARLY // 2, 0, do, prob, inv, o, qkv, dq)


def back_early(gp, da_o, da_p, x1, prob, inv, o, qkv, w, vec, dbf):
    t, d = gp.shape
    blk = lambda n: pl.BlockSpec((BLOCK, n), lambda b: (b, 0))
    sd = jax.ShapeDtypeStruct
    fixed = lambda s: pl.BlockSpec(s, lambda b: (0,) * len(s), pipeline_mode=pl.Buffered(1))
    cols = 3 * 64 * EARLY
    return pl.pallas_call(
        back_early_body,
        grid=(t // BLOCK,),
        in_specs=[blk(d), blk(d), blk(d), blk(d),
                  pl.BlockSpec((1, EARLY, BLOCK, BLOCK), lambda b: (b, 0, 0, 0)), blk(d), blk(d), blk(3 * d),
                  pl.BlockSpec((d, d), lambda b: (0, 3), pipeline_mode=pl.Buffered(1)),
                  fixed(vec.shape), fixed(dbf.shape)],
        out_specs=[blk(d), blk(d), blk(cols), pl.BlockSpec((128, d), lambda b: (0, 0))],
        out_shape=[sd((t, d), F32), sd((t, d), BF16), sd((t, cols), BF16), sd((128, d), F32)],
        compiler_params=params(),
        cost_estimate=pl.CostEstimate(flops=2 * t * d * 4 * d, bytes_accessed=24 << 20, transcendentals=0),
        name="attend_back_early",
    )(gp, da_o, da_p, x1, prob, inv, o, qkv, w, vec, dbf)


def back_late_body(meta, *refs):
    tok = refs[0:4]
    dx1, dl, dqe, prob, inv, o, qkv, w, vec, acc_in = refs[4:14]
    gt_o, dq, acc = refs[14:17]
    gt, sems = refs[17:]
    b = pl.program_id(0)
    nb = pl.num_programs(0)
    d = dl.shape[1]
    slot = lax.rem(b, 2)
    n = 64 * EARLY

    def puts(step, sl):
        return [
            pltpu.make_async_copy(
                gt.at[sl, pl.ds(i * UNIT, UNIT)],
                gt_o.at[pl.ds(pl.multiple_of(meta[PER * step + i] * UNIT, UNIT), UNIT)],
                sems.at[sl, i],
            )
            for i in range(PER)
        ]

    @pl.when(b == 0)
    def _():
        acc[...] = acc_in[...]

    @pl.when(b >= 2)
    def _():
        for cp in puts(b - 2, slot):
            cp.wait()

    do = nt(dl[...], w[n:, 3 * d : 4 * d]).astype(BF16)
    heads_back((HEADS - EARLY) // 2, EARLY // 2, do, prob, inv, o, qkv, dq)
    rest = d - n
    da1 = None
    for i in range(3):
        part = nt(dqe[:, i * n : (i + 1) * n], w[:, i * d : i * d + n])
        part = part + nt(dq[:, i * rest : (i + 1) * rest], w[:, i * d + n : (i + 1) * d])
        da1 = part if da1 is None else da1 + part
    x = jnp.concatenate([r[...] for r in tok], axis=0).astype(F32)
    n1, r1 = norm_stats(x)
    acc[0:1] += jnp.sum(da1 * n1, axis=0, keepdims=True)
    acc[1:2] += jnp.sum(da1, axis=0, keepdims=True)
    gt[slot] = dx1[...] + norm_back(da1, n1, r1, vec[0:1])
    for cp in puts(b, slot):
        cp.start()

    @pl.when(b == nb - 1)
    def _():
        for cp in puts(b - 1, 1 - slot) + puts(b, slot):
            cp.wait()


def back_late(meta, tokens, dx1, dl, dqe, prob, inv, o, qkv, w, vec, acc_in):
    t, d = tokens.shape
    late = HEADS - EARLY
    blk = lambda n: pl.BlockSpec((BLOCK, n), lambda b, meta: (b, 0))
    sd = jax.ShapeDtypeStruct
    fixed = lambda s: pl.BlockSpec(s, lambda b, meta: (0,) * len(s), pipeline_mode=pl.Buffered(1))
    return pl.pallas_call(
        back_late_body,
        grid_spec=pltpu.PrefetchScalarGridSpec(
            num_scalar_prefetch=1,
            grid=(t // BLOCK,),
            in_specs=[unit_spec(i, d) for i in range(PER)] + [
                blk(d), blk(d), blk(dqe.shape[1]),
                pl.BlockSpec((1, late, BLOCK, BLOCK), lambda b, meta: (b, EARLY // late, 0, 0)), blk(d), blk(d), blk(3 * d),
            ] + [fixed(a.shape) for a in (w, vec, acc_in)],
            out_specs=[ANY, blk(3 * 64 * late), pl.BlockSpec((128, d), lambda b, meta: (0, 0))],
            scratch_shapes=[pltpu.VMEM((2, BLOCK, d), F32), pltpu.SemaphoreType.DMA((2, PER))],
        ),
        out_shape=[sd((t, d), F32), sd((t, 3 * 64 * late), BF16), sd((128, d), F32)],
        compiler_params=params(),
        cost_estimate=pl.CostEstimate(flops=2 * t * d * 5 * d, bytes_accessed=20 << 20, transcendentals=0),
        name="attend_back_late",
    )(meta, *([tokens] * PER), dx1, dl, dqe, prob, inv, o, qkv, w, vec, acc_in)


def split(meta, stage, send_o, keep_o, at, width):
    c = meta[I_C]
    rows = stage.shape[0] // 4
    n = rows // 2
    for zz in range(4):
        for i in range(2):
            for out, h in ((send_o, 1 - c), (keep_o, c)):
                lot = stage[pl.ds(pl.multiple_of(zz * rows + n * h + (n // 2) * i, 16), n // 2), 0:width]
                out[i, 0, zz, :, pl.ds(at, width)] = lot[0 : n // 4]
                out[i, 1, zz, :, pl.ds(at, width)] = lot[n // 4 :]


def grads_early_body(meta, a1, dq, o, dl, send_o, keep_o, stage):
    d = a1.shape[1]
    s = pl.program_id(0)
    last = pl.num_programs(0) - 1

    @pl.when(s < last)
    def _():
        stage[...] = tn(a1[...], dq[...]).astype(BF16)

    @pl.when(s == last)
    def _():
        stage[...] = tn(o[...], dl[...]).astype(BF16)

    split(meta, stage, send_o, keep_o, pl.multiple_of(s * d, 128), d)


def grads_late_body(meta, a1, dq, acc, *refs):
    d = a1.shape[1]
    c = meta[I_C]
    rows = d // 4
    dbs, (send_o, keep_o, stage) = refs[: len(PARTS)], refs[len(PARTS) :]
    stage[...] = tn(a1[...], dq[...]).astype(BF16)
    split(meta, stage, send_o, keep_o, 0, d)
    stage[:, 0:128] = acc[...].T.astype(BF16)
    stage[:, 128:256] = jnp.zeros((d, 128), BF16)
    for zz in range(4):
        parts = []
        for hh in range(2):
            for src, (ng, go) in zip(dbs, PARTS):
                for k in range(ng):
                    at = (zz * ng + k) * 128
                    parts.append(jnp.where(hh == c, src[0:1, at : at + 128], 0.0))
        parts.append(jnp.zeros((16 - len(parts), 128), F32))
        stage[zz * rows : zz * rows + 16, 128:256] = jnp.concatenate(parts, axis=0).astype(BF16)
    split(meta, stage, send_o, keep_o, d, EXT)


def grads(body, steps, wide, meta, a1, dq, *rest, cost=None):
    t, d = a1.shape
    cost = cost or pl.CostEstimate(flops=2 * t * d * steps * d, bytes_accessed=12 << 20, transcendentals=0)
    half = (2, 2, 4, d // 32, wide)
    sd = jax.ShapeDtypeStruct
    fixed = lambda a: pl.BlockSpec(a.shape, lambda s, meta: (0,) * a.ndim, pipeline_mode=pl.Buffered(1))
    outf = pl.BlockSpec(half, lambda s, meta: (0,) * 5)
    last = dq.shape[1] // d - 1
    return pl.pallas_call(
        body,
        grid_spec=pltpu.PrefetchScalarGridSpec(
            num_scalar_prefetch=1,
            grid=(steps,),
            in_specs=[fixed(a1), pl.BlockSpec((t, d), lambda s, meta: (0, jnp.minimum(s, last)))]
            + [fixed(a) for a in rest],
            out_specs=[outf, outf],
            scratch_shapes=[pltpu.VMEM((d, d), BF16)],
        ),
        out_shape=[sd(half, BF16), sd(half, BF16)],
        compiler_params=params(),
        cost_estimate=cost,
        name="weight_grads",
    )(meta, a1, dq, *rest)


def out_body(meta, ya, yb, x1, vec, out, buf, sems):
    b = pl.program_id(0)
    slot = lax.rem(b, 2)

    def puts(step, sl):
        return [
            pltpu.make_async_copy(
                buf.at[sl, pl.ds(i * UNIT, UNIT)],
                out.at[pl.ds(pl.multiple_of(meta[PER * step + i] * UNIT, UNIT), UNIT)],
                sems.at[sl, i],
            )
            for i in range(PER)
        ]

    @pl.when(b >= 2)
    def _():
        for cp in puts(b - 2, slot):
            cp.wait()

    y = ya[...].astype(F32) + yb[...].astype(F32)
    buf[slot] = (x1[...] + (y + vec[5:6])).astype(BF16)
    for cp in puts(b, slot):
        cp.start()

    @pl.when(b == pl.num_programs(0) - 1)
    def _():
        for cp in puts(b - 1, 1 - slot) + puts(b, slot):
            cp.wait()


def layer_output(meta, ya, yb, x1, vec):
    t, d = x1.shape
    blk = lambda n: pl.BlockSpec((BLOCK, n), lambda b, meta: (b, 0))
    fixed = lambda s: pl.BlockSpec(s, lambda b, meta: (0,) * len(s), pipeline_mode=pl.Buffered(1))
    return pl.pallas_call(
        out_body,
        grid_spec=pltpu.PrefetchScalarGridSpec(
            num_scalar_prefetch=1,
            grid=(t // BLOCK,),
            in_specs=[blk(d), blk(d), blk(d), fixed(vec.shape)],
            out_specs=ANY,
            scratch_shapes=[pltpu.VMEM((2, BLOCK, d), BF16), pltpu.SemaphoreType.DMA((2, PER))],
        ),
        out_shape=jax.ShapeDtypeStruct((t, d), BF16),
        compiler_params=params(),
        cost_estimate=pl.CostEstimate(flops=4 * t * d, bytes_accessed=8 << 20, transcendentals=0),
        name="layer_out",
    )(meta, ya, yb, x1, vec)


def halve_body(jobs, meta, *refs):
    at, to = 0, sum(2 * n for _, n, _ in jobs)
    for place, n, loops in jobs:
        ks, vs, (send, keep) = refs[at : at + n], refs[at + n : at + 2 * n], refs[to : to + 2]
        at, to = at + 2 * n, to + 2
        bit = meta[place]
        for out, sel in ((send, 1 - bit), (keep, bit)):
            for pre in range(ks[0].shape[0]):

                def step(r, carry):
                    col = 0
                    for k, v in zip(ks, vs):
                        w = k.shape[-1]
                        part = k[pre, sel, r].astype(F32) + v[pre, sel, r].astype(F32)
                        out[pre, r, :, col : col + w] = part.astype(BF16)
                        col += w
                    return carry

                lax.fori_loop(0, loops, step, 0)


def halve(meta, *jobs):
    sd = jax.ShapeDtypeStruct
    jobs = [(p, k if isinstance(k, list) else [k], v if isinstance(v, list) else [v]) for p, k, v in jobs]
    outs = []
    for _, ks, _ in jobs:
        shape = ks[0].shape
        outs += [sd((shape[0],) + shape[2:-1] + (sum(k.shape[-1] for k in ks),), BF16)] * 2
    arrays = [a for _, ks, vs in jobs for a in (*ks, *vs)]
    size = sum(a.size for a in arrays) // 2
    return pl.pallas_call(
        functools.partial(halve_body, tuple((p, len(ks), ks[0].shape[2]) for p, ks, _ in jobs)),
        in_specs=[pl.BlockSpec(memory_space=pltpu.SMEM)] + [WHOLE] * len(arrays),
        out_specs=[WHOLE] * len(outs),
        out_shape=outs,
        compiler_params=params(),
        cost_estimate=pl.CostEstimate(flops=size, bytes_accessed=6 * size, transcendentals=0),
        name="add_halve",
    )(meta, *arrays)


def total(routes, k, v):
    piece = k.astype(F32) + v.astype(F32)
    if routes.n_dp > 8:
        groups = [[j + 8 * o for o in range(routes.n_dp // 8)] for j in range(8)]
        piece = lax.psum(piece, "dp", axis_index_groups=groups)
    return piece.astype(BF16)


def ranks(meta, t):
    cc, x, y = holder(meta, t)
    return cc, 2 * jnp.where(cc == 0, x, y) + jnp.where(cc == 0, y, x)


def final_hidden_body(meta, *refs):
    pieces = refs[:8]
    d1, d2 = refs[8:10]
    rows, ff = d1.shape
    d = d2.shape[1]
    quarter = rows // 4
    nk = d // 128
    for t in range(8):
        cc, q = ranks(meta, t)
        at = 0
        for ng, go in PARTS:
            r1 = pl.ds(pl.multiple_of(q * quarter, 16), quarter)
            for zz in range(4):
                for g in range(ng):
                    col = pl.multiple_of(zz * (ff // 4) + cc * (ff // 8) + (go + g) * 128, 128)
                    d1[r1, pl.ds(col, 128)] = pieces[t][at : at + quarter, :].astype(F32)
                    at += quarter
            for g in range(ng):
                r2 = pl.ds(pl.multiple_of(cc * (ff // 8) + (go + g) * 128 + q * 32, 32), 32)
                for k in range(nk):
                    d2[r2, k * 128 : (k + 1) * 128] = pieces[t][at : at + 32, :].astype(F32)
                    at += 32


def final_mixed_body(meta, *refs):
    pieces = refs[:8]
    dqkv, dout, dg1, ds1, dbo, dg2, ds2, dbf, db1 = refs[8:17]
    ext = refs[17]
    n = pieces[0].shape[0]
    d = dout.shape[1]
    for t in range(8):
        cc, x, y = holder(meta, t)
        first, second = jnp.where(cc == 0, x, y), jnp.where(cc == 0, y, x)
        rows = pl.ds(pl.multiple_of(n * (4 * cc + 2 * first + second), n), n)
        v = pieces[t][...].astype(F32)
        m = 64 * EARLY
        for k in range(3):
            dqkv[rows, k * d : k * d + m] = v[:, k * m : (k + 1) * m]
            at = 3 * m + d + k * (d - m)
            dqkv[rows, k * d + m : (k + 1) * d] = v[:, at : at + d - m]
        dout[rows, :] = v[:, 3 * m : 3 * m + d]
        ext[rows, :] = v[:, 4 * d :]
    vec = ext[:, 0:128].T
    for i, ref in enumerate((dg1, ds1, dbo, dg2, ds2, dbf)):
        ref[...] = vec[i]
    for r in range(db1.shape[0] // 128):
        db1[pl.ds(128 * r, 128)] = ext[r, 128:256]


def final(body, meta, pieces, outs, scratch=()):
    sd = [jax.ShapeDtypeStruct(s, F32) for s in outs]
    res = pl.pallas_call(
        body,
        in_specs=[pl.BlockSpec(memory_space=pltpu.SMEM)] + [WHOLE] * 8,
        out_specs=[WHOLE] * len(outs),
        scratch_shapes=list(scratch),
        out_shape=sd,
        compiler_params=params(),
        name="place_sums",
    )(meta, *pieces)
    return res


def scalars(chip_ids):
    n = chip_ids.shape[0] // UNIT
    ids = chip_ids.reshape(n, UNIT)[:, 0]
    here = jnp.arange(n, dtype=jnp.int32)
    same = (ids[:, None] == ids[None, :]).astype(jnp.int32)
    long = jnp.sum(same, axis=1) > 1
    longs = long.astype(jnp.int32)
    before = jnp.sum(jnp.where(here[None, :] < here[:, None], longs[None, :], 0), axis=1)
    total = jnp.sum(longs)
    pos = jnp.where(long, before, total + here - before)
    src = jnp.sum(jnp.where(pos[None, :] == here[:, None], here[None, :], 0), axis=1)
    dp, z = lax.axis_index("dp"), lax.axis_index("fsdp")
    c, x, y = dp & 1, (dp >> 1) & 1, (dp >> 2) & 1
    b1, b2 = jnp.where(c == 0, x, y), jnp.where(c == 0, y, x)
    rest = jnp.stack([total >> 2, c, x, y, z, b1, b2, jnp.zeros_like(z), z & 1, z >> 1]).astype(jnp.int32)
    return jnp.concatenate([src.astype(jnp.int32), rest])


def on_device(n_dp, n_z, tokens, chip_ids, ln1_gain, ln1_bias, w_qkv, w_out, b_out, ln2_gain, ln2_bias,
              w_fc1, b_fc1, w_fc2, b_fc2, cotangent):
    routes = Routes(n_dp, n_z)
    t, d = tokens.shape
    ff = w_fc1.shape[1]
    rows = w_qkv.shape[0]
    pos = lax.axis_index("dp").astype(jnp.int32).reshape(1)
    meta = scalars(chip_ids)

    vecs = (ln1_gain, ln1_bias, b_out, ln2_gain, ln2_bias, b_fc2)
    mixed, near, far, hid = pack(pos, w_qkv, w_out, vecs, b_fc1, w_fc1, w_fc2)

    mate, far_h = routes.z_flip(hid, 1), routes.z_flip(hid, 2)
    last_h = routes.z_flip(far_h, 1)
    p_mixed = gather_mixed(routes, near, far, (mate,), last_h)
    block = jnp.stack([mate, far_h, last_h])
    p_hid = [block, routes.first(block), routes.second(block)]
    qkv, prob, inv, o, x1, a2, a1, gp, w, vec, b1, dbf = k1(
        meta, tokens, cotangent, tie(mixed, block), p_mixed, ff)
    swap = lax.optimization_barrier((a2, gp, *p_hid[1:]))
    p_hid.append(routes.second(swap[2]))
    a2p, gpp = routes.core(swap[0]), routes.core(swap[1])
    yo, do, yp, dp, sh, kh, db = mlp(0, meta, a2, a2p, gp, gpp, b1, w_fc1, w_fc2, p_hid)

    cut = lambda a, pre, loops: a.reshape(pre, 2, loops, 96, 128)
    nh = sh.shape[2] // 96
    yq, dq = routes.core(yp), routes.core(dp)
    got_h = routes.first(sh)
    dx1, dl, dqe, acc = back_early(gp, do, dq, x1, prob, inv, o, qkv, w, vec, dbf)
    early = 3 * 64 * EARLY + d
    late = 4 * d - early + EXT
    sm, km = grads(grads_early_body, early // d, early, meta, a1, dqe, o, dl, cost=SHORT)
    got_m = routes.core(tie(sm, got_h))
    s_h, k_h = halve(meta, (I_B2, cut(kh, 1, 4 * nh), cut(tie(got_h, sm), 1, 4 * nh)))
    got_h = routes.second(s_h)
    chunk = lambda a, pre, loops: a.reshape(pre, 2, loops, d // 32, a.shape[-1])
    s_m, k_m = halve(meta, (I_B1, chunk(km, 1, 8), chunk(tie(got_m, s_h), 1, 8)))
    got_m = routes.first(s_m)
    gt, dql, acc = back_late(meta, tokens, tie(dx1, s_m, yq), dl, dqe, prob, inv, o, qkv, w, vec, acc)

    s_h, k_h, s_m, k_m = halve(
        meta, (I_Z + 4, cut(k_h, 2, nh), cut(tie(got_h, acc), 2, nh)),
        (I_B2, chunk(k_m, 1, 4), chunk(tie(got_m, acc), 1, 4)))
    got_m, got_h = routes.second(s_m), routes.z_flip(s_h, 1)
    sl, kl = grads(grads_late_body, 1, late, meta, tie(a1, s_m), dql, acc, db)
    got_l = routes.core(tie(sl, got_m, got_h))
    s_m, k_m, s_h, k_h = halve(
        meta, (I_Z + 4, chunk(k_m, 2, 1), chunk(tie(got_m, sl), 2, 1)),
        (I_Z + 5, cut(k_h, 1, nh), cut(tie(got_h, sl), 1, nh)))
    got_m, got_h = routes.z_flip(s_m, 1), routes.z_flip(s_h, 2)
    s_l, k_l = halve(meta, (I_B1, chunk(kl, 1, 8), chunk(tie(got_l, s_h), 1, 8)))
    got_l = routes.first(s_l)
    layer_out = layer_output(meta, yo, yq, x1, tie(vec, s_l))
    s_l, k_l = halve(meta, (I_B2, chunk(k_l, 1, 4), chunk(tie(got_l, layer_out), 1, 4)))
    got_l = routes.second(s_l)
    s_l, k_l, s_m, k_m = halve(meta, (I_Z + 4, chunk(k_l, 2, 1), chunk(got_l, 2, 1)),
                               (I_Z + 5, chunk(k_m, 1, 1), chunk(tie(got_m, s_l), 1, 1)))
    piece = total(routes, k_h.reshape(-1, 128), tie(got_h, s_l).reshape(-1, 128))
    near_by = around(routes, piece)
    got_l, got_m = routes.z_flip(s_l, 1), routes.z_flip(s_m, 2)
    s_l, k_l = halve(meta, (I_Z + 5, chunk(k_l, 1, 1), chunk(tie(got_l, piece), 1, 1)))
    got_l = tie(routes.z_flip(s_l, 2), *near_by)
    side = lambda a, b: jnp.concatenate([a.reshape(d // 32, -1), b.reshape(d // 32, -1)], axis=1)
    piece = total(routes, side(k_m, k_l), side(got_m, got_l))
    near_m = around(routes, piece)
    pieces = near_by + [routes.core(b) for b in lax.optimization_barrier((*near_by, piece))[:4]]
    g_fc1, g_fc2 = final(final_hidden_body, meta, pieces, [w_fc1.shape, w_fc2.shape])
    near_m = list(lax.optimization_barrier((*near_m, g_fc1))[:4])
    pieces_m = near_m + [routes.core(b) for b in near_m]

    vecs = [(rows,)] * 6
    g_qkv, g_out, dg1, ds1, dbo, dg2, ds2, dbf2, db1 = final(
        final_mixed_body, meta, pieces_m, [w_qkv.shape, w_out.shape, *vecs, b_fc1.shape],
        [pltpu.VMEM((rows, EXT), F32)])
    return (layer_out, gt, dg1, ds1, g_qkv, g_out, dbo, dg2, ds2, g_fc1, db1, g_fc2, dbf2)


def solution(mesh):
    token, part, plain = P(ALL, None), P("fsdp", None), P("fsdp")
    return jax.shard_map(
        functools.partial(on_device, mesh.shape["dp"], mesh.shape["fsdp"]),
        mesh=mesh,
        in_specs=(token, P(ALL), plain, plain, part, part, plain, plain, plain, part, plain, part, plain, token),
        out_specs=(token, token, plain, plain, part, part, plain, plain, plain, part, plain, part, plain),
        check_vma=False,
    )
```

```python
import functools
import math

import jax
import jax.numpy as jnp
from jax import lax
from jax.experimental import pallas as pl
from jax.experimental.pallas import tpu as pltpu
from jax.sharding import PartitionSpec as P

HEADS = 12
HEAD = 64
UNIT = 64
BLOCK = 256
PER = BLOCK // UNIT
EPS = 1e-05
NEG = -1e30
RSQRT2 = 1.0 / math.sqrt(2.0)
RSQRT_TAU = 1.0 / math.sqrt(2.0 * math.pi)
SCALE = 1.0 / math.sqrt(HEAD)
EXT = 256
VMEM_LIMIT = 64 * 1024 * 1024 - 65536
ALL = ("dp", "fsdp")
F32 = jnp.float32
BF16 = jnp.bfloat16

I_LONG, I_C, I_X, I_Y, I_Z, I_B1, I_B2 = 16, 17, 18, 19, 20, 21, 22


def nn(a, b):
    return lax.dot_general(a, b, (((1,), (0,)), ((), ())), preferred_element_type=F32)


def nt(a, b):
    return lax.dot_general(a, b, (((1,), (1,)), ((), ())), preferred_element_type=F32)


def tn(a, b):
    return lax.dot_general(a, b, (((0,), (0,)), ((), ())), preferred_element_type=F32)


SHORT = pl.CostEstimate(flops=1, bytes_accessed=1, transcendentals=0)


def params(**kw):
    return pltpu.CompilerParams(vmem_limit_bytes=VMEM_LIMIT, **kw)


ANY = pl.BlockSpec(memory_space=pl.ANY)
WHOLE = pl.BlockSpec(memory_space=pltpu.VMEM)


def tie(a, *after):
    return lax.optimization_barrier((a,) + after)[0]


class Routes:
    def __init__(self, n_dp, n_z):
        self.n_dp, self.n_z = n_dp, n_z

    def table(self, move):
        pairs = []
        for d in range(self.n_dp):
            for z in range(self.n_z):
                e, w = move(d, z)
                pairs.append((d * self.n_z + z, e * self.n_z + w % self.n_z))
        return pairs

    def core(self, a):
        return lax.ppermute(a, ALL, self.table(lambda d, z: (d ^ 1, z)))

    def first(self, a):
        return lax.ppermute(a, ALL, self.table(lambda d, z: (d ^ (2 if d % 2 == 0 else 4), z)))

    def second(self, a):
        return lax.ppermute(a, ALL, self.table(lambda d, z: (d ^ (4 if d % 2 == 0 else 2), z)))

    def z_near(self, a):
        return lax.ppermute(a, ALL, self.table(lambda d, z: (d, z + (1 if d % 2 == 0 else self.n_z - 1))))

    def z_far(self, a):
        return lax.ppermute(a, ALL, self.table(lambda d, z: (d, z + 2)))

    def z_flip(self, a, bit):
        return lax.ppermute(a, ALL, self.table(lambda d, z: (d, z ^ bit)))

    def diagonal(self, a):
        return lax.ppermute(a, ALL, self.table(lambda d, z: (d ^ 6, z)))


def spread(routes, block):
    own = around(routes, block)
    return own + [routes.core(b) for b in own]


def around(routes, block):
    return [block, routes.first(block), routes.second(block), routes.diagonal(block)]


def holder(meta, t):
    flip = t // 4
    cc = meta[I_C] if flip == 0 else 1 - meta[I_C]
    x, y = meta[I_X], meta[I_Y]
    t = t % 4
    if t == 1:
        x, y = x ^ (1 - cc), y ^ cc
    elif t == 2:
        x, y = x ^ cc, y ^ (1 - cc)
    elif t == 3:
        x, y = x ^ 1, y ^ 1
    return cc, x, y


def gather_mixed(routes, near, far, early, late):
    block = jnp.concatenate([routes.z_near(near), routes.z_far(far)], axis=1)
    one = routes.first(block)
    two = routes.second(block)
    own = [block, one, two, routes.second(tie(one, two, *early))]
    return own + [routes.core(b) for b in own[:3]] + [routes.core(tie(own[3], late))]


def mixed_copies(meta, shard, blocks, w, sems):
    rows, wide = shard.shape
    quarter, part = rows // 4, wide // 2
    z = meta[I_Z]
    out = [(shard, w.at[pl.ds(pl.multiple_of(z * rows, 16), rows)])]
    for t, block in enumerate(blocks):
        cc, x, y = holder(meta, t)
        q = 2 * y + x
        plane = lax.rem(z + jnp.where(cc == 0, 3, 1), 4)
        far = lax.rem(z + 2, 4)
        out.append((block.at[:, pl.ds(0, wide)],
                    w.at[pl.ds(pl.multiple_of(plane * rows + q * quarter, 16), quarter)]))
        out.append((block.at[:, pl.ds(wide, part)],
                    w.at[pl.ds(pl.multiple_of(far * rows + q * quarter, 16), quarter),
                         pl.ds(pl.multiple_of(cc * part, 128), part)]))
    return [pltpu.make_async_copy(s, d, sems.at[i]) for i, (s, d) in enumerate(out)]


PARTS = ((3, 0),)


def piece_rows(ng, rows, d):
    return 4 * ng * (rows // 4) + ng * (d // 128) * 32


def pack_body(pos, *refs):
    w_qkv, w_out = refs[0:2]
    vecs, b1, f1, f2 = refs[2:8], refs[8], refs[9], refs[10]
    mixed, near, far = refs[11:14]
    outs, sems = refs[14 : 14 + len(PARTS)], refs[14 + len(PARTS)]
    c, x, y = pos[0] & 1, (pos[0] >> 1) & 1, (pos[0] >> 2) & 1
    p = 2 * y + x
    d = w_out.shape[1]
    rows = w_out.shape[0]
    quarter = rows // 4
    ff = f1.shape[1]
    copies = []
    for out, (ng, go) in zip(outs, PARTS):
        for zz in range(4):
            for g in range(ng):
                col = pl.multiple_of(zz * (ff // 4) + c * (ff // 8) + (go + g) * 128, 128)
                copies.append((f1.at[pl.ds(pl.multiple_of(p * quarter, 16), quarter), pl.ds(col, 128)],
                               out.at[pl.ds((zz * ng + g) * quarter, quarter)]))
        base = 4 * ng * quarter
        for g in range(ng):
            row = pl.multiple_of(c * (ff // 8) + (go + g) * 128 + p * 32, 32)
            for k in range(d // 128):
                copies.append((f2.at[pl.ds(row, 32), pl.ds(k * 128, 128)],
                               out.at[pl.ds(base + (g * (d // 128) + k) * 32, 32)]))
    copies = [pltpu.make_async_copy(s, t, sems.at[i]) for i, (s, t) in enumerate(copies)]
    for cp in copies:
        cp.start()
    mixed[:, 0 : 3 * d] = w_qkv[...]
    mixed[:, 3 * d : 4 * d] = w_out[...]
    lines = [v[...].astype(F32).reshape(1, rows) for v in vecs] + [jnp.zeros((128 - len(vecs), rows), F32)]
    mixed[:, 4 * d : 4 * d + 128] = jnp.concatenate(lines, axis=0).T.astype(BF16)
    n = b1.shape[0] // 128
    lines = [b1[pl.ds(128 * i, 128)].astype(F32).reshape(1, 128) for i in range(n)] + [jnp.zeros((rows - n, 128), F32)]
    mixed[:, 4 * d + 128 :] = jnp.concatenate(lines, axis=0).astype(BF16)
    own = pl.ds(pl.multiple_of(p * quarter, 16), quarter)
    near[...] = mixed[own, :]
    part = mixed.shape[1] // 2
    far[...] = mixed[own, pl.ds(pl.multiple_of(c * part, 128), part)]
    for cp in copies:
        cp.wait()


def pack(pos, w_qkv, w_out, vecs, b1, f1, f2):
    rows, d = w_out.shape
    wide = 4 * d + EXT
    sd = jax.ShapeDtypeStruct
    count = sum(4 * ng + ng * (d // 128) for ng, _ in PARTS)
    return pl.pallas_call(
        pack_body,
        in_specs=[pl.BlockSpec(memory_space=pltpu.SMEM)] + [WHOLE] * 9 + [ANY] * 2,
        out_specs=[WHOLE] * (3 + len(PARTS)),
        scratch_shapes=[pltpu.SemaphoreType.DMA((count,))],
        out_shape=[sd((rows, wide), BF16), sd((rows // 4, wide), BF16), sd((rows // 4, wide // 2), BF16)]
        + [sd((piece_rows(ng, rows, d), 128), BF16) for ng, _ in PARTS],
        compiler_params=params(),
        name="pack",
    )(pos, w_qkv, w_out, *vecs, b1, f1, f2)


def norm_stats(rows):
    centred = rows - jnp.mean(rows, axis=-1, keepdims=True)
    inverse = lax.rsqrt(jnp.mean(centred * centred, axis=-1, keepdims=True) + EPS)
    return centred * inverse, inverse


def norm_back(grad, normed, inverse, gain):
    e = grad * gain
    return inverse * (
        e - jnp.mean(e, axis=-1, keepdims=True) - normed * jnp.mean(e * normed, axis=-1, keepdims=True)
    )


def lane_masks():
    lane = lax.broadcasted_iota(jnp.int32, (1, 2 * HEAD), 1)
    low = jnp.where(lane < HEAD, 1.0, 0.0).astype(BF16)
    return low, (1.0 - low.astype(F32)).astype(BF16)


def k1_body(meta, *refs):
    tok, cot = refs[0:4], refs[4:8]
    shard, blocks = refs[8], refs[9:17]
    qkv_o, prob_o, inv_o, o_o, x1_o, a2_o, a1_o, gp_o, w_o, vec_o, b1_o, dbf_o = refs[17:29]
    w, vec, sems, out_sem = refs[29:]
    b = pl.program_id(0)
    d = w.shape[0]

    @pl.when(b == 0)
    def _():
        copies = mixed_copies(meta, shard, blocks, w, sems)
        for cp in copies:
            cp.start()
        dbf_o[...] = jnp.zeros_like(dbf_o)

    x = jnp.concatenate([r[...] for r in tok], axis=0).astype(F32)
    g = jnp.concatenate([r[...] for r in cot], axis=0)
    gp_o[...] = g
    dbf_o[0:1] += jnp.sum(g.astype(F32), axis=0, keepdims=True)
    n1, _ = norm_stats(x)

    @pl.when(b == 0)
    def _():
        for cp in mixed_copies(meta, shard, blocks, w, sems):
            cp.wait()
        pltpu.make_async_copy(w, w_o, out_sem).start()
        ext = w[:, 4 * d : 4 * d + 128].astype(F32).T
        vec[...] = ext[0:16]
        vec_o[...] = ext[0:16]
        rows = d // 4
        for zz in range(4):
            for r in range(b1_o.shape[1] // 128):
                b1_o[zz : zz + 1, 128 * r : 128 * (r + 1)] = w[
                    zz * rows : zz * rows + 8, 4 * d + 128 : 4 * d + 256
                ].astype(F32)[r : r + 1]

    g1, s1, b_out = vec[0:1], vec[1:2], vec[2:3]
    g2, s2 = vec[3:4], vec[4:5]
    a1 = (n1 * g1 + s1).astype(BF16)
    a1_o[...] = a1
    for k in range(3):
        qkv_o[:, k * d : (k + 1) * d] = nn(a1, w[:, k * d : (k + 1) * d]).astype(BF16)
    row = lax.broadcasted_iota(jnp.int32, (BLOCK, BLOCK), 0) // UNIT
    col = lax.broadcasted_iota(jnp.int32, (BLOCK, BLOCK), 1) // UNIT
    keep = (row == col) | (b < meta[I_LONG])
    low, high = lane_masks()
    left = lax.broadcasted_iota(jnp.int32, (BLOCK, 2 * HEAD), 1) < HEAD
    for j in range(HEADS // 2):
        s = slice(128 * j, 128 * (j + 1))
        q = qkv_o[:, s]
        k = qkv_o[:, d + 128 * j : d + 128 * (j + 1)]
        v = qkv_o[:, 2 * d + 128 * j : 2 * d + 128 * (j + 1)]
        mixed, inv = None, []
        for h, m in ((0, low), (1, high)):
            sc = jnp.where(keep, nt(q * (m * SCALE), k), NEG)
            e = jnp.exp(sc - jnp.max(sc, axis=-1, keepdims=True))
            inv.append(1.0 / jnp.sum(e, axis=-1, keepdims=True))
            e = e.astype(BF16)
            prob_o[0, 2 * j + h] = e
            part = nn(e, v * m)
            mixed = part if mixed is None else mixed + part
        inv = jnp.where(left, inv[0], inv[1])
        inv_o[:, s] = inv
        o_o[:, s] = (mixed * inv).astype(BF16)
    x1 = x + (nn(o_o[...], w[:, 3 * d : 4 * d]) + b_out)
    x1_o[...] = x1
    n2, _ = norm_stats(x1)
    a2_o[...] = (n2 * g2 + s2).astype(BF16)

    @pl.when(b == pl.num_programs(0) - 1)
    def _():
        pltpu.make_async_copy(w, w_o, out_sem).wait()


def unit_spec(i, d):
    return pl.BlockSpec((UNIT, d), lambda b, meta: (meta[PER * b + i], 0))


def k1(meta, tokens, cot, shard, blocks, ff):
    t, d = tokens.shape
    nb = t // BLOCK
    wide = shard.shape[1]
    blk = lambda n: pl.BlockSpec((BLOCK, n), lambda b, meta: (b, 0))
    fixed = lambda s: pl.BlockSpec(s, lambda b, meta: (0,) * len(s))
    sd = jax.ShapeDtypeStruct
    return pl.pallas_call(
        k1_body,
        grid_spec=pltpu.PrefetchScalarGridSpec(
            num_scalar_prefetch=1,
            grid=(nb,),
            in_specs=[unit_spec(i, d) for i in range(PER)] * 2 + [ANY] * 9,
            out_specs=[
                blk(3 * d),
                pl.BlockSpec((1, HEADS, BLOCK, BLOCK), lambda b, meta: (b, 0, 0, 0)),
                blk(d), blk(d), blk(d), blk(d), blk(d), blk(d), ANY,
                fixed((16, d)), fixed((4, ff // 4)), fixed((8, d)),
            ],
            scratch_shapes=[
                pltpu.VMEM((d, wide), BF16),
                pltpu.VMEM((16, d), F32),
                pltpu.SemaphoreType.DMA((17,)),
                pltpu.SemaphoreType.DMA,
            ],
        ),
        out_shape=[
            sd((t, 3 * d), BF16), sd((nb, HEADS, BLOCK, BLOCK), BF16), sd((t, d), F32), sd((t, d), BF16), sd((t, d), F32),
            sd((t, d), BF16), sd((t, d), BF16), sd((t, d), BF16), sd((d, wide), BF16),
            sd((16, d), F32), sd((4, ff // 4), F32), sd((8, d), F32),
        ],
        compiler_params=params(),
        cost_estimate=pl.CostEstimate(flops=2 * t * d * 5 * d, bytes_accessed=40 << 20, transcendentals=t * BLOCK * HEADS),
        name="norm_qkv_attend",
    )(meta, *([tokens] * PER), *([cot] * PER), shard, *blocks)


def gelu_and_slope(z):
    t = 1.0 / (1.0 + (0.3275911 * RSQRT2) * jnp.abs(z))
    e = jnp.exp(-0.5 * z * z)
    poly = t * (0.5 * 0.254829592 + t * (-0.5 * 0.284496736 + t * (0.5 * 1.421413741 + t * (
        -0.5 * 1.453152027 + t * (0.5 * 1.061405429)))))
    tail = poly * e
    cdf = jnp.where(z >= 0.0, 1.0 - tail, tail)
    return z * cdf, cdf + z * e * RSQRT_TAU


def mlp_body(ng, go, first, meta, *refs):
    a2o, a2p, g_o, g_p, b1, f1, f2 = refs[0:7]
    blocks = refs[7:11]
    at = 11
    prev = None
    if not first:
        prev, at = refs[11:15], 15
    yo, do, yp, dp, send, keep, db = refs[at : at + 7]
    a2, g, u_s, dz_s, w1, w2, dw1, dw2, sems = refs[at + 7 :]
    b = pl.program_id(0)
    last = pl.num_programs(0) - 1
    t, d = a2o.shape
    nb = t // BLOCK
    n = 128 * ng
    c, x, y, z = meta[I_C], meta[I_X], meta[I_Y], meta[I_Z]
    rows = f1.shape[0]
    quarter = rows // 4
    nk = d // 128

    def loads():
        ff = f1.shape[1]
        early = [(a2o, a2.at[pl.ds(0, t)]), (g_o, g.at[pl.ds(0, t)])]
        for zz in range(4):
            col = pl.multiple_of(zz * (ff // 4) + c * (ff // 8) + go * 128, 128)
            early.append((f1.at[:, pl.ds(col, n)], w1.at[pl.ds(pl.multiple_of(z * rows, 16), rows), pl.ds(zz * n, n)]))
        row = pl.multiple_of(c * (ff // 8) + go * 128, 128)
        early.append((f2.at[pl.ds(row, n)], w2.at[pl.ds(pl.multiple_of(z * n, 128), n)]))
        late = [(a2p, a2.at[pl.ds(t, t)]), (g_p, g.at[pl.ds(t, t)])]
        cps = [pltpu.make_async_copy(s, q, sems.at[i]) for i, (s, q) in enumerate(early + late)]
        return cps[: len(early)], cps[len(early) :]

    @pl.when(b == 0)
    def _():
        early, late = loads()
        for cp in early + late:
            cp.start()
        db[...] = jnp.zeros_like(db)
        for k, blk in enumerate(blocks):
            xx, yy = x, y
            if k == 1:
                xx, yy = x ^ (1 - c), y ^ c
            elif k == 2:
                xx, yy = x ^ c, y ^ (1 - c)
            elif k == 3:
                xx, yy = x ^ 1, y ^ 1
            p = 2 * yy + xx

            def place(f, carry):
                plane = z ^ (f + 1)
                r1 = pl.ds(pl.multiple_of(plane * rows + p * quarter, 16), quarter)
                for j in range(4 * ng):
                    w1[r1, j * 128 : (j + 1) * 128] = blk[f, j * quarter : (j + 1) * quarter, :]
                for gg in range(ng):
                    r2 = pl.ds(pl.multiple_of(plane * n + gg * 128 + p * 32, 32), 32)
                    for kk in range(nk):
                        lo = 4 * ng * quarter + (gg * nk + kk) * 32
                        w2[r2, kk * 128 : (kk + 1) * 128] = blk[f, lo : lo + 32, :]
                return carry

            lax.fori_loop(0, 3, place, 0)
        for cp in early:
            cp.wait()

    @pl.when(b == nb)
    def _():
        for cp in loads()[1]:
            cp.wait()

    rr = pl.ds(pl.multiple_of(b * BLOCK, BLOCK), BLOCK)
    a = a2[rr, :]
    gr = g[rr, :]
    lane = pl.ds(pl.multiple_of(c * (b1.shape[1] // 2) + go * 128, 128), n)
    bias = jnp.concatenate([b1[zz : zz + 1, lane] for zz in range(4)], axis=1)
    for k in range(2 * ng):
        cols = slice(k * 256, (k + 1) * 256)
        u, s = gelu_and_slope(nn(a, w1[:, cols]) + bias[:, cols])
        u_s[rr, cols] = u.astype(BF16)
        dz = (nt(gr, w2[cols, :]) * s).astype(BF16)
        dz_s[rr, cols] = dz
        db[0:1, cols] += jnp.sum(dz.astype(F32), axis=0, keepdims=True)
    yv = nn(u_s[rr, :], w2[...])
    dv = nt(dz_s[rr, :], w1[...])

    def put(y_ref, d_ref, y_old, d_old):
        y_ref[...] = (yv if y_old is None else yv + y_old[...].astype(F32)).astype(BF16)
        d_ref[...] = (dv if d_old is None else dv + d_old[...].astype(F32)).astype(BF16)

    @pl.when(b < nb)
    def _():
        put(yo, do, *((None, None) if first else prev[0:2]))

    @pl.when(b >= nb)
    def _():
        put(yp, dp, *((None, None) if first else prev[2:4]))

    @pl.when(b == last)
    def _():
        def weights(k, carry):
            cols = pl.ds(pl.multiple_of(k * 256, 256), 256)
            dw1[:, cols] = tn(a2[...], dz_s[:, cols]).astype(BF16)
            dw2[cols, :] = tn(u_s[:, cols], g[...]).astype(BF16)
            return carry

        lax.fori_loop(0, 2 * ng, weights, 0)
        for out, sel in ((send, 1 - meta[I_B1]), (keep, meta[I_B1])):
            for i in range(2):

                def cut(plane, carry):
                    r1 = pl.ds(pl.multiple_of(plane * rows + sel * 2 * quarter + i * quarter, 16), quarter)
                    for j in range(4 * ng):
                        out[i, plane, j * quarter : (j + 1) * quarter, :] = dw1[r1, j * 128 : (j + 1) * 128]
                    for gg in range(ng):
                        r2 = pl.ds(pl.multiple_of(plane * n + gg * 128 + sel * 64 + i * 32, 32), 32)
                        for kk in range(nk):
                            lo = 4 * ng * quarter + (gg * nk + kk) * 32
                            out[i, plane, lo : lo + 32, :] = dw2[r2, kk * 128 : (kk + 1) * 128]
                    return carry

                lax.fori_loop(0, 4, cut, 0)


def mlp(part, meta, a2o, a2p, g_o, g_p, b1, f1, f2, blocks, prev=()):
    ng, go = PARTS[part]
    first = not prev
    t, d = a2o.shape
    nb = t // BLOCK
    n = 128 * ng
    size = blocks[0].shape[1]
    sd = jax.ShapeDtypeStruct
    fixed = lambda s: pl.BlockSpec(s, lambda i, meta: (0,) * len(s), pipeline_mode=pl.Buffered(1))
    outf = lambda s: pl.BlockSpec(s, lambda i, meta: (0,) * len(s))
    own = pl.BlockSpec((BLOCK, d), lambda i, meta: (jnp.minimum(i, nb - 1), 0))
    other = pl.BlockSpec((BLOCK, d), lambda i, meta: (jnp.maximum(i - nb, 0), 0))
    tok = sd((t, d), BF16)
    half = (2, 4, size, 128)
    return pl.pallas_call(
        functools.partial(mlp_body, ng, go, first),
        grid_spec=pltpu.PrefetchScalarGridSpec(
            num_scalar_prefetch=1,
            grid=(2 * nb,),
            in_specs=[ANY] * 4 + [fixed(b1.shape)] + [ANY] * 2 + [fixed(k.shape) for k in blocks]
            + ([] if first else [own, own, other, other]),
            out_specs=[own, own, other, other, outf(half), outf(half), outf((8, 4 * n))],
            scratch_shapes=[
                pltpu.VMEM((2 * t, d), BF16), pltpu.VMEM((2 * t, d), BF16),
                pltpu.VMEM((2 * t, 4 * n), BF16), pltpu.VMEM((2 * t, 4 * n), BF16),
                pltpu.VMEM((d, 4 * n), BF16), pltpu.VMEM((4 * n, d), BF16),
                pltpu.VMEM((d, 4 * n), BF16), pltpu.VMEM((4 * n, d), BF16),
                pltpu.SemaphoreType.DMA((9,)),
            ],
        ),
        out_shape=[tok, tok, tok, tok, sd(half, BF16), sd(half, BF16), sd((8, 4 * n), F32)],
        compiler_params=params(),
        cost_estimate=pl.CostEstimate(flops=2 * 2 * t * d * 4 * n * 6, bytes_accessed=30 << 20, transcendentals=2 * t * 4 * n),
        name="hidden_first" if first else "hidden_second",
    )(meta, a2o, a2p, g_o, g_p, b1, f1, f2, *blocks, *prev)


EARLY = 8


def heads_back(pairs, lo, do, prob, inv, o, qkv, out):
    d = qkv.shape[1] // 3
    n = 128 * pairs
    lo_m, hi_m = lane_masks()
    for j in range(pairs):
        cols = slice(128 * (lo + j), 128 * (lo + j + 1))
        q, k, v = (qkv[:, i * d + cols.start : i * d + cols.stop] for i in range(3))
        dop = (do[:, 128 * j : 128 * (j + 1)].astype(F32) * inv[:, cols]).astype(BF16)
        dot = dop.astype(F32) * o[:, cols].astype(F32)
        dq = dk = dv = None
        for h, m in ((0, lo_m), (1, hi_m)):
            e = prob[0, 2 * j + h]
            mean = jnp.sum(dot * m.astype(F32), axis=-1, keepdims=True)
            dom = dop * m
            ds = (e.astype(F32) * (nt(dom, v) - mean)).astype(BF16)
            ms = m * SCALE
            parts = (nn(ds, k * ms), tn(ds, q * ms), tn(e, dom))
            dq, dk, dv = parts if dq is None else (dq + parts[0], dk + parts[1], dv + parts[2])
        for i, a in enumerate((dq, dk, dv)):
            out[:, i * n + 128 * j : i * n + 128 * (j + 1)] = a.astype(BF16)


def back_early_body(gp, da_o, da_p, x1_r, prob, inv, o, qkv, w_out, vec, dbf, dx1_o, dl, dq, acc):
    n = 64 * EARLY

    @pl.when(pl.program_id(0) == 0)
    def _():
        acc[...] = jnp.zeros_like(acc)
        acc[5:6] = dbf[0:1]

    da2 = da_o[...].astype(F32) + da_p[...].astype(F32)
    n2, r2 = norm_stats(x1_r[...])
    dx1 = gp[...].astype(F32) + norm_back(da2, n2, r2, vec[3:4])
    low = dx1.astype(BF16)
    acc[3:4] += jnp.sum(da2 * n2, axis=0, keepdims=True)
    acc[4:5] += jnp.sum(da2, axis=0, keepdims=True)
    acc[2:3] += jnp.sum(low.astype(F32), axis=0, keepdims=True)
    dx1_o[...] = dx1
    dl[...] = low
    do = nt(low, w_out[0:n, :]).astype(BF16)
    heads_back(EARLY // 2, 0, do, prob, inv, o, qkv, dq)


def back_early(gp, da_o, da_p, x1, prob, inv, o, qkv, w, vec, dbf):
    t, d = gp.shape
    blk = lambda n: pl.BlockSpec((BLOCK, n), lambda b: (b, 0))
    sd = jax.ShapeDtypeStruct
    fixed = lambda s: pl.BlockSpec(s, lambda b: (0,) * len(s), pipeline_mode=pl.Buffered(1))
    cols = 3 * 64 * EARLY
    return pl.pallas_call(
        back_early_body,
        grid=(t // BLOCK,),
        in_specs=[blk(d), blk(d), blk(d), blk(d),
                  pl.BlockSpec((1, EARLY, BLOCK, BLOCK), lambda b: (b, 0, 0, 0)), blk(d), blk(d), blk(3 * d),
                  pl.BlockSpec((d, d), lambda b: (0, 3), pipeline_mode=pl.Buffered(1)),
                  fixed(vec.shape), fixed(dbf.shape)],
        out_specs=[blk(d), blk(d), blk(cols), pl.BlockSpec((128, d), lambda b: (0, 0))],
        out_shape=[sd((t, d), F32), sd((t, d), BF16), sd((t, cols), BF16), sd((128, d), F32)],
        compiler_params=params(),
        cost_estimate=pl.CostEstimate(flops=2 * t * d * 4 * d, bytes_accessed=24 << 20, transcendentals=0),
        name="attend_back_early",
    )(gp, da_o, da_p, x1, prob, inv, o, qkv, w, vec, dbf)


def back_late_body(meta, *refs):
    tok = refs[0:4]
    dx1, dl, dqe, prob, inv, o, qkv, w, vec, acc_in = refs[4:14]
    gt_o, dq, acc = refs[14:17]
    gt, sems = refs[17:]
    b = pl.program_id(0)
    nb = pl.num_programs(0)
    d = dl.shape[1]
    slot = lax.rem(b, 2)
    n = 64 * EARLY

    def puts(step, sl):
        return [
            pltpu.make_async_copy(
                gt.at[sl, pl.ds(i * UNIT, UNIT)],
                gt_o.at[pl.ds(pl.multiple_of(meta[PER * step + i] * UNIT, UNIT), UNIT)],
                sems.at[sl, i],
            )
            for i in range(PER)
        ]

    @pl.when(b == 0)
    def _():
        acc[...] = acc_in[...]

    @pl.when(b >= 2)
    def _():
        for cp in puts(b - 2, slot):
            cp.wait()

    do = nt(dl[...], w[n:, 3 * d : 4 * d]).astype(BF16)
    heads_back((HEADS - EARLY) // 2, EARLY // 2, do, prob, inv, o, qkv, dq)
    rest = d - n
    da1 = None
    for i in range(3):
        part = nt(dqe[:, i * n : (i + 1) * n], w[:, i * d : i * d + n])
        part = part + nt(dq[:, i * rest : (i + 1) * rest], w[:, i * d + n : (i + 1) * d])
        da1 = part if da1 is None else da1 + part
    x = jnp.concatenate([r[...] for r in tok], axis=0).astype(F32)
    n1, r1 = norm_stats(x)
    acc[0:1] += jnp.sum(da1 * n1, axis=0, keepdims=True)
    acc[1:2] += jnp.sum(da1, axis=0, keepdims=True)
    gt[slot] = dx1[...] + norm_back(da1, n1, r1, vec[0:1])
    for cp in puts(b, slot):
        cp.start()

    @pl.when(b == nb - 1)
    def _():
        for cp in puts(b - 1, 1 - slot) + puts(b, slot):
            cp.wait()


def back_late(meta, tokens, dx1, dl, dqe, prob, inv, o, qkv, w, vec, acc_in):
    t, d = tokens.shape
    late = HEADS - EARLY
    blk = lambda n: pl.BlockSpec((BLOCK, n), lambda b, meta: (b, 0))
    sd = jax.ShapeDtypeStruct
    fixed = lambda s: pl.BlockSpec(s, lambda b, meta: (0,) * len(s), pipeline_mode=pl.Buffered(1))
    return pl.pallas_call(
        back_late_body,
        grid_spec=pltpu.PrefetchScalarGridSpec(
            num_scalar_prefetch=1,
            grid=(t // BLOCK,),
            in_specs=[unit_spec(i, d) for i in range(PER)] + [
                blk(d), blk(d), blk(dqe.shape[1]),
                pl.BlockSpec((1, late, BLOCK, BLOCK), lambda b, meta: (b, EARLY // late, 0, 0)), blk(d), blk(d), blk(3 * d),
            ] + [fixed(a.shape) for a in (w, vec, acc_in)],
            out_specs=[ANY, blk(3 * 64 * late), pl.BlockSpec((128, d), lambda b, meta: (0, 0))],
            scratch_shapes=[pltpu.VMEM((2, BLOCK, d), F32), pltpu.SemaphoreType.DMA((2, PER))],
        ),
        out_shape=[sd((t, d), F32), sd((t, 3 * 64 * late), BF16), sd((128, d), F32)],
        compiler_params=params(),
        cost_estimate=pl.CostEstimate(flops=2 * t * d * 5 * d, bytes_accessed=20 << 20, transcendentals=0),
        name="attend_back_late",
    )(meta, *([tokens] * PER), dx1, dl, dqe, prob, inv, o, qkv, w, vec, acc_in)


def split(meta, stage, send_o, keep_o, at, width):
    c = meta[I_C]
    rows = stage.shape[0] // 4
    n = rows // 2
    for zz in range(4):
        for i in range(2):
            for out, h in ((send_o, 1 - c), (keep_o, c)):
                lot = stage[pl.ds(pl.multiple_of(zz * rows + n * h + (n // 2) * i, 16), n // 2), 0:width]
                out[i, 0, zz, :, pl.ds(at, width)] = lot[0 : n // 4]
                out[i, 1, zz, :, pl.ds(at, width)] = lot[n // 4 :]


def grads_early_body(meta, a1, dq, o, dl, send_o, keep_o, stage):
    d = a1.shape[1]
    s = pl.program_id(0)
    last = pl.num_programs(0) - 1

    @pl.when(s < last)
    def _():
        stage[...] = tn(a1[...], dq[...]).astype(BF16)

    @pl.when(s == last)
    def _():
        stage[...] = tn(o[...], dl[...]).astype(BF16)

    split(meta, stage, send_o, keep_o, pl.multiple_of(s * d, 128), d)


def grads_late_body(meta, a1, dq, acc, *refs):
    d = a1.shape[1]
    c = meta[I_C]
    rows = d // 4
    dbs, (send_o, keep_o, stage) = refs[: len(PARTS)], refs[len(PARTS) :]
    stage[...] = tn(a1[...], dq[...]).astype(BF16)
    split(meta, stage, send_o, keep_o, 0, d)
    stage[:, 0:128] = acc[...].T.astype(BF16)
    stage[:, 128:256] = jnp.zeros((d, 128), BF16)
    for zz in range(4):
        parts = []
        for hh in range(2):
            for src, (ng, go) in zip(dbs, PARTS):
                for k in range(ng):
                    at = (zz * ng + k) * 128
                    parts.append(jnp.where(hh == c, src[0:1, at : at + 128], 0.0))
        parts.append(jnp.zeros((16 - len(parts), 128), F32))
        stage[zz * rows : zz * rows + 16, 128:256] = jnp.concatenate(parts, axis=0).astype(BF16)
    split(meta, stage, send_o, keep_o, d, EXT)


def grads(body, steps, wide, meta, a1, dq, *rest, cost=None):
    t, d = a1.shape
    cost = cost or pl.CostEstimate(flops=2 * t * d * steps * d, bytes_accessed=12 << 20, transcendentals=0)
    half = (2, 2, 4, d // 32, wide)
    sd = jax.ShapeDtypeStruct
    fixed = lambda a: pl.BlockSpec(a.shape, lambda s, meta: (0,) * a.ndim, pipeline_mode=pl.Buffered(1))
    outf = pl.BlockSpec(half, lambda s, meta: (0,) * 5)
    last = dq.shape[1] // d - 1
    return pl.pallas_call(
        body,
        grid_spec=pltpu.PrefetchScalarGridSpec(
            num_scalar_prefetch=1,
            grid=(steps,),
            in_specs=[fixed(a1), pl.BlockSpec((t, d), lambda s, meta: (0, jnp.minimum(s, last)))]
            + [fixed(a) for a in rest],
            out_specs=[outf, outf],
            scratch_shapes=[pltpu.VMEM((d, d), BF16)],
        ),
        out_shape=[sd(half, BF16), sd(half, BF16)],
        compiler_params=params(),
        cost_estimate=cost,
        name="weight_grads",
    )(meta, a1, dq, *rest)


def out_body(meta, ya, yb, x1, vec, out, buf, sems):
    b = pl.program_id(0)
    slot = lax.rem(b, 2)

    def puts(step, sl):
        return [
            pltpu.make_async_copy(
                buf.at[sl, pl.ds(i * UNIT, UNIT)],
                out.at[pl.ds(pl.multiple_of(meta[PER * step + i] * UNIT, UNIT), UNIT)],
                sems.at[sl, i],
            )
            for i in range(PER)
        ]

    @pl.when(b >= 2)
    def _():
        for cp in puts(b - 2, slot):
            cp.wait()

    y = ya[...].astype(F32) + yb[...].astype(F32)
    buf[slot] = (x1[...] + (y + vec[5:6])).astype(BF16)
    for cp in puts(b, slot):
        cp.start()

    @pl.when(b == pl.num_programs(0) - 1)
    def _():
        for cp in puts(b - 1, 1 - slot) + puts(b, slot):
            cp.wait()


def layer_output(meta, ya, yb, x1, vec):
    t, d = x1.shape
    blk = lambda n: pl.BlockSpec((BLOCK, n), lambda b, meta: (b, 0))
    fixed = lambda s: pl.BlockSpec(s, lambda b, meta: (0,) * len(s), pipeline_mode=pl.Buffered(1))
    return pl.pallas_call(
        out_body,
        grid_spec=pltpu.PrefetchScalarGridSpec(
            num_scalar_prefetch=1,
            grid=(t // BLOCK,),
            in_specs=[blk(d), blk(d), blk(d), fixed(vec.shape)],
            out_specs=ANY,
            scratch_shapes=[pltpu.VMEM((2, BLOCK, d), BF16), pltpu.SemaphoreType.DMA((2, PER))],
        ),
        out_shape=jax.ShapeDtypeStruct((t, d), BF16),
        compiler_params=params(),
        cost_estimate=pl.CostEstimate(flops=4 * t * d, bytes_accessed=8 << 20, transcendentals=0),
        name="layer_out",
    )(meta, ya, yb, x1, vec)


def halve_body(jobs, meta, *refs):
    at, to = 0, sum(2 * n for _, n, _ in jobs)
    for place, n, loops in jobs:
        ks, vs, (send, keep) = refs[at : at + n], refs[at + n : at + 2 * n], refs[to : to + 2]
        at, to = at + 2 * n, to + 2
        bit = meta[place]
        for out, sel in ((send, 1 - bit), (keep, bit)):
            for pre in range(ks[0].shape[0]):

                def step(r, carry):
                    col = 0
                    for k, v in zip(ks, vs):
                        w = k.shape[-1]
                        part = k[pre, sel, r].astype(F32) + v[pre, sel, r].astype(F32)
                        out[pre, r, :, col : col + w] = part.astype(BF16)
                        col += w
                    return carry

                lax.fori_loop(0, loops, step, 0)


def halve(meta, *jobs):
    sd = jax.ShapeDtypeStruct
    jobs = [(p, k if isinstance(k, list) else [k], v if isinstance(v, list) else [v]) for p, k, v in jobs]
    outs = []
    for _, ks, _ in jobs:
        shape = ks[0].shape
        outs += [sd((shape[0],) + shape[2:-1] + (sum(k.shape[-1] for k in ks),), BF16)] * 2
    arrays = [a for _, ks, vs in jobs for a in (*ks, *vs)]
    size = sum(a.size for a in arrays) // 2
    return pl.pallas_call(
        functools.partial(halve_body, tuple((p, len(ks), ks[0].shape[2]) for p, ks, _ in jobs)),
        in_specs=[pl.BlockSpec(memory_space=pltpu.SMEM)] + [WHOLE] * len(arrays),
        out_specs=[WHOLE] * len(outs),
        out_shape=outs,
        compiler_params=params(),
        cost_estimate=pl.CostEstimate(flops=size, bytes_accessed=6 * size, transcendentals=0),
        name="add_halve",
    )(meta, *arrays)


def total(routes, k, v):
    piece = k.astype(F32) + v.astype(F32)
    if routes.n_dp > 8:
        groups = [[j + 8 * o for o in range(routes.n_dp // 8)] for j in range(8)]
        piece = lax.psum(piece, "dp", axis_index_groups=groups)
    return piece.astype(BF16)


def ranks(meta, t):
    cc, x, y = holder(meta, t)
    return cc, 2 * jnp.where(cc == 0, x, y) + jnp.where(cc == 0, y, x)


def final_hidden_body(meta, *refs):
    pieces = refs[:8]
    d1, d2 = refs[8:10]
    rows, ff = d1.shape
    d = d2.shape[1]
    quarter = rows // 4
    nk = d // 128
    for t in range(8):
        cc, q = ranks(meta, t)
        at = 0
        for ng, go in PARTS:
            r1 = pl.ds(pl.multiple_of(q * quarter, 16), quarter)
            for zz in range(4):
                for g in range(ng):
                    col = pl.multiple_of(zz * (ff // 4) + cc * (ff // 8) + (go + g) * 128, 128)
                    d1[r1, pl.ds(col, 128)] = pieces[t][at : at + quarter, :].astype(F32)
                    at += quarter
            for g in range(ng):
                r2 = pl.ds(pl.multiple_of(cc * (ff // 8) + (go + g) * 128 + q * 32, 32), 32)
                for k in range(nk):
                    d2[r2, k * 128 : (k + 1) * 128] = pieces[t][at : at + 32, :].astype(F32)
                    at += 32


def final_mixed_body(meta, *refs):
    pieces = refs[:8]
    dqkv, dout, dg1, ds1, dbo, dg2, ds2, dbf, db1 = refs[8:17]
    ext = refs[17]
    n = pieces[0].shape[0]
    d = dout.shape[1]
    for t in range(8):
        cc, x, y = holder(meta, t)
        first, second = jnp.where(cc == 0, x, y), jnp.where(cc == 0, y, x)
        rows = pl.ds(pl.multiple_of(n * (4 * cc + 2 * first + second), n), n)
        v = pieces[t][...].astype(F32)
        m = 64 * EARLY
        for k in range(3):
            dqkv[rows, k * d : k * d + m] = v[:, k * m : (k + 1) * m]
            at = 3 * m + d + k * (d - m)
            dqkv[rows, k * d + m : (k + 1) * d] = v[:, at : at + d - m]
        dout[rows, :] = v[:, 3 * m : 3 * m + d]
        ext[rows, :] = v[:, 4 * d :]
    vec = ext[:, 0:128].T
    for i, ref in enumerate((dg1, ds1, dbo, dg2, ds2, dbf)):
        ref[...] = vec[i]
    for r in range(db1.shape[0] // 128):
        db1[pl.ds(128 * r, 128)] = ext[r, 128:256]


def final(body, meta, pieces, outs, scratch=()):
    sd = [jax.ShapeDtypeStruct(s, F32) for s in outs]
    res = pl.pallas_call(
        body,
        in_specs=[pl.BlockSpec(memory_space=pltpu.SMEM)] + [WHOLE] * 8,
        out_specs=[WHOLE] * len(outs),
        scratch_shapes=list(scratch),
        out_shape=sd,
        compiler_params=params(),
        name="place_sums",
    )(meta, *pieces)
    return res


def scalars(chip_ids):
    n = chip_ids.shape[0] // UNIT
    ids = chip_ids.reshape(n, UNIT)[:, 0]
    here = jnp.arange(n, dtype=jnp.int32)
    same = (ids[:, None] == ids[None, :]).astype(jnp.int32)
    long = jnp.sum(same, axis=1) > 1
    longs = long.astype(jnp.int32)
    before = jnp.sum(jnp.where(here[None, :] < here[:, None], longs[None, :], 0), axis=1)
    total = jnp.sum(longs)
    pos = jnp.where(long, before, total + here - before)
    src = jnp.sum(jnp.where(pos[None, :] == here[:, None], here[None, :], 0), axis=1)
    dp, z = lax.axis_index("dp"), lax.axis_index("fsdp")
    c, x, y = dp & 1, (dp >> 1) & 1, (dp >> 2) & 1
    b1, b2 = jnp.where(c == 0, x, y), jnp.where(c == 0, y, x)
    rest = jnp.stack([total >> 2, c, x, y, z, b1, b2, jnp.zeros_like(z), z & 1, z >> 1]).astype(jnp.int32)
    return jnp.concatenate([src.astype(jnp.int32), rest])


def on_device(n_dp, n_z, tokens, chip_ids, ln1_gain, ln1_bias, w_qkv, w_out, b_out, ln2_gain, ln2_bias,
              w_fc1, b_fc1, w_fc2, b_fc2, cotangent):
    routes = Routes(n_dp, n_z)
    t, d = tokens.shape
    ff = w_fc1.shape[1]
    rows = w_qkv.shape[0]
    pos = lax.axis_index("dp").astype(jnp.int32).reshape(1)
    meta = scalars(chip_ids)

    vecs = (ln1_gain, ln1_bias, b_out, ln2_gain, ln2_bias, b_fc2)
    mixed, near, far, hid = pack(pos, w_qkv, w_out, vecs, b_fc1, w_fc1, w_fc2)

    mate, far_h = routes.z_flip(hid, 1), routes.z_flip(hid, 2)
    last_h = routes.z_flip(far_h, 1)
    p_mixed = gather_mixed(routes, near, far, (mate,), last_h)
    block = jnp.stack([mate, far_h, last_h])
    p_hid = [block, routes.first(block), routes.second(block)]
    qkv, prob, inv, o, x1, a2, a1, gp, w, vec, b1, dbf = k1(
        meta, tokens, cotangent, tie(mixed, block), p_mixed, ff)
    swap = lax.optimization_barrier((a2, gp, *p_hid[1:]))
    p_hid.append(routes.second(swap[2]))
    a2p, gpp = routes.core(swap[0]), routes.core(swap[1])
    yo, do, yp, dp, sh, kh, db = mlp(0, meta, a2, a2p, gp, gpp, b1, w_fc1, w_fc2, p_hid)

    cut = lambda a, pre, loops: a.reshape(pre, 2, loops, 96, 128)
    nh = sh.shape[2] // 96
    yq, dq = routes.core(yp), routes.core(dp)
    got_h = routes.first(sh)
    dx1, dl, dqe, acc = back_early(gp, do, dq, x1, prob, inv, o, qkv, w, vec, dbf)
    early = 3 * 64 * EARLY + d
    late = 4 * d - early + EXT
    sm, km = grads(grads_early_body, early // d, early, meta, a1, dqe, o, dl, cost=SHORT)
    got_m = routes.core(tie(sm, got_h))
    s_h, k_h = halve(meta, (I_B2, cut(kh, 1, 4 * nh), cut(tie(got_h, sm), 1, 4 * nh)))
    got_h = routes.second(s_h)
    chunk = lambda a, pre, loops: a.reshape(pre, 2, loops, d // 32, a.shape[-1])
    s_m, k_m = halve(meta, (I_B1, chunk(km, 1, 8), chunk(tie(got_m, s_h), 1, 8)))
    got_m = routes.first(s_m)
    gt, dql, acc = back_late(meta, tokens, tie(dx1, s_m, yq), dl, dqe, prob, inv, o, qkv, w, vec, acc)

    s_h, k_h, s_m, k_m = halve(
        meta, (I_Z + 4, cut(k_h, 2, nh), cut(tie(got_h, acc), 2, nh)),
        (I_B2, chunk(k_m, 1, 4), chunk(tie(got_m, acc), 1, 4)))
    got_m, got_h = routes.second(s_m), routes.z_flip(s_h, 1)
    sl, kl = grads(grads_late_body, 1, late, meta, tie(a1, s_m), dql, acc, db)
    got_l = routes.core(tie(sl, got_m, got_h))
    s_m, k_m, s_h, k_h = halve(
        meta, (I_Z + 4, chunk(k_m, 2, 1), chunk(tie(got_m, sl), 2, 1)),
        (I_Z + 5, cut(k_h, 1, nh), cut(tie(got_h, sl), 1, nh)))
    got_m, got_h = routes.z_flip(s_m, 1), routes.z_flip(s_h, 2)
    s_l, k_l = halve(meta, (I_B1, chunk(kl, 1, 8), chunk(tie(got_l, s_h), 1, 8)))
    got_l = routes.first(s_l)
    layer_out = layer_output(meta, yo, yq, x1, tie(vec, s_l))
    s_l, k_l = halve(meta, (I_B2, chunk(k_l, 1, 4), chunk(tie(got_l, layer_out), 1, 4)))
    got_l = routes.second(s_l)
    s_l, k_l, s_m, k_m = halve(meta, (I_Z + 4, chunk(k_l, 2, 1), chunk(got_l, 2, 1)),
                               (I_Z + 5, chunk(k_m, 1, 1), chunk(tie(got_m, s_l), 1, 1)))
    piece = total(routes, k_h.reshape(-1, 128), tie(got_h, s_l).reshape(-1, 128))
    near_by = around(routes, piece)
    got_l, got_m = routes.z_flip(s_l, 1), routes.z_flip(s_m, 2)
    s_l, k_l = halve(meta, (I_Z + 5, chunk(k_l, 1, 1), chunk(tie(got_l, piece), 1, 1)))
    got_l = tie(routes.z_flip(s_l, 2), *near_by)
    side = lambda a, b: jnp.concatenate([a.reshape(d // 32, -1), b.reshape(d // 32, -1)], axis=1)
    piece = total(routes, side(k_m, k_l), side(got_m, got_l))
    near_m = around(routes, piece)
    pieces = near_by + [routes.core(b) for b in lax.optimization_barrier((*near_by, piece))[:4]]
    g_fc1, g_fc2 = final(final_hidden_body, meta, pieces, [w_fc1.shape, w_fc2.shape])
    near_m = list(lax.optimization_barrier((*near_m, g_fc1))[:4])
    pieces_m = near_m + [routes.core(b) for b in near_m]

    vecs = [(rows,)] * 6
    g_qkv, g_out, dg1, ds1, dbo, dg2, ds2, dbf2, db1 = final(
        final_mixed_body, meta, pieces_m, [w_qkv.shape, w_out.shape, *vecs, b_fc1.shape],
        [pltpu.VMEM((rows, EXT), F32)])
    return (layer_out, gt, dg1, ds1, g_qkv, g_out, dbo, dg2, ds2, g_fc1, db1, g_fc2, dbf2)


def solution(mesh):
    token, part, plain = P(ALL, None), P("fsdp", None), P("fsdp")
    return jax.shard_map(
        functools.partial(on_device, mesh.shape["dp"], mesh.shape["fsdp"]),
        mesh=mesh,
        in_specs=(token, P(ALL), plain, plain, part, part, plain, plain, plain, part, plain, part, plain, token),
        out_specs=(token, token, plain, plain, part, part, plain, plain, plain, part, plain, part, plain),
        check_vma=False,
    )
```
